32 devices in a mesh: dp: 8 (over z, x), mp: 4 (over y, core).
Axes of the slice: x: 2, y: 2, z: 4, core: 2. Of those that a mesh axis runs over, the one named last changes fastest.
Arguments:
- tokens: bfloat16 [16384, 512], P('dp'), may hold values from -6 to 6
- cotangent: bfloat16 [16384, 512], P('dp'), may hold values from -6 to 6
- bucket: int32 [16384, 1], P('dp'), may hold values from 0 to 7, as said below
- cell: int32 [16384], P('dp'), may hold values from 0 to 1, as said below
- features: bfloat16 [4, 64, 256], replicated, may hold values from -4 to 4
- qkv_weight: bfloat16 [3, 512, 512], P(None, None, 'mp'), may hold values from -0.25 to 0.25
- out_weight: bfloat16 [512, 512], P('mp'), may hold values from -1 to 1
- out_bias: float32 [512], replicated, may hold values from -3 to 3
- norm1_gain: float32 [512], replicated, may hold values from 0.25 to 1.75
- norm1_bias: float32 [512], replicated, may hold values from -3 to 3
- norm2_gain: float32 [512], replicated, may hold values from 0.25 to 1.75
- norm2_bias: float32 [512], replicated, may hold values from -3 to 3
- up_weight: bfloat16 [512, 2048], P(None, 'mp'), may hold values from -0.25 to 0.25
- up_bias: float32 [2048], P('mp'), may hold values from -3 to 3
- down_weight: bfloat16 [2048, 512], P('mp'), may hold values from -0.125 to 0.125
- down_bias: float32 [512], replicated, may hold values from -3 to 3
Outputs:
- output: bfloat16 [16384, 512], P('dp')
- grad_tokens: float32 [16384, 512], P('dp')
- grad_qkv_weight: float32 [3, 512, 512], P(None, None, 'mp')
- grad_out_weight: float32 [512, 512], P('mp')
- grad_out_bias: float32 [512], replicated
- grad_norm1_gain: float32 [512], replicated
- grad_norm1_bias: float32 [512], replicated
- grad_norm2_gain: float32 [512], replicated
- grad_norm2_bias: float32 [512], replicated
- grad_up_weight: float32 [512, 2048], P(None, 'mp')
- grad_up_bias: float32 [2048], P('mp')
- grad_down_weight: float32 [2048, 512], P('mp')
- grad_down_bias: float32 [512], replicated
The draws below stay inside these ranges and needn't reach their ends.
Inputs may be any that keep to these rules, and one draw needn't show every extreme that they name: The 2048 rows of one device name every bucket at least once and one bucket at most 512 times, and every device names some bucket exactly 512 times. In every bucket one cell, drawn from the seed, holds tokens from every device.
All inputs are finite; a program needn't handle non-finite values.
Results may differ from the reference program's by a relative error of at most 0.012.
The reference program's roundings to bfloat16 on the way count: a program that leaves them out, or rounds other values in their place, can miss the bound.
Values may be sent and summed in bfloat16 or wider, within the bound.
A program may use at most 192 MiB of HBM per device.

```python
import jax
import jax.numpy as jnp
from jax import lax

D = 512
HEADS = 8
HD = 64
M = 256
FF = 2048
FEATS = 4
STEP = 5
SEG = 2
TOK_DEV = 2048
CAP = 512
TOKENS = 16384
N_DP = 8


def routing_law(key):
    spanning = jax.random.randint(jax.random.fold_in(key, 11), (N_DP,), 0, SEG)
    offset = jax.random.randint(jax.random.fold_in(key, 12), (), 0, N_DP)
    heavy_pool = max(1, N_DP // 8)
    remaining = TOK_DEV - N_DP - CAP + 1

    def one_device(position):
        device_key = jax.random.fold_in(jax.random.fold_in(key, 13), position)
        heavy_one = (offset + jax.random.randint(jax.random.fold_in(device_key, 1), (), 0, heavy_pool)) % N_DP
        others = (heavy_one + 1 + jax.random.permutation(jax.random.fold_in(device_key, 2), N_DP - 1)) % N_DP
        filler = others[jnp.arange(remaining) % (N_DP - 1)].astype(jnp.int32)
        chosen = jnp.concatenate([jnp.arange(N_DP, dtype=jnp.int32), jnp.full((CAP - 1,), heavy_one, jnp.int32), filler])
        leading = jnp.concatenate([jnp.ones((N_DP,), jnp.int32), jnp.zeros((TOK_DEV - N_DP,), jnp.int32)])
        random_cell = jax.random.randint(jax.random.fold_in(device_key, 3), (TOK_DEV,), 0, SEG)
        cell_rows = jnp.where(leading == 1, spanning[chosen], random_cell).astype(jnp.int32)
        shuffle = jax.random.permutation(jax.random.fold_in(device_key, 4), TOK_DEV)
        return (chosen[shuffle], cell_rows[shuffle])
    buckets, cell_rows = jax.vmap(one_device)(jnp.arange(N_DP, dtype=jnp.int32))
    return (buckets.reshape(TOKENS, 1).astype(jnp.int32), cell_rows.reshape(TOKENS).astype(jnp.int32))


def draw_bucket(key, part):
    return routing_law(key)[0]


def draw_cell(key, part):
    return routing_law(key)[1]


def levels(own_key, extent, split, least, top_value):
    gain, own = 1.0, jax.random.fold_in(own_key, 6)
    for dim, blocks in split:
        draws = jnp.exp(jax.random.uniform(jax.random.fold_in(own, dim), (blocks,), jnp.float32, least / len(split), top_value / len(split)))
        gain = gain * jnp.repeat(draws, extent[dim] // blocks).reshape([-1 if axis == dim else 1 for axis in range(len(extent))])
    return gain


def noise(rng, dims, deviation, bound, split=(), held_as=jnp.bfloat16):
    values = deviation * jax.random.normal(rng, dims, jnp.float32)
    if split:
        values = values * levels(rng, dims, split, -0.22, 0.18)
    return jnp.clip(values, -bound, bound).astype(held_as)


def setup_inputs(seed: int = 0) -> dict:
    key_list = jax.random.split(jax.random.key(seed), 17)
    tokens = noise(key_list[0], (TOKENS, D), 1.0, 6.0, ((0, 8),))
    cotangent = noise(key_list[1], (TOKENS, D), 1.0, 6.0, ((0, 8),))
    bucket = draw_bucket(jax.random.fold_in(key_list[16], 71), 0)
    cell = draw_cell(jax.random.fold_in(key_list[16], 71), 0)
    features = noise(key_list[4], (FEATS, HD, M), 1.0, 4.0)
    qkv_weight = noise(key_list[5], (3, D, D), D ** -0.5, 0.25, ((2, 4),))
    out_weight = noise(key_list[6], (D, D), (D // 16) ** -0.5, 1.0, ((0, 4),))
    out_bias = noise(key_list[7], (D,), 0.5, 3.0, (), jnp.float32)
    norm1_gain = jnp.clip(1.0 + 0.15 * jax.random.normal(key_list[8], (D,), jnp.float32), 0.25, 1.75)
    norm1_bias = noise(key_list[9], (D,), 0.5, 3.0, (), jnp.float32)
    norm2_gain = jnp.clip(1.0 + 0.15 * jax.random.normal(key_list[10], (D,), jnp.float32), 0.25, 1.75)
    norm2_bias = noise(key_list[11], (D,), 0.5, 3.0, (), jnp.float32)
    up_weight = noise(key_list[12], (D, FF), D ** -0.5, 0.25, ((1, 4),))
    up_bias = noise(key_list[13], (FF,), 0.5, 3.0, ((0, 4),), jnp.float32)
    down_weight = noise(key_list[14], (FF, D), FF ** -0.5, 0.125, ((0, 4),))
    down_bias = noise(key_list[15], (D,), 0.5, 3.0, (), jnp.float32)
    return dict(tokens=tokens, cotangent=cotangent, bucket=bucket, cell=cell, features=features, qkv_weight=qkv_weight, out_weight=out_weight, out_bias=out_bias, norm1_gain=norm1_gain, norm1_bias=norm1_bias, norm2_gain=norm2_gain, norm2_bias=norm2_bias, up_weight=up_weight, up_bias=up_bias, down_weight=down_weight, down_bias=down_bias)


EXACT_PRECISION = lax.Precision.HIGHEST

@jax.custom_vjp
def low(v):
    return lax.optimization_barrier(v.astype(jnp.bfloat16)).astype(jnp.float32)

@jax.custom_vjp
def low_back(v):
    return v

def low_keep(v):
    return (low(v), None)

def low_pass(kept, grad):
    return (grad,)

def back_keep(v):
    return (v, None)

def back_low(kept, grad):
    return (low(grad),)
low.defvjp(low_keep, low_pass)
low_back.defvjp(back_keep, back_low)

def layer_norm(values, norm_gain, norm_bias):
    average = lax.optimization_barrier(jnp.mean(values, -1, keepdims=True))
    centred = values - average
    spread = lax.optimization_barrier(jnp.mean(centred * centred, -1, keepdims=True))
    return centred * lax.rsqrt(spread + 1e-05) * norm_gain + norm_bias

def feature_map(rows, feature_rows):
    scale = HD ** (-0.25)
    projected = jnp.einsum('thd,dm->thm', rows, feature_rows, precision=EXACT_PRECISION) * scale
    squares = 0.5 * scale * scale * lax.optimization_barrier(jnp.sum(rows * rows, -1, keepdims=True))
    return low(jnp.exp(projected - squares))

def forward(tokens, qkv_weight, out_weight, out_bias, norm1_gain, norm1_bias, norm2_gain, norm2_bias, up_weight, up_bias, down_weight, down_bias, cell_of, feature_rows):
    token_count = tokens.shape[0]
    normed = low_back(low(layer_norm(tokens, norm1_gain, norm1_bias)))
    projected = low_back(low(jnp.einsum('td,cde->cte', normed, qkv_weight, precision=EXACT_PRECISION)))
    query = projected[0].reshape(token_count, HEADS, HD)
    key_rows = projected[1].reshape(token_count, HEADS, HD)
    value_matrix_rows = projected[2].reshape(token_count, HEADS, HD)
    query_feature_map = feature_map(query, feature_rows)
    key_feature_map = feature_map(key_rows, feature_rows)

    def cell_step(running, cell_number):
        attention_numerator, denominator = running
        within_cell = (cell_of == cell_number).astype(key_feature_map.dtype)
        cell_memory_state = low(jnp.einsum('ciu,cib->iub', key_feature_map * within_cell[:, None, None], value_matrix_rows, precision=EXACT_PRECISION))
        cell_total = jnp.einsum('thm,t->hm', key_feature_map, within_cell, precision=EXACT_PRECISION)
        attention_numerator = attention_numerator + within_cell[:, None, None] * jnp.einsum('fba,bay->fby', query_feature_map, cell_memory_state, precision=EXACT_PRECISION)
        denominator = denominator + within_cell[:, None] * jnp.einsum('thm,hm->th', query_feature_map, cell_total, precision=EXACT_PRECISION)
        return ((attention_numerator, denominator), None)
    start = (jnp.zeros((token_count, HEADS, HD), value_matrix_rows.dtype), jnp.zeros((token_count, HEADS), value_matrix_rows.dtype))
    (attention_numerator, denominator), _ = lax.scan(jax.checkpoint(cell_step), start, jnp.arange(N_DP * SEG, dtype=jnp.int32))
    attention = low_back(low((attention_numerator / denominator[..., None]).reshape(token_count, D)))
    branch = low_back(low(jnp.dot(attention, out_weight, precision=EXACT_PRECISION)))
    midstream = tokens + branch + out_bias
    normed2 = low(layer_norm(midstream, norm2_gain, norm2_bias))
    preact = low_back(jnp.dot(normed2, up_weight, precision=EXACT_PRECISION) + up_bias)
    active = low(jax.nn.gelu(preact, approximate=False))
    branch_out = low_back(jnp.dot(active, down_weight, precision=EXACT_PRECISION))
    return midstream + branch_out + down_bias

def reference(tokens, cotangent, bucket, cell, features, qkv_weight, out_weight, out_bias, norm1_gain, norm1_bias, norm2_gain, norm2_bias, up_weight, up_bias, down_weight, down_bias):
    cell_of = (bucket[:, 0] * SEG + cell).astype(jnp.int32)
    feature_rows = features[STEP % FEATS].astype(jnp.float32)
    weights = tuple((w.astype(jnp.float32) for w in (qkv_weight, out_weight, out_bias, norm1_gain, norm1_bias, norm2_gain, norm2_bias, up_weight, up_bias, down_weight, down_bias)))

    def layer(*values):
        return forward(*values, cell_of, feature_rows)
    result, pull = jax.vjp(layer, tokens.astype(jnp.float32), *weights)
    grads = pull(cotangent.astype(jnp.float32))
    return (result.astype(jnp.bfloat16), grads[0], grads[1], grads[2], grads[3], grads[4], grads[5], grads[6], grads[7], grads[8], grads[9], grads[10], grads[11])
```

```python
import functools
from types import SimpleNamespace

import jax
import jax.numpy as jnp
from jax import lax
from jax.experimental import pallas as pl
from jax.experimental.pallas import tpu as pltpu
from jax.sharding import PartitionSpec as P

HD = 64
FEATS = 4
STEP = 5
SEG = 2
PAD = 8
SCALE = HD**-0.25
HALF_SQUARE = 0.5 * SCALE * SCALE
EPS = 1e-05

BF = jnp.bfloat16
F32 = jnp.float32
MESH = pl.DeviceIdType.MESH
LANES = 128
TILE = 256


def dot(a, b):
    return jnp.dot(a, b, preferred_element_type=F32)


def dot_nt(a, b):
    return lax.dot_general(a, b, (((1,), (1,)), ((), ())), preferred_element_type=F32)


def dot_tn(a, b):
    return lax.dot_general(a, b, (((0,), (0,)), ((), ())), preferred_element_type=F32)


def lane(shape):
    return lax.broadcasted_iota(jnp.int32, shape, len(shape) - 1)


def roll_half(x):
    return pltpu.roll(x, HD, 1)


def loop(count, body, unroll=False):
    if unroll or count <= 4:
        for i in range(count):
            body(i)
    else:

        def step(i, carry):
            body(i)
            return carry

        lax.fori_loop(0, count, step, 0)


def rows_of(i, size):
    if isinstance(i, int):
        return pl.ds(i * size, size)
    return pl.ds(pl.multiple_of(i * size, size), size)


def normalised(values):
    average = jnp.mean(values, -1, keepdims=True)
    centred = values - average
    spread = jnp.mean(centred * centred, -1, keepdims=True)
    scale = lax.rsqrt(spread + EPS)
    return centred * scale, scale


def norm_back(upstream, hat, scale, gain):
    e = gain * upstream
    return (
        e
        - jnp.mean(e, -1, keepdims=True)
        - hat * jnp.mean(e * hat, -1, keepdims=True)
    ) * scale


def round_up(a, b):
    return (a + b - 1) // b * b


class Plan:
    def __init__(self, n, nm, tokens, width, local, feats, hidden):
        self.n, self.nm, self.T, self.D, self.L, self.M, self.F = (
            n,
            nm,
            tokens,
            width,
            local,
            feats,
            hidden,
        )
        self.H = local // HD
        self.HM = self.H * feats
        self.Tm = tokens // nm
        self.big = n > 8
        self.G8 = n * PAD
        used = hidden + hidden + local
        self.used = used
        self.rp = round_up((used + n - 1) // n, 16)
        self.rq = round_up((3 * width + n - 1) // n, 16)
        self.R = self.rp * n
        n2 = n // 2
        T, D, L, HM, Tm, R = self.T, self.D, self.L, self.HM, self.Tm, self.R
        vm = "vmem"
        states = (n, HM, SEG * HD)
        place = "hbm" if self.big else vm
        self.inputs = [
            ("tok", "hbm"),
            ("bkt", vm),
            ("cel", vm),
            ("feat", vm),
            ("wqkv", vm),
            ("g1", vm),
            ("b1", vm),
            ("ob", vm),
            ("g2", vm),
            ("b2", vm),
            ("db", vm),
            ("cot", "hbm"),
            ("ow", "hbm"),
            ("up", "hbm"),
            ("ub", "hbm"),
            ("dn", "hbm"),
        ]
        self.outputs = [
            ("out_o", "hbm", (T, D), BF),
            ("gtok_o", "hbm", (T, D), BF),
            ("ffg_o", "hbm", (n, self.rp, D), BF),
            ("qkvg_o", "hbm", (n, self.rq, L), BF),
            ("small_o", vm, (16, D), F32),
        ]
        big_states = [("sp", states), ("rb", states), ("sall", states), ("gall", states)]
        if self.big:
            self.outputs += [(name, "hbm", shape, BF) for name, shape in big_states]
        self.scratch = [
            ("wcat", (D, 4 * L), BF),
            ("f2", (L, HM), BF),
            ("wb", (HM, 2 * L), BF),
            ("ccb", (T, LANES), BF),
            ("oh2", (T, 2 * self.G8), BF),
            ("nm", (T, D), BF),
            ("qk", (2, T, L), BF),
            ("vv", (2, T, L), BF),
            ("qf", (T, HM), BF),
            ("kf", (T, HM), BF),
            ("ft", (HM, T), BF),
            ("tp", (n, PAD, HM), F32),
            ("trb", (n, PAD, HM), F32),
            ("tall", (n, PAD, HM), F32),
            ("gtall", (n, PAD, HM), F32),
            ("tot2", (2 * self.G8, HM), BF),
            ("acc", (HM, SEG * HD), F32),
            ("attf", (T, L), F32),
            ("inv", (T, L), F32),
            ("attb", (T, L), BF),
            ("arow", (nm, Tm, L), BF),
            ("wq_g", (nm, 3, D, L), BF),
            ("ow_g", (nm, L, D), BF),
            ("up_g", (nm, D, hidden), BF),
            ("ub_g", (nm, 1, hidden), F32),
            ("dn_g", (nm, hidden, D), BF),
            ("cotv", (Tm, D), BF),
            ("tokv", (Tm, D), BF),
            ("mid", (Tm, D), F32),
            ("nm2", (Tm, D), BF),
            ("nm2t", (D, Tm), BF),
            ("act", (Tm, hidden), BF),
            ("gp", (Tm, hidden), BF),
            ("bo", (Tm, D), F32),
            ("gn2", (Tm, D), F32),
            ("gb", (Tm, D), BF),
            ("outv", (Tm, D), BF),
            ("small", (16, D), F32),
            ("small_m", (nm, 16, D), F32),
            ("small_d", (n, 16, D), F32),
            ("ffp", (nm, used, D), BF),
            ("ffc", (2, used, D), BF),
            ("ffy", (R, D), BF),
            ("ffx", (n2, self.rp, D), BF),
            ("ffz", (n2, self.rp, D), BF),
            ("gas", (nm, Tm, L), BF),
            ("gar", (nm, Tm, L), BF),
            ("gad", (2, T, L), BF),
            ("gg", (2, T, L), BF),
            ("gd", (T, L), F32),
            ("grads", (3, T, L), BF),
            ("garr", (nm, 3, Tm, L), BF),
            ("qkvp", (n, self.rq, L), BF),
            ("qkvx", (n2, self.rq, L), BF),
            ("qkvz", (n2, self.rq, L), BF),
            ("gtv", (Tm, D), BF),
        ]
        if self.big:
            self.scratch += [("stage_a", (2, HM, SEG * HD), BF), ("stage_b", (2, HM, SEG * HD), BF)]
        else:
            self.scratch += [(name, shape, BF) for name, shape in big_states]
        self.sems = {
            "rs": n,
            "rst": n,
            "ag": n,
            "agt": n,
            "rs2": n,
            "rst2": n,
            "ag2": n,
            "agt2": n,
            "a2a": nm,
            "gaa": nm,
            "grq": nm,
            "grk": nm,
            "wy": 5,
            "wc": 10,
            "ffc": 2,
            "ffy": 1,
            "ffx": 1,
            "ffz": n2,
            "ffgz": n2,
            "ffgx": 1,
            "qx": 1,
            "qz": n2,
            "qgz": n2,
            "qgx": 1,
            "oy": 1,
            "oc": 2,
            "ty": 1,
            "tc": 2,
            "sm": nm,
            "sd": n,
        }
        self.local_sems = 16

    def names(self):
        return (
            [x[0] for x in self.inputs]
            + [x[0] for x in self.outputs]
            + [x[0] for x in self.scratch]
            + [f"{k}_{end}" for k in self.sems for end in ("s", "r")]
            + ["lsem"]
        )


def layer_kernel(plan, *refs):
    r = SimpleNamespace(**dict(zip(plan.names(), refs, strict=True)))
    n, nm, T, D, L, M, HM, Tm, H = (
        plan.n,
        plan.nm,
        plan.T,
        plan.D,
        plan.L,
        plan.M,
        plan.HM,
        plan.Tm,
        plan.H,
    )
    hidden = plan.F
    n2 = n // 2
    tiles = T // TILE
    me, m = lax.axis_index("dp"), lax.axis_index("mp")
    sib = m + 1 - 2 * lax.rem(m, 2)
    far = lax.rem(m + nm // 2, nm)
    farsib = lax.rem(sib + nm // 2, nm)
    xpart = me + 1 - 2 * lax.rem(me, 2)
    xme, zme = lax.rem(me, 2), me // 2

    def sem(name, index):
        return getattr(r, f"{name}_s").at[index], getattr(r, f"{name}_r").at[index]

    def copy(src, dst, name, sent, dp=None, mp=None, got=None):
        send, _ = sem(name, sent)
        _, recv = sem(name, sent if got is None else got)
        return pltpu.make_async_remote_copy(
            src_ref=src,
            dst_ref=dst,
            send_sem=send,
            recv_sem=recv,
            device_id=(me if dp is None else dp, m if mp is None else mp),
            device_id_type=MESH,
        )

    def local(src, dst, index):
        return pltpu.make_async_copy(src, dst, r.lsem.at[index])

    low = lane((1, LANES)) < HD

    barrier = pltpu.get_barrier_semaphore()

    def greet(k):
        pl.semaphore_signal(
            barrier, inc=1, device_id=(lax.rem(me + 1 + k, n), m), device_id_type=MESH
        )

    loop(n - 1, greet)
    for k in range(1, nm):
        pl.semaphore_signal(
            barrier, inc=1, device_id=(me, lax.rem(m + k, nm)), device_id_type=MESH
        )

    mine = rows_of(m, Tm)
    tok_in = local(r.tok, r.nm, 10)
    own_in = [local(r.cot.at[mine], r.cotv, 0), local(r.tok.at[mine], r.tokv, 11)]
    for c in [tok_in, *own_in]:
        c.start()

    r.wcat[:, 0:L] = r.wqkv[0]
    r.wcat[:, L : 2 * L] = r.wqkv[1]
    wv = r.wqkv[2].astype(F32)
    wv_rolled = roll_half(wv)
    r.wcat[:, 2 * L : 3 * L] = jnp.where(low, wv, wv_rolled).astype(BF)
    r.wcat[:, 3 * L : 4 * L] = jnp.where(low, wv_rolled, wv).astype(BF)
    feature_rows = r.feat[STEP % FEATS]
    r.f2[...] = jnp.zeros((L, HM), BF)
    for h in range(H):
        r.f2[h * HD : (h + 1) * HD, h * M : (h + 1) * M] = feature_rows
    r.wb[:, 0:L] = r.f2[...].astype(F32).T.astype(BF)
    head_of_row = lax.broadcasted_iota(jnp.int32, (HM, L), 0) // M
    r.wb[:, L : 2 * L] = jnp.where(head_of_row == lane((HM, L)) // HD, 1.0, 0.0).astype(BF)

    def ids(i):
        rows = rows_of(i, LANES)
        b, c = r.bkt[pl.ds(i, 1), :].astype(F32), r.cel[pl.ds(i, 1), :].astype(F32)
        square = (LANES, LANES)
        cell = jnp.broadcast_to(SEG * b + c, square).T - jnp.where(low, 0.0, 1.0)
        r.ccb[rows, :] = cell.astype(BF)
        padded = PAD * b + c
        column = jnp.broadcast_to(padded, square).T
        for block in range(2 * plan.G8 // LANES):
            number = (lane(square) + block * LANES) % plan.G8
            r.oh2[rows, block * LANES : (block + 1) * LANES] = jnp.where(
                column == number.astype(F32), 1.0, 0.0
            ).astype(BF)

    loop(T // LANES, ids)
    tok_in.wait()

    def phi(u):
        wide = u.astype(F32)
        squares = wide * wide
        first = jnp.sum(jnp.where(low, squares, 0.0), -1, keepdims=True)
        second = jnp.sum(jnp.where(low, 0.0, squares), -1, keepdims=True)
        projected = dot(u, r.f2[...]) * SCALE
        shift = jnp.where(lane((1, HM)) < M, first, second) * HALF_SQUARE
        return jnp.exp(projected - shift)

    def project(i):
        rows = rows_of(i, TILE)
        hat, _ = normalised(r.nm[rows, :].astype(F32))
        normed = (hat * r.g1[...] + r.b1[...]).astype(BF)
        r.nm[rows, :] = normed
        u = dot(normed, r.wcat[...]).astype(BF)
        q, k = u[:, 0:L], u[:, L : 2 * L]
        r.qk[0, rows, :], r.qk[1, rows, :] = q, k
        r.vv[0, rows, :], r.vv[1, rows, :] = u[:, 2 * L : 3 * L], u[:, 3 * L : 4 * L]
        r.qf[rows, :] = phi(q).astype(BF)
        features = phi(k)
        r.kf[rows, :] = features.astype(BF)
        r.ft[:, rows] = features.T.astype(BF)

    loop(tiles, project)

    pl.semaphore_wait(barrier, n - 1 + nm - 1)

    shards = [
        (r.wqkv, r.wq_g),
        (r.ow, r.ow_g),
        (r.up, r.up_g),
        (r.ub, r.ub_g),
        (r.dn, r.dn_g),
    ]
    own_copies, y_copies, core_copies = [], [], []
    for i, (src, dst) in enumerate(shards):
        own_copies.append(local(src, dst.at[m], 1 + i))
        y_copies.append(copy(src, dst.at[m], "wy", i, mp=far))
        core_copies.append(copy(src, dst.at[m], "wc", 2 * i, mp=sib))
    for c in own_copies + y_copies + core_copies:
        c.start()

    def state_pair(ref, p, stage):
        if plan.big:
            pltpu.sync_copy(ref.at[pl.ds(2 * p, 2)], stage)
            return stage
        return ref.at[pl.ds(2 * p, 2)]

    def masked_pair(rows, dup, p):
        code = r.ccb[rows, :]
        first = jnp.full((1, LANES), 1.0, F32) * (4 * p)
        left = jnp.where(code == first.astype(BF), dup, jnp.zeros_like(dup))
        right = jnp.where(code == (first + 2.0).astype(BF), dup, jnp.zeros_like(dup))
        return jnp.concatenate([left, right], 1)

    everything = pl.ds(0, T)

    def scatter_states(dup, name, name_t):
        def pair(kk):
            p = lax.rem(zme + 1 + kk, n2)
            staged = r.stage_a if plan.big else r.sp.at[pl.ds(2 * p, 2)]
            for h in range(H):
                hs = slice(h * M, (h + 1) * M)
                block = dot(r.ft[hs, :], masked_pair(everything, dup[h], p))
                staged[0, hs, :] = block[:, :LANES].astype(BF)
                staged[1, hs, :] = block[:, LANES:].astype(BF)
            if plan.big:
                pltpu.sync_copy(r.stage_a, r.sp.at[pl.ds(2 * p, 2)])
            for side in range(2):
                j = 2 * p + side

                @pl.when(j != me)
                def _():
                    copy(r.sp.at[j], r.rb.at[me], name, j, dp=j, got=me).start()
                    copy(r.tp.at[j], r.trb.at[me], name_t, j, dp=j, got=me).start()

        loop(n2, pair, unroll=False)

    def reduce_states(name, name_t, all_s, all_t, ag, agt):
        if plan.big:
            pltpu.sync_copy(r.sp.at[pl.ds(me, 1)], r.stage_b.at[pl.ds(0, 1)])
            r.acc[...] = r.stage_b[0].astype(F32)
        else:
            r.acc[...] = r.sp[me].astype(F32)
        all_t[me] = r.tp[me]

        def add(k):
            j = lax.rem(me + 1 + k, n)
            copy(r.sp.at[j], r.rb.at[j], name, j, dp=j).wait_recv()
            copy(r.tp.at[j], r.trb.at[j], name_t, j, dp=j).wait_recv()
            if plan.big:
                pltpu.sync_copy(r.rb.at[pl.ds(j, 1)], r.stage_b.at[pl.ds(0, 1)])
                r.acc[...] += r.stage_b[0].astype(F32)
            else:
                r.acc[...] += r.rb[j].astype(F32)
            all_t[me] += r.trb[j]

        loop(n - 1, add)
        if plan.big:
            r.stage_b[0] = r.acc[...].astype(BF)
            pltpu.sync_copy(r.stage_b.at[pl.ds(0, 1)], all_s.at[pl.ds(me, 1)])
        else:
            all_s[me] = r.acc[...].astype(BF)

        def send(k):
            j = lax.rem(me + 1 + k, n)
            copy(all_s.at[me], all_s.at[me], ag, j, dp=j, got=me).start()
            copy(all_t.at[me], all_t.at[me], agt, j, dp=j, got=me).start()

        loop(n - 1, send)

    def gathered_states(name, name_t, all_s, all_t, ag, agt):
        def wait(k):
            j = lax.rem(me + 1 + k, n)
            copy(all_s.at[j], all_s.at[j], ag, j, dp=j).wait_recv()
            copy(all_t.at[j], all_t.at[j], agt, j, dp=j).wait_recv()

        loop(n - 1, wait)

        def sent(k):
            j = lax.rem(me + 1 + k, n)
            copy(r.sp.at[j], r.rb.at[me], name, j, dp=j, got=me).wait_send()
            copy(r.tp.at[j], r.trb.at[me], name_t, j, dp=j, got=me).wait_send()
            copy(all_s.at[me], all_s.at[me], ag, j, dp=j, got=me).wait_send()
            copy(all_t.at[me], all_t.at[me], agt, j, dp=j, got=me).wait_send()

        loop(n - 1, sent)
        total = all_t[...].reshape(plan.G8, HM)
        top = total.astype(BF)
        r.tot2[0 : plan.G8, :] = top
        r.tot2[plan.G8 :, :] = (total - top.astype(F32)).astype(BF)

    r.tp[...] = dot_tn(r.oh2[:, : plan.G8], r.kf[...]).reshape(n, PAD, HM)
    scatter_states([r.vv[0], r.vv[1]], "rs", "rst")

    def turn(i):
        rows = rows_of(i, TILE)
        r.ft[:, rows] = r.qf[rows, :].astype(F32).T.astype(BF)

    loop(tiles, turn)
    onward = []
    for i, (_, dst) in enumerate(shards):
        copy(dst.at[far], dst.at[far], "wy", i, mp=far).wait_recv()
        c = copy(dst.at[far], dst.at[far], "wc", 2 * i + 1, mp=sib)
        c.start()
        onward.append(c)

    reduce_states("rs", "rst", r.sall, r.tall, "ag", "agt")
    gathered_states("rs", "rst", r.sall, r.tall, "ag", "agt")

    def select_heads(rows, left, all_s):
        code = r.ccb[rows, :].astype(F32)

        def pair(h, p, total):
            hs = slice(h * M, (h + 1) * M)
            blocks = state_pair(all_s, p, r.stage_a if plan.big else None)
            right = jnp.concatenate([blocks[0, hs, :], blocks[1, hs, :]], 1)
            product = dot(left[:, hs], right)
            first = jnp.full((1, LANES), 1.0, F32) * (4 * p)
            total = jnp.where(code == first, product[:, :LANES], total)
            return jnp.where(code == first + 2.0, product[:, LANES:], total)

        heads = []
        for h in range(H):
            total = jnp.zeros((left.shape[0], LANES), F32)
            if plan.big:
                total = lax.fori_loop(0, n2, functools.partial(pair, h), total)
            else:
                for p in range(n2):
                    total = pair(h, p, total)
            heads.append(total + roll_half(total))
        return jnp.where(low, heads[0], heads[1])

    def own_totals(rows):
        return dot(r.oh2[rows, :], r.tot2[...])

    def halves(first, second):
        return jnp.where(low, first, second)

    def attend(i):
        rows = rows_of(i, TILE)
        queries = r.qf[rows, :]
        numerator = select_heads(rows, queries, r.sall)
        product = queries.astype(F32) * own_totals(rows)
        denominator = halves(
            jnp.sum(product[:, :M], -1, keepdims=True),
            jnp.sum(product[:, M:], -1, keepdims=True),
        )
        attention = numerator / denominator
        r.attf[rows, :] = attention
        r.inv[rows, :] = 1.0 / denominator
        r.attb[rows, :] = attention.astype(BF)

    per_chunk = Tm // TILE
    chunk_order = [far, farsib, sib, m]

    def chunks(body, after):
        for k, target in enumerate(chunk_order):
            loop(per_chunk, lambda i, target=target: body(target * per_chunk + i))
            after(k, target)

    def send_attention(k, target):
        if k < nm - 1:
            copy(
                r.attb.at[rows_of(target, Tm)], r.arow.at[m], "a2a", target, mp=target, got=m
            ).start()
        else:
            r.arow[m] = r.attb[rows_of(m, Tm), :]

    chunks(attend, send_attention)

    for c in own_copies:
        c.wait()
    for i, (_, dst) in enumerate(shards):
        copy(dst.at[sib], dst.at[sib], "wc", 2 * i, mp=sib).wait_recv()
        copy(dst.at[farsib], dst.at[farsib], "wc", 2 * i + 1, mp=sib).wait_recv()
    for c in y_copies + core_copies + onward:
        c.wait_send()
    for c in own_in:
        c.wait()
    for target in chunk_order[: nm - 1]:
        copy(r.arow.at[target], r.arow.at[target], "a2a", target, mp=target).wait_recv()

    r.small[...] = jnp.zeros((16, D), F32)

    def project_out(i):
        rows = rows_of(i, TILE)
        columns = jnp.concatenate([r.arow[s, rows, :] for s in range(nm)], 1)
        branch = dot(columns, r.ow_g[...].reshape(D, D)).astype(BF).astype(F32)
        middle = r.tokv[rows, :].astype(F32) + branch + r.ob[...]
        r.mid[rows, :] = middle
        hat, _ = normalised(middle)
        normed = hat * r.g2[...] + r.b2[...]
        r.nm2[rows, :] = normed.astype(BF)
        r.nm2t[:, rows] = normed.T.astype(BF)
        r.small[0:1, :] += jnp.sum(r.cotv[rows, :].astype(F32), 0, keepdims=True)

    loop(Tm // TILE, project_out)

    def units(s):
        up, down = r.up_g[s], r.dn_g[s]

        def tile(i):
            rows = rows_of(i, TILE)
            preact = dot(r.nm2[rows, :], up) + r.ub_g[s]
            spread = 0.5 + 0.5 * lax.erf(preact * (0.5**0.5))
            active = (preact * spread).astype(BF)
            r.act[rows, :] = active
            slope = spread + preact * jnp.exp(preact * preact * -0.5) * 0.3989422804014327
            grad = (dot_nt(r.cotv[rows, :], down) * slope).astype(BF)
            r.gp[rows, :] = grad
            forward, backward = dot(active, down), dot_nt(grad, up)
            r.bo[rows, :] += forward
            r.gn2[rows, :] += backward
            r.small[pl.ds(8 + s, 1), :] += jnp.sum(grad.astype(F32), 0, keepdims=True)

        loop(Tm // TILE, tile)
        r.ffp[s, 0:hidden, :] = dot(r.nm2t[...], r.gp[...]).astype(BF)
        r.ffp[s, hidden : 2 * hidden, :] = dot_tn(r.act[...], r.cotv[...]).astype(BF)

    r.bo[...] = jnp.zeros((Tm, D), F32)
    r.gn2[...] = jnp.zeros((Tm, D), F32)
    lax.fori_loop(0, nm, lambda s, carry: (units(s), carry)[1], 0)

    def norm2_back(i):
        rows = rows_of(i, TILE)
        middle = r.mid[rows, :]
        r.outv[rows, :] = (middle + r.bo[rows, :] + r.db[...]).astype(BF)
        hat, scale = normalised(middle)
        upstream = r.gn2[rows, :]
        r.small[1:2, :] += jnp.sum(upstream * hat, 0, keepdims=True)
        r.small[2:3, :] += jnp.sum(upstream, 0, keepdims=True)
        grad = r.cotv[rows, :].astype(F32) + norm_back(upstream, hat, scale, r.g2[...])
        r.mid[rows, :] = grad
        r.small[3:4, :] += jnp.sum(grad, 0, keepdims=True)
        low_grad = grad.astype(BF)
        r.gb[rows, :] = low_grad
        back = dot_nt(low_grad, r.ow_g[...].reshape(D, D)).astype(BF)
        for s in range(nm):
            r.gas[s, rows, :] = back[:, s * L : (s + 1) * L]

    loop(Tm // TILE, norm2_back)
    for target in chunk_order[: nm - 1]:
        copy(r.gas.at[target], r.gar.at[m], "gaa", target, mp=target, got=m).start()
    r.gar[m] = r.gas[m]
    for s in range(nm):
        r.ffp[s, 2 * hidden : 2 * hidden + L, :] = dot_tn(r.arow[s], r.gb[...]).astype(BF)

    ff_core = [
        copy(r.ffp.at[sib], r.ffc.at[0], "ffc", 0, mp=sib),
        copy(r.ffp.at[farsib], r.ffc.at[1], "ffc", 1, mp=sib),
    ]
    out_mine = local(r.outv, r.out_o.at[mine], 6)
    out_y = copy(r.outv, r.out_o.at[mine], "oy", 0, mp=far)
    out_core = copy(r.outv, r.out_o.at[mine], "oc", 0, mp=sib)
    for c in [*ff_core, out_mine, out_core]:
        c.start()

    for target in chunk_order[: nm - 1]:
        copy(r.gar.at[target], r.gar.at[target], "gaa", target, mp=target).wait_recv()
    out_y.start()

    def grad_rows(i):
        rows = rows_of(i, TILE)
        s = i // per_chunk
        inner = rows_of(i - s * per_chunk, TILE)
        grad = r.gar[s, inner, :].astype(F32)
        inv = r.inv[rows, :]
        scaled = grad * inv
        g_roll, s_roll = roll_half(grad), roll_half(scaled)
        r.gad[0, rows, :] = halves(grad, g_roll).astype(BF)
        r.gad[1, rows, :] = halves(g_roll, grad).astype(BF)
        r.gg[0, rows, :] = halves(scaled, s_roll).astype(BF)
        r.gg[1, rows, :] = halves(s_roll, scaled).astype(BF)
        product = scaled * r.attf[rows, :]
        r.gd[rows, :] = -halves(
            jnp.sum(jnp.where(low, product, 0.0), -1, keepdims=True),
            jnp.sum(jnp.where(low, 0.0, product), -1, keepdims=True),
        )

    loop(tiles, grad_rows)

    def head_column(values, h):
        return values[:, h * HD : h * HD + 1]

    for h in range(H):
        column = r.gd[:, h * HD : h * HD + 1]
        top = column.astype(BF).astype(F32)
        upper = lane((1, 2 * plan.G8)) < plan.G8
        weights = r.oh2[...] * jnp.where(upper, top, column - top).astype(BF)
        summed = dot_tn(weights, r.qf[:, h * M : (h + 1) * M])
        summed = summed[: plan.G8] + summed[plan.G8 :]
        r.tp[:, :, h * M : (h + 1) * M] = summed.reshape(n, PAD, M)
    scatter_states([r.gg[0], r.gg[1]], "rs2", "rst2")

    def contract(rows, dup, all_s, h):
        hs = slice(h * M, (h + 1) * M)

        def pair(p, total):
            blocks = state_pair(all_s, p, r.stage_a if plan.big else None)
            right = jnp.concatenate([blocks[0, hs, :], blocks[1, hs, :]], 1)
            return total + dot_nt(masked_pair(rows, dup[h, rows, :], p), right)

        total = jnp.zeros((TILE, M), F32)
        if plan.big:
            return lax.fori_loop(0, n2, pair, total)
        for p in range(n2):
            total = pair(p, total)
        return total

    def feature_back(rows, which, grad_features):
        u = r.qk[which, rows, :]
        weighted = (grad_features * phi(u)).astype(BF)
        both = dot(weighted, r.wb[...])
        return (
            both[:, :L] * SCALE - both[:, L:] * u.astype(F32) * (SCALE * SCALE)
        ).astype(BF)

    def query_back(i):
        rows = rows_of(i, TILE)
        totals = own_totals(rows)
        inv, gd = r.inv[rows, :], r.gd[rows, :]
        parts = [
            contract(rows, r.gad, r.sall, h) * head_column(inv, h)
            + totals[:, h * M : (h + 1) * M] * head_column(gd, h)
            for h in range(H)
        ]
        r.grads[0, rows, :] = feature_back(rows, 0, jnp.concatenate(parts, 1))

    loop(tiles, query_back)
    for target in chunk_order[: nm - 1]:
        copy(
            r.grads.at[0, rows_of(target, Tm)], r.garr.at[m, 0], "grq", target, mp=target, got=m
        ).start()

    copy(r.ffp.at[m], r.ffc.at[0], "ffc", 0, mp=sib).wait_recv()
    copy(r.ffp.at[far], r.ffc.at[1], "ffc", 1, mp=sib).wait_recv()
    for c in ff_core:
        c.wait_send()
    step = 128

    def core_sum(i):
        rows = rows_of(i, step)
        r.ffp[far, rows, :] = (
            r.ffp[far, rows, :].astype(F32) + r.ffc[1, rows, :].astype(F32)
        ).astype(BF)

    loop(plan.used // step, core_sum)
    used = pl.ds(0, plan.used)
    ff_y = copy(r.ffp.at[far], r.ffy.at[used], "ffy", 0, mp=far)
    ff_y.start()

    reduce_states("rs2", "rst2", r.gall, r.gtall, "ag2", "agt2")

    ff_y.wait_recv()
    ff_y.wait_send()

    def y_sum(i):
        rows = rows_of(i, step)
        r.ffy[rows, :] = (
            r.ffp[m, rows, :].astype(F32)
            + r.ffc[0, rows, :].astype(F32)
            + r.ffy[rows, :].astype(F32)
        ).astype(BF)

    loop(plan.used // step, y_sum)

    class Reduction:
        def __init__(self, source, rx, rz, out, names, rows, lsem):
            self.source, self.rx, self.rz, self.out = source, rx, rz, out
            self.x, self.z, self.gz, self.gx = names
            self.rows, self.lsem = rows, lsem

        def block(self, k):
            return self.source(xme * n2 + k)

        def start(self):
            first = self.source(pl.ds((1 - xme) * n2, n2))
            self.sent = copy(first, self.rx, self.x, 0, dp=xpart)
            self.sent.start()

        def scatter(self):
            self.sent.wait()

            def add(k):
                ref = self.block(k)
                ref[...] = (ref[...].astype(F32) + self.rx[k].astype(F32)).astype(BF)

            loop(n2, add)

            def send(k):
                z = lax.rem(zme + 1 + k, n2)
                copy(self.block(z), self.rz.at[zme], self.z, z, dp=2 * z + xme, got=zme).start()

            loop(n2 - 1, send)

        def gather(self):
            own = self.block(zme)

            total = own[...].astype(F32)

            def take(k, total):
                z = lax.rem(zme + 1 + k, n2)
                copy(self.block(z), self.rz.at[z], self.z, z, dp=2 * z + xme).wait()
                return total + self.rz[z].astype(F32)

            if n2 <= 4:
                for k in range(n2 - 1):
                    total = take(k, total)
            else:
                total = lax.fori_loop(0, n2 - 1, take, total)
            own[...] = total.astype(BF)
            spot = self.out.at[xme * n2 + zme]
            self.kept = local(own, spot, self.lsem)
            self.kept.start()

            def send(k):
                z = lax.rem(zme + 1 + k, n2)
                copy(own, spot, self.gz, z, dp=2 * z + xme, got=zme).start()

            loop(n2 - 1, send)

        def spread(self):
            own = self.block(zme)
            self.kept.wait()

            def wait(k):
                z = lax.rem(zme + 1 + k, n2)
                copy(own, self.out.at[xme * n2 + z], self.gz, z, dp=2 * z + xme).wait()

            loop(n2 - 1, wait)
            half = self.out.at[pl.ds(xme * n2, n2)]
            self.last = copy(half, half, self.gx, 0, dp=xpart)
            self.last.start()

        def finish(self):
            half = self.out.at[pl.ds((1 - xme) * n2, n2)]
            copy(half, half, self.gx, 0, dp=xpart).wait_recv()
            self.last.wait_send()

    rp, rq = plan.rp, plan.rq

    def ff_block(index):
        return r.ffy.reshape(n, rp, D).at[index]

    ff = Reduction(ff_block, r.ffx, r.ffz, r.ffg_o, ("ffx", "ffz", "ffgz", "ffgx"), rp, 7)
    ff.start()

    out_far = rows_of(far, Tm)
    copy(r.outv, r.out_o.at[out_far], "oy", 0, mp=far).wait_recv()
    out_on = copy(r.out_o.at[out_far], r.out_o.at[out_far], "oc", 1, mp=sib)
    out_on.start()

    gathered_states("rs2", "rst2", r.gall, r.gtall, "ag2", "agt2")

    def key_back(i):
        rows = rows_of(i, TILE)
        totals = own_totals(rows)
        parts = [
            contract(rows, r.vv, r.gall, h) + totals[:, h * M : (h + 1) * M] for h in range(H)
        ]
        r.grads[1, rows, :] = feature_back(rows, 1, jnp.concatenate(parts, 1))
        r.grads[2, rows, :] = select_heads(rows, r.kf[rows, :], r.gall).astype(BF)

    def send_grads(k, target):
        if k < nm - 1:
            spot = rows_of(target, Tm)
            copy(
                r.grads.at[pl.ds(1, 2), spot], r.garr.at[m, pl.ds(1, 2)], "grk", target, mp=target, got=m
            ).start()
        else:
            for a in range(3):
                r.garr[m, a] = r.grads[a, rows_of(m, Tm), :]

    chunks(key_back, send_grads)
    ff.scatter()

    for a in range(3):
        part = dot_tn(r.nm[...], r.grads[a]).astype(BF)
        r.qkvp.reshape(n * rq, L)[a * D : (a + 1) * D, :] = part
    qkv = Reduction(
        lambda index: r.qkvp.at[index], r.qkvx, r.qkvz, r.qkvg_o, ("qx", "qz", "qgz", "qgx"), rq, 8
    )
    qkv.start()

    for target in chunk_order[: nm - 1]:
        copy(r.garr.at[target, 0], r.garr.at[target, 0], "grq", target, mp=target).wait_recv()
        pair = r.garr.at[target, pl.ds(1, 2)]
        copy(pair, pair, "grk", target, mp=target).wait_recv()

    def norm1_back(i):
        rows = rows_of(i, TILE)
        upstream = jnp.zeros((TILE, D), F32)
        for s in range(nm):
            left = jnp.concatenate([r.garr[s, a, rows, :] for a in range(3)], 1)
            right = jnp.concatenate([r.wq_g[s, a] for a in range(3)], 1)
            upstream += dot_nt(left, right)
        upstream = upstream.astype(BF).astype(F32)
        hat, scale = normalised(r.tokv[rows, :].astype(F32))
        r.small[4:5, :] += jnp.sum(upstream * hat, 0, keepdims=True)
        r.small[5:6, :] += jnp.sum(upstream, 0, keepdims=True)
        r.gtv[rows, :] = (r.mid[rows, :] + norm_back(upstream, hat, scale, r.g1[...])).astype(BF)

    loop(Tm // TILE, norm1_back)
    tok_mine = local(r.gtv, r.gtok_o.at[mine], 9)
    tok_y = copy(r.gtv, r.gtok_o.at[mine], "ty", 0, mp=far)
    tok_core = copy(r.gtv, r.gtok_o.at[mine], "tc", 0, mp=sib)
    for c in (tok_y, tok_core, tok_mine):
        c.start()

    small_m = []
    for k, target in enumerate(chunk_order[: nm - 1]):
        c = copy(r.small, r.small_m.at[m], "sm", target, mp=target, got=m)
        c.start()
        small_m.append(c)
    ff.gather()
    qkv.scatter()
    total = r.small[...]
    for target in chunk_order[: nm - 1]:
        copy(r.small, r.small_m.at[target], "sm", target, mp=target).wait_recv()
        total += r.small_m[target]
    for c in small_m:
        c.wait_send()
    r.small_m[m] = total

    def small_send(k):
        j = lax.rem(me + 1 + k, n)
        copy(r.small_m.at[m], r.small_d.at[me], "sd", j, dp=j, got=me).start()

    loop(n - 1, small_send)
    qkv.gather()
    ff.spread()
    qkv.spread()
    r.small_o[...] = r.small_m[m]

    def small_take(k):
        j = lax.rem(me + 1 + k, n)
        copy(r.small_m.at[m], r.small_d.at[j], "sd", j, dp=j).wait()
        r.small_o[...] += r.small_d[j]

    loop(n - 1, small_take)
    r.small_o[6:7, :] = r.small_o[pl.ds(8 + m, 1), :]

    tok_far = rows_of(far, Tm)
    copy(r.gtv, r.gtok_o.at[tok_far], "ty", 0, mp=far).wait_recv()
    tok_on = copy(r.gtok_o.at[tok_far], r.gtok_o.at[tok_far], "tc", 1, mp=sib)
    tok_on.start()
    ff.finish()
    qkv.finish()
    for name, here in (("oc", r.out_o), ("tc", r.gtok_o)):
        for index, owner in enumerate((sib, farsib)):
            spot = here.at[rows_of(owner, Tm)]
            copy(spot, spot, name, index, mp=sib).wait_recv()
    for c in (out_y, out_core, out_on, tok_y, tok_core, tok_on):
        c.wait_send()
    for c in (out_mine, tok_mine):
        c.wait()
    for target in chunk_order[: nm - 1]:
        copy(
            r.attb.at[rows_of(target, Tm)], r.arow.at[m], "a2a", target, mp=target
        ).wait_send()
        copy(r.gas.at[target], r.gar.at[m], "gaa", target, mp=target).wait_send()
        spot = rows_of(target, Tm)
        copy(r.grads.at[0, spot], r.garr.at[m, 0], "grq", target, mp=target).wait_send()
        copy(
            r.grads.at[pl.ds(1, 2), spot], r.garr.at[m, pl.ds(1, 2)], "grk", target, mp=target
        ).wait_send()


def per_device(
    n,
    nm,
    tokens,
    cotangent,
    bucket,
    cell,
    features,
    qkv_weight,
    out_weight,
    out_bias,
    norm1_gain,
    norm1_bias,
    norm2_gain,
    norm2_bias,
    up_weight,
    up_bias,
    down_weight,
    down_bias,
):
    count, width = tokens.shape
    local, hidden = qkv_weight.shape[2], up_weight.shape[1]
    plan = Plan(n, nm, count, width, local, features.shape[2], hidden)
    spaces = {"vmem": pltpu.VMEM, "hbm": pl.ANY}
    line = lambda v: v.reshape(1, -1)
    grid_ids = (count // LANES, LANES)
    outs = pl.pallas_call(
        functools.partial(layer_kernel, plan),
        out_shape=[jax.ShapeDtypeStruct(s, d) for _, _, s, d in plan.outputs],
        in_specs=[pl.BlockSpec(memory_space=spaces[k]) for _, k in plan.inputs],
        out_specs=[pl.BlockSpec(memory_space=spaces[k]) for _, k, _, _ in plan.outputs],
        scratch_shapes=[pltpu.VMEM(s, d) for _, s, d in plan.scratch]
        + [pltpu.SemaphoreType.DMA((c,)) for c in plan.sems.values() for _ in range(2)]
        + [pltpu.SemaphoreType.DMA((plan.local_sems,))],
        compiler_params=pltpu.CompilerParams(
            collective_id=1, has_side_effects=True, vmem_limit_bytes=63 << 20
        ),
        name="performer_layer",
    )(
        tokens,
        bucket.reshape(grid_ids),
        cell.reshape(grid_ids),
        features,
        qkv_weight,
        line(norm1_gain),
        line(norm1_bias),
        line(out_bias),
        line(norm2_gain),
        line(norm2_bias),
        line(down_bias),
        cotangent,
        out_weight,
        up_weight,
        line(up_bias),
        down_weight,
    )
    output, grad_tokens, ff, qkv, small = outs[:5]
    ff = ff.reshape(-1, width).astype(F32)
    qkv = qkv.reshape(-1, local)[: 3 * width].astype(F32).reshape(3, width, local)
    return (
        output,
        grad_tokens.astype(F32),
        qkv,
        ff[2 * hidden : 2 * hidden + local],
        small[3],
        small[4],
        small[5],
        small[1],
        small[2],
        ff[:hidden],
        small[6],
        ff[hidden : 2 * hidden],
        small[0],
    )


def solution(mesh):
    return jax.shard_map(
        functools.partial(per_device, mesh.shape["dp"], mesh.shape["mp"]),
        mesh=mesh,
        in_specs=(
            P("dp", None),
            P("dp", None),
            P("dp", None),
            P("dp"),
            P(),
            P(None, None, "mp"),
            P("mp", None),
            P(),
            P(),
            P(),
            P(),
            P(),
            P(None, "mp"),
            P("mp"),
            P("mp", None),
            P(),
        ),
        out_specs=(
            P("dp", None),
            P("dp", None),
            P(None, None, "mp"),
            P("mp", None),
            P(),
            P(),
            P(),
            P(),
            P(),
            P(None, "mp"),
            P("mp"),
            P("mp", None),
            P(),
        ),
        check_vma=False,
    )
```

```python
import functools
from types import SimpleNamespace

import jax
import jax.numpy as jnp
from jax import lax
from jax.experimental import pallas as pl
from jax.experimental.pallas import tpu as pltpu
from jax.sharding import PartitionSpec as P

HD = 64
FEATS = 4
STEP = 5
SEG = 2
PAD = 8
SCALE = HD**-0.25
HALF_SQUARE = 0.5 * SCALE * SCALE
EPS = 1e-05

BF = jnp.bfloat16
F32 = jnp.float32
MESH = pl.DeviceIdType.MESH
LANES = 128
TILE = 256


def dot(a, b):
    return jnp.dot(a, b, preferred_element_type=F32)


def dot_nt(a, b):
    return lax.dot_general(a, b, (((1,), (1,)), ((), ())), preferred_element_type=F32)


def dot_tn(a, b):
    return lax.dot_general(a, b, (((0,), (0,)), ((), ())), preferred_element_type=F32)


def lane(shape):
    return lax.broadcasted_iota(jnp.int32, shape, len(shape) - 1)


def roll_half(x):
    return pltpu.roll(x, HD, 1)


def loop(count, body, unroll=False):
    if unroll or count <= 4:
        for i in range(count):
            body(i)
    else:

        def step(i, carry):
            body(i)
            return carry

        lax.fori_loop(0, count, step, 0)


def rows_of(i, size):
    if isinstance(i, int):
        return pl.ds(i * size, size)
    return pl.ds(pl.multiple_of(i * size, size), size)


def normalised(values):
    average = jnp.mean(values, -1, keepdims=True)
    centred = values - average
    spread = jnp.mean(centred * centred, -1, keepdims=True)
    scale = lax.rsqrt(spread + EPS)
    return centred * scale, scale


def norm_back(upstream, hat, scale, gain):
    e = gain * upstream
    return (
        e
        - jnp.mean(e, -1, keepdims=True)
        - hat * jnp.mean(e * hat, -1, keepdims=True)
    ) * scale


def round_up(a, b):
    return (a + b - 1) // b * b


class Plan:
    def __init__(self, n, nm, tokens, width, local, feats, hidden):
        self.n, self.nm, self.T, self.D, self.L, self.M, self.F = (
            n,
            nm,
            tokens,
            width,
            local,
            feats,
            hidden,
        )
        self.H = local // HD
        self.HM = self.H * feats
        self.Tm = tokens // nm
        self.big = n > 8
        self.G8 = n * PAD
        self.rest = hidden + local
        self.ru, self.rd, self.rq = (
            round_up((rows + n - 1) // n, 16) for rows in (hidden, self.rest, 3 * width)
        )
        n2 = n // 2
        T, D, L, HM, Tm = self.T, self.D, self.L, self.HM, self.Tm
        vm = "vmem"
        states = (n, HM, SEG * HD)
        place = "hbm" if self.big else vm
        self.inputs = [
            ("tok", "hbm"),
            ("bkt", vm),
            ("cel", vm),
            ("feat", vm),
            ("wqkv", vm),
            ("g1", vm),
            ("b1", vm),
            ("ob", vm),
            ("g2", vm),
            ("b2", vm),
            ("db", vm),
            ("cot", "hbm"),
            ("ow", "hbm"),
            ("up", "hbm"),
            ("ub", "hbm"),
            ("dn", "hbm"),
        ]
        self.outputs = [
            ("out_o", "hbm", (T, D), BF),
            ("gtok_o", "hbm", (T, D), BF),
            ("upg_o", "hbm", (n, self.ru, D), BF),
            ("dng_o", "hbm", (n, self.rd, D), BF),
            ("qkvg_o", "hbm", (n, self.rq, L), BF),
            ("small_o", vm, (16, D), F32),
        ]
        big_states = [("sp", states), ("rb", states), ("sall", states), ("gall", states)]
        if self.big:
            self.outputs += [(name, "hbm", shape, BF) for name, shape in big_states]
        self.scratch = [
            ("wcat", (D, 4 * L), BF),
            ("f2", (L, HM), BF),
            ("wb", (HM, 2 * L), BF),
            ("ccb", (T, LANES), BF),
            ("oh2", (T, 2 * self.G8), BF),
            ("nm", (T, D), BF),
            ("qk", (2, T, L), BF),
            ("vv", (2, T, L), BF),
            ("qf", (T, HM), BF),
            ("kf", (T, HM), BF),
            ("ft", (HM, T), BF),
            ("tp", (n, PAD, LANES), F32),
            ("trb", (n, PAD, LANES), F32),
            ("tall", (n, PAD, LANES), F32),
            ("gtall", (n, PAD, LANES), F32),
            ("tot2", (2 * self.G8, HM), BF),
            ("acc", (HM, SEG * HD), F32),
            ("attf", (T, L), F32),
            ("inv", (T, L), F32),
            ("attb", (T, L), BF),
            ("arow", (nm, Tm, L), BF),
            ("wq_g", (nm, 3, D, L), BF),
            ("ow_g", (nm, L, D), BF),
            ("up_g", (nm, D, hidden), BF),
            ("ub_g", (nm, 1, hidden), F32),
            ("dn_g", (nm, hidden, D), BF),
            ("cotv", (Tm, D), BF),
            ("tokv", (Tm, D), BF),
            ("mid", (Tm, D), F32),
            ("nm2", (Tm, D), BF),
            ("nm2t", (D, Tm), BF),
            ("act", (Tm, hidden), BF),
            ("gp", (Tm, hidden), BF),
            ("bo", (Tm, D), F32),
            ("gn2", (Tm, D), F32),
            ("gb", (Tm, D), BF),
            ("outv", (Tm, D), BF),
            ("small", (16, D), F32),
            ("small_m", (nm, 16, D), F32),
            ("small_d", (n, 16, D), F32),
            ("upp", (nm, hidden, D), BF),
            ("upc", (2, hidden, D), BF),
            ("upy", (n, self.ru, D), BF),
            ("upx", (n2, self.ru, D), BF),
            ("upz", (n2, self.ru, D), BF),
            ("dnp", (nm, self.rest, D), BF),
            ("dnc", (2, self.rest, D), BF),
            ("dny", (n, self.rd, D), BF),
            ("dnx", (n2, self.rd, D), BF),
            ("dnz", (n2, self.rd, D), BF),
            ("gas", (nm, Tm, L), BF),
            ("gar", (nm, Tm, L), BF),
            ("gad", (2, T, L), BF),
            ("gg", (2, T, L), BF),
            ("gd", (T, L), F32),
            ("grads", (3, T, L), BF),
            ("garr", (nm, 3, Tm, L), BF),
            ("qkvp", (n, self.rq, L), BF),
            ("qkvx", (n2, self.rq, L), BF),
            ("qkvz", (n2, self.rq, L), BF),
            ("gtv", (Tm, D), BF),
        ]
        if self.big:
            self.scratch += [("stage_a", (2, HM, SEG * HD), BF), ("stage_b", (2, HM, SEG * HD), BF)]
        else:
            self.scratch += [(name, shape, BF) for name, shape in big_states]
        self.sems = {
            "rsx": n2,
            "rtx": n2,
            "rsz": n2,
            "rtz": n2,
            "agz": n2,
            "atz": n2,
            "agx": n2,
            "atx": n2,
            "gsx": n2,
            "gtx": n2,
            "gsz": n2,
            "gtz": n2,
            "ggz": n2,
            "hgz": n2,
            "ggx": n2,
            "hgx": n2,
            "a2a": nm,
            "gaa": nm * (Tm // TILE),
            "grq": nm,
            "grk": nm,
            "wy": 5,
            "wc": 10,
            "uc": 2,
            "uy": 1,
            "ux": 1,
            "uz": n2,
            "ugz": n2,
            "ugx": 1,
            "dc": 2,
            "dy": 1,
            "dx": 1,
            "dz": n2,
            "dgz": n2,
            "dgx": 1,
            "qx": 1,
            "qz": n2,
            "qgz": n2,
            "qgx": 1,
            "oy": 1,
            "oc": 2,
            "ty": 1,
            "tc": 2,
            "sm": nm,
            "sd": n,
        }
        self.local_sems = 16

    def names(self):
        return (
            [x[0] for x in self.inputs]
            + [x[0] for x in self.outputs]
            + [x[0] for x in self.scratch]
            + [f"{k}_{end}" for k in self.sems for end in ("s", "r")]
            + ["lsem"]
        )


def layer_kernel(plan, *refs):
    r = SimpleNamespace(**dict(zip(plan.names(), refs, strict=True)))
    n, nm, T, D, L, M, HM, Tm, H = (
        plan.n,
        plan.nm,
        plan.T,
        plan.D,
        plan.L,
        plan.M,
        plan.HM,
        plan.Tm,
        plan.H,
    )
    hidden = plan.F
    n2 = n // 2
    tiles = T // TILE
    me, m = lax.axis_index("dp"), lax.axis_index("mp")
    sib = m + 1 - 2 * lax.rem(m, 2)
    far = lax.rem(m + nm // 2, nm)
    farsib = lax.rem(sib + nm // 2, nm)
    xpart = me + 1 - 2 * lax.rem(me, 2)
    xme, zme = lax.rem(me, 2), me // 2

    def sem(name, index):
        return getattr(r, f"{name}_s").at[index], getattr(r, f"{name}_r").at[index]

    def copy(src, dst, name, sent, dp=None, mp=None, got=None):
        send, _ = sem(name, sent)
        _, recv = sem(name, sent if got is None else got)
        return pltpu.make_async_remote_copy(
            src_ref=src,
            dst_ref=dst,
            send_sem=send,
            recv_sem=recv,
            device_id=(me if dp is None else dp, m if mp is None else mp),
            device_id_type=MESH,
        )

    def local(src, dst, index):
        return pltpu.make_async_copy(src, dst, r.lsem.at[index])

    low = lane((1, LANES)) < HD

    barrier = pltpu.get_barrier_semaphore()

    def greet(k):
        pl.semaphore_signal(
            barrier, inc=1, device_id=(lax.rem(me + 1 + k, n), m), device_id_type=MESH
        )

    loop(n - 1, greet)
    for k in range(1, nm):
        pl.semaphore_signal(
            barrier, inc=1, device_id=(me, lax.rem(m + k, nm)), device_id_type=MESH
        )

    mine = rows_of(m, Tm)
    tok_in = local(r.tok, r.nm, 10)
    own_in = [local(r.cot.at[mine], r.cotv, 0), local(r.tok.at[mine], r.tokv, 11)]
    for c in [tok_in, *own_in]:
        c.start()

    r.wcat[:, 0:L] = r.wqkv[0]
    r.wcat[:, L : 2 * L] = r.wqkv[1]
    wv = r.wqkv[2].astype(F32)
    wv_rolled = roll_half(wv)
    r.wcat[:, 2 * L : 3 * L] = jnp.where(low, wv, wv_rolled).astype(BF)
    r.wcat[:, 3 * L : 4 * L] = jnp.where(low, wv_rolled, wv).astype(BF)
    feature_rows = r.feat[STEP % FEATS]
    r.f2[...] = jnp.zeros((L, HM), BF)
    for h in range(H):
        r.f2[h * HD : (h + 1) * HD, h * M : (h + 1) * M] = feature_rows
    r.wb[:, 0:L] = r.f2[...].astype(F32).T.astype(BF)
    head_of_row = lax.broadcasted_iota(jnp.int32, (HM, L), 0) // M
    r.wb[:, L : 2 * L] = jnp.where(head_of_row == lane((HM, L)) // HD, 1.0, 0.0).astype(BF)

    count = T // LANES
    numbers = SEG * r.bkt[...].astype(F32) + r.cel[...].astype(F32)
    numbers = jnp.concatenate([numbers, jnp.zeros((LANES - count, LANES), F32)], 0).T
    for i in range(count):
        rows = pl.ds(i * LANES, LANES)
        column = jnp.broadcast_to(numbers[:, i : i + 1], (LANES, LANES))
        r.ccb[rows, :] = (column - jnp.where(low, 0.0, 1.0)).astype(BF)
        for block in range(2 * plan.G8 // LANES):
            place = (lane((1, LANES)) + block * LANES) % plan.G8
            number = place // PAD * SEG + place % SEG
            r.oh2[rows, block * LANES : (block + 1) * LANES] = jnp.where(
                column == number.astype(F32), 1.0, 0.0
            ).astype(BF)
    part_of_row = lax.broadcasted_iota(jnp.int32, (plan.G8, LANES), 0) % PAD // SEG

    def pack_totals(table):
        packed = jnp.zeros((plan.G8, LANES), F32)
        for q in range(HM // LANES):
            packed += jnp.where(part_of_row == q, table[:, q * LANES : (q + 1) * LANES], 0.0)
        return packed.reshape(n, PAD, LANES)

    def spread_totals(packed):
        packed = packed.reshape(plan.G8, LANES)
        return jnp.concatenate(
            [jnp.where(part_of_row == q, packed, 0.0) for q in range(HM // LANES)], 1
        )

    def phi(u):
        wide = u.astype(F32)
        squares = wide * wide
        first = jnp.sum(jnp.where(low, squares, 0.0), -1, keepdims=True)
        second = jnp.sum(jnp.where(low, 0.0, squares), -1, keepdims=True)
        projected = dot(u, r.f2[...]) * SCALE
        shift = jnp.where(lane((1, HM)) < M, first, second) * HALF_SQUARE
        return jnp.exp(projected - shift)

    tok_in.wait()
    pl.semaphore_wait(barrier, n - 1 + nm - 1)

    def project(i):
        rows = rows_of(i, TILE)
        hat, _ = normalised(r.nm[rows, :].astype(F32))
        normed = (hat * r.g1[...] + r.b1[...]).astype(BF)
        r.nm[rows, :] = normed
        u = dot(normed, r.wcat[:, L:]).astype(BF)
        k = u[:, 0:L]
        r.qk[1, rows, :] = k
        r.vv[0, rows, :], r.vv[1, rows, :] = u[:, L : 2 * L], u[:, 2 * L : 3 * L]
        features = phi(k)
        r.kf[rows, :] = features.astype(BF)
        r.ft[:, rows] = features.T.astype(BF)

    def queries(i):
        rows = rows_of(i, TILE)
        q = dot(r.nm[rows, :], r.wcat[:, 0:L]).astype(BF)
        r.qk[0, rows, :] = q
        r.qf[rows, :] = phi(q).astype(BF)

    shards = [
        (r.wqkv, r.wq_g),
        (r.ow, r.ow_g),
        (r.up, r.up_g),
        (r.ub, r.ub_g),
        (r.dn, r.dn_g),
    ]
    own_copies, y_copies, core_copies = [], [], []
    for i, (src, dst) in enumerate(shards):
        own_copies.append(local(src, dst.at[m], 1 + i))
        y_copies.append(copy(src, dst.at[m], "wy", i, mp=far))
        core_copies.append(copy(src, dst.at[m], "wc", 2 * i, mp=sib))
    for c in own_copies + y_copies + core_copies:
        c.start()
    loop(tiles, project)

    def state_pair(ref, p, stage):
        if plan.big:
            pltpu.sync_copy(ref.at[pl.ds(2 * p, 2)], stage)
            return stage
        return ref.at[pl.ds(2 * p, 2)]

    def masked_pair(rows, dup, p):
        code = r.ccb[rows, :]
        first = jnp.full((1, LANES), 1.0, F32) * (4 * p)
        left = jnp.where(code == first.astype(BF), dup, jnp.zeros_like(dup))
        right = jnp.where(code == (first + 2.0).astype(BF), dup, jnp.zeros_like(dup))
        return jnp.concatenate([left, right], 1)

    everything = pl.ds(0, T)

    class States:
        def __init__(self, all_s, all_t, names):
            self.all_s, self.all_t = all_s, all_t
            self.x, self.tx, self.z, self.tz, self.gz, self.hz, self.gx, self.hx = names

        def to_x(self, p):
            j = 2 * p + 1 - xme
            return [
                copy(r.sp.at[j], r.rb.at[p], self.x, p, dp=xpart),
                copy(r.tp.at[j], r.trb.at[p], self.tx, p, dp=xpart),
            ]

        def to_z(self, p):
            j = 2 * p + xme
            return [
                copy(r.sp.at[j], r.rb.at[n2 + zme], self.z, p, dp=j, got=zme),
                copy(r.tp.at[j], r.trb.at[n2 + zme], self.tz, p, dp=j, got=zme),
            ]

        def from_z(self, p):
            j = 2 * p + xme
            return [
                copy(r.sp.at[j], r.rb.at[n2 + p], self.z, p, dp=j),
                copy(r.tp.at[j], r.trb.at[n2 + p], self.tz, p, dp=j),
            ]

        def out_z(self, p):
            j = 2 * p + xme
            return [
                copy(self.all_s.at[me], self.all_s.at[me], self.gz, p, dp=j, got=zme),
                copy(self.all_t.at[me], self.all_t.at[me], self.hz, p, dp=j, got=zme),
            ]

        def in_z(self, p):
            j = 2 * p + xme
            return [
                copy(self.all_s.at[j], self.all_s.at[j], self.gz, p, dp=j),
                copy(self.all_t.at[j], self.all_t.at[j], self.hz, p, dp=j),
            ]

        def out_x(self, p):
            j = 2 * p + xme
            return [
                copy(self.all_s.at[j], self.all_s.at[j], self.gx, p, dp=xpart),
                copy(self.all_t.at[j], self.all_t.at[j], self.hx, p, dp=xpart),
            ]

        def in_x(self, p):
            j = 2 * p + 1 - xme
            return [
                copy(self.all_s.at[j], self.all_s.at[j], self.gx, p, dp=xpart),
                copy(self.all_t.at[j], self.all_t.at[j], self.hx, p, dp=xpart),
            ]

        def start(self, dup):
            def pair(kk):
                p = lax.rem(zme + 1 + kk, n2)
                staged = r.stage_a if plan.big else r.sp.at[pl.ds(2 * p, 2)]
                for h in range(H):
                    hs = slice(h * M, (h + 1) * M)
                    block = dot(r.ft[hs, :], masked_pair(everything, dup[h], p))
                    staged[0, hs, :] = block[:, :LANES].astype(BF)
                    staged[1, hs, :] = block[:, LANES:].astype(BF)
                if plan.big:
                    pltpu.sync_copy(r.stage_a, r.sp.at[pl.ds(2 * p, 2)])
                for c in self.to_x(p):
                    c.start()

            loop(n2, pair)

        def add_x(self, p):
            for c in self.to_x(p):
                c.wait_recv()
            j = 2 * p + xme
            r.tp[j] += r.trb[p]
            if plan.big:
                pltpu.sync_copy(r.sp.at[pl.ds(j, 1)], r.stage_b.at[pl.ds(0, 1)])
                pltpu.sync_copy(r.rb.at[pl.ds(p, 1)], r.stage_b.at[pl.ds(1, 1)])
                return r.stage_b[0].astype(F32) + r.stage_b[1].astype(F32)
            return r.sp[j].astype(F32) + r.rb[p].astype(F32)

        def combine(self, between):
            def step(k):
                p = lax.rem(zme + 1 + k, n2)
                j = 2 * p + xme
                total = self.add_x(p).astype(BF)
                if plan.big:
                    r.stage_b[0] = total
                    pltpu.sync_copy(r.stage_b.at[pl.ds(0, 1)], r.sp.at[pl.ds(j, 1)])
                else:
                    r.sp[j] = total
                for c in self.to_z(p):
                    c.start()

            for k in range(n2 - 1) if n2 <= 4 else ():
                step(k)
                between()
            if n2 > 4:
                loop(n2 - 1, step)
            r.acc[...] = self.add_x(zme)
            between(everything=True)

            def take(k):
                p = lax.rem(zme + 1 + k, n2)
                for c in self.from_z(p):
                    c.wait_recv()
                if plan.big:
                    pltpu.sync_copy(r.rb.at[pl.ds(n2 + p, 1)], r.stage_b.at[pl.ds(0, 1)])
                    r.acc[...] += r.stage_b[0].astype(F32)
                else:
                    r.acc[...] += r.rb[n2 + p].astype(F32)
                r.tp[me] += r.trb[n2 + p]

            loop(n2 - 1, take)
            self.all_t[me] = r.tp[me]
            if plan.big:
                r.stage_b[0] = r.acc[...].astype(BF)
                pltpu.sync_copy(r.stage_b.at[pl.ds(0, 1)], self.all_s.at[pl.ds(me, 1)])
            else:
                self.all_s[me] = r.acc[...].astype(BF)

            def send(k):
                for c in self.out_z(lax.rem(zme + 1 + k, n2)):
                    c.start()

            loop(n2 - 1, send)
            for c in self.out_x(zme):
                c.start()

        def onward(self):
            def step(k):
                p = lax.rem(zme + 1 + k, n2)
                for c in self.in_z(p):
                    c.wait_recv()
                for c in self.out_x(p):
                    c.start()

            loop(n2 - 1, step)

        def finish(self):
            def wait(p):
                for c in self.in_x(p):
                    c.wait_recv()
                for c in [*self.to_x(p), *self.out_x(p)]:
                    c.wait_send()

            loop(n2, wait)

            def sent(k):
                p = lax.rem(zme + 1 + k, n2)
                for c in [*self.to_z(p), *self.out_z(p)]:
                    c.wait_send()

            loop(n2 - 1, sent)
            total = spread_totals(self.all_t[...])
            top = total.astype(BF)
            r.tot2[0 : plan.G8, :] = top
            r.tot2[plan.G8 :, :] = (total - top.astype(F32)).astype(BF)

    class Meanwhile:
        def __init__(self, each, pieces):
            self.each, self.pieces = each, list(pieces)

        def __call__(self, everything=False):
            many = len(self.pieces) if everything else self.each
            for piece in self.pieces[:many]:
                piece()
            self.pieces = self.pieces[many:]

    first = States(
        r.sall, r.tall, ("rsx", "rtx", "rsz", "rtz", "agz", "atz", "agx", "atx")
    )
    r.tp[...] = pack_totals(dot_tn(r.oh2[:, : plan.G8], r.kf[...]))
    first.start([r.vv[0], r.vv[1]])

    onward = []

    def weights_on():
        for i, (_, dst) in enumerate(shards):
            copy(dst.at[far], dst.at[far], "wy", i, mp=far).wait_recv()
            c = copy(dst.at[far], dst.at[far], "wc", 2 * i + 1, mp=sib)
            c.start()
            onward.append(c)

    def turn(i):
        rows = rows_of(i, TILE)
        r.ft[:, rows] = r.qf[rows, :].astype(F32).T.astype(BF)

    def query_pair(i):
        return lambda: loop(2, lambda k: queries(2 * i + k))

    first.combine(Meanwhile(1, [query_pair(i) for i in range(tiles // 2)]))
    loop(tiles, turn)
    first.onward()
    weights_on()
    first.finish()

    def select_heads(rows, left, all_s):
        code = r.ccb[rows, :].astype(F32)

        def pair(h, p, total):
            hs = slice(h * M, (h + 1) * M)
            blocks = state_pair(all_s, p, r.stage_a if plan.big else None)
            right = jnp.concatenate([blocks[0, hs, :], blocks[1, hs, :]], 1)
            product = dot(left[:, hs], right)
            first = jnp.full((1, LANES), 1.0, F32) * (4 * p)
            total = jnp.where(code == first, product[:, :LANES], total)
            return jnp.where(code == first + 2.0, product[:, LANES:], total)

        heads = []
        for h in range(H):
            total = jnp.zeros((left.shape[0], LANES), F32)
            if plan.big:
                total = lax.fori_loop(0, n2, functools.partial(pair, h), total)
            else:
                for p in range(n2):
                    total = pair(h, p, total)
            heads.append(total + roll_half(total))
        return jnp.where(low, heads[0], heads[1])

    def own_totals(rows):
        return dot(r.oh2[rows, :], r.tot2[...])

    def halves(first, second):
        return jnp.where(low, first, second)

    def attend(i):
        rows = rows_of(i, TILE)
        queries = r.qf[rows, :]
        numerator = select_heads(rows, queries, r.sall)
        product = queries.astype(F32) * own_totals(rows)
        denominator = halves(
            jnp.sum(product[:, :M], -1, keepdims=True),
            jnp.sum(product[:, M:], -1, keepdims=True),
        )
        attention = numerator / denominator
        r.attf[rows, :] = attention
        r.inv[rows, :] = 1.0 / denominator
        r.attb[rows, :] = attention.astype(BF)

    per_chunk = Tm // TILE
    chunk_order = [far, farsib, sib, m]

    def chunks(body, after):
        for k, target in enumerate(chunk_order):
            loop(per_chunk, lambda i, target=target: body(target * per_chunk + i))
            after(k, target)

    def send_attention(k, target):
        if k < nm - 1:
            copy(
                r.attb.at[rows_of(target, Tm)], r.arow.at[m], "a2a", target, mp=target, got=m
            ).start()
        else:
            r.arow[m] = r.attb[rows_of(m, Tm), :]

    chunks(attend, send_attention)

    for c in own_copies:
        c.wait()
    for i, (_, dst) in enumerate(shards):
        copy(dst.at[sib], dst.at[sib], "wc", 2 * i, mp=sib).wait_recv()
        copy(dst.at[farsib], dst.at[farsib], "wc", 2 * i + 1, mp=sib).wait_recv()
    for c in y_copies + core_copies + onward:
        c.wait_send()
    for c in own_in:
        c.wait()
    for target in chunk_order[: nm - 1]:
        copy(r.arow.at[target], r.arow.at[target], "a2a", target, mp=target).wait_recv()

    r.small[...] = jnp.zeros((16, D), F32)

    def project_out(i):
        rows = rows_of(i, TILE)
        columns = jnp.concatenate([r.arow[s, rows, :] for s in range(nm)], 1)
        branch = dot(columns, r.ow_g[...].reshape(D, D)).astype(BF).astype(F32)
        middle = r.tokv[rows, :].astype(F32) + branch + r.ob[...]
        r.mid[rows, :] = middle
        hat, _ = normalised(middle)
        normed = hat * r.g2[...] + r.b2[...]
        r.nm2[rows, :] = normed.astype(BF)
        r.nm2t[:, rows] = normed.T.astype(BF)
        r.small[0:1, :] += jnp.sum(r.cotv[rows, :].astype(F32), 0, keepdims=True)

    loop(Tm // TILE, project_out)

    def units(s):
        up, down = r.up_g[s], r.dn_g[s]

        def tile(i):
            rows = rows_of(i, TILE)
            preact = dot(r.nm2[rows, :], up) + r.ub_g[s]
            spread = 0.5 + 0.5 * lax.erf(preact * (0.5**0.5))
            active = (preact * spread).astype(BF)
            r.act[rows, :] = active
            slope = spread + preact * jnp.exp(preact * preact * -0.5) * 0.3989422804014327
            grad = (dot_nt(r.cotv[rows, :], down) * slope).astype(BF)
            r.gp[rows, :] = grad
            forward, backward = dot(active, down), dot_nt(grad, up)
            r.bo[rows, :] += forward
            r.gn2[rows, :] += backward
            r.small[pl.ds(8 + s, 1), :] += jnp.sum(grad.astype(F32), 0, keepdims=True)

        loop(Tm // TILE, tile)
        r.upp[s] = dot(r.nm2t[...], r.gp[...]).astype(BF)
        r.dnp[s, 0:hidden, :] = dot_tn(r.act[...], r.cotv[...]).astype(BF)

    r.bo[...] = jnp.zeros((Tm, D), F32)
    r.gn2[...] = jnp.zeros((Tm, D), F32)
    lax.fori_loop(0, nm, lambda s, carry: (units(s), carry)[1], 0)

    def norm2_back(i):
        rows = rows_of(i, TILE)
        middle = r.mid[rows, :]
        r.outv[rows, :] = (middle + r.bo[rows, :] + r.db[...]).astype(BF)
        hat, scale = normalised(middle)
        upstream = r.gn2[rows, :]
        r.small[1:2, :] += jnp.sum(upstream * hat, 0, keepdims=True)
        r.small[2:3, :] += jnp.sum(upstream, 0, keepdims=True)
        grad = r.cotv[rows, :].astype(F32) + norm_back(upstream, hat, scale, r.g2[...])
        r.mid[rows, :] = grad
        r.small[3:4, :] += jnp.sum(grad, 0, keepdims=True)
        low_grad = grad.astype(BF)
        r.gb[rows, :] = low_grad
        back = dot_nt(low_grad, r.ow_g[...].reshape(D, D)).astype(BF)
        for s in range(nm):
            r.gas[s, rows, :] = back[:, s * L : (s + 1) * L]
        for target in chunk_order[: nm - 1]:
            grad_copy(target, i).start()

    def grad_copy(target, i):
        rows = rows_of(i, TILE)
        spot = target * per_chunk + i
        return copy(
            r.gas.at[target, rows],
            r.gar.at[m, rows],
            "gaa",
            spot,
            mp=target,
            got=m * per_chunk + i,
        )

    def grad_arrival(target, i):
        rows = r.gar.at[target, rows_of(i, TILE)]
        return copy(rows, rows, "gaa", target * per_chunk + i, mp=target)

    up_core = [
        copy(r.upp.at[sib], r.upc.at[0], "uc", 0, mp=sib),
        copy(r.upp.at[farsib], r.upc.at[1], "uc", 1, mp=sib),
    ]
    dn_core = [
        copy(r.dnp.at[sib], r.dnc.at[0], "dc", 0, mp=sib),
        copy(r.dnp.at[farsib], r.dnc.at[1], "dc", 1, mp=sib),
    ]
    for c in up_core:
        c.start()
    loop(Tm // TILE, norm2_back)
    r.gar[m] = r.gas[m]
    for s in range(nm):
        r.dnp[s, hidden : hidden + L, :] = dot_tn(r.arow[s], r.gb[...]).astype(BF)
    out_mine = local(r.outv, r.out_o.at[mine], 6)
    out_y = copy(r.outv, r.out_o.at[mine], "oy", 0, mp=far)
    out_core = copy(r.outv, r.out_o.at[mine], "oc", 0, mp=sib)
    for c in [*dn_core, out_mine, out_core]:
        c.start()

    def core_sum(copies, part, other, y, name):
        for c in copies:
            c.wait()
        rows = part.shape[1]

        def add(i):
            strip = rows_of(i, LANES)
            part[far, strip, :] = (
                part[far, strip, :].astype(F32) + other[1, strip, :].astype(F32)
            ).astype(BF)

        loop(rows // LANES, add)
        flat = y.reshape(y.shape[0] * y.shape[1], D).at[pl.ds(0, rows)]
        return copy(part.at[far], flat, name, 0, mp=far)

    def y_sum(sent, part, other, y):
        sent.wait()
        flat = y.reshape(y.shape[0] * y.shape[1], D)

        def add(i):
            strip = rows_of(i, LANES)
            flat[strip, :] = (
                part[m, strip, :].astype(F32)
                + other[0, strip, :].astype(F32)
                + flat[strip, :].astype(F32)
            ).astype(BF)

        loop(part.shape[1] // LANES, add)

    up_y = core_sum(up_core, r.upp, r.upc, r.upy, "uy")
    for target in chunk_order[: nm - 1]:
        for i in range(per_chunk):
            grad_arrival(target, i).wait_recv()
    up_y.start()

    def grad_rows(i):
        rows = rows_of(i, TILE)
        s = i // per_chunk
        inner = rows_of(i - s * per_chunk, TILE)
        grad = r.gar[s, inner, :].astype(F32)
        inv = r.inv[rows, :]
        scaled = grad * inv
        g_roll, s_roll = roll_half(grad), roll_half(scaled)
        r.gad[0, rows, :] = halves(grad, g_roll).astype(BF)
        r.gad[1, rows, :] = halves(g_roll, grad).astype(BF)
        r.gg[0, rows, :] = halves(scaled, s_roll).astype(BF)
        r.gg[1, rows, :] = halves(s_roll, scaled).astype(BF)
        product = scaled * r.attf[rows, :]
        r.gd[rows, :] = -halves(
            jnp.sum(jnp.where(low, product, 0.0), -1, keepdims=True),
            jnp.sum(jnp.where(low, 0.0, product), -1, keepdims=True),
        )

    loop(tiles, grad_rows)

    def head_column(values, h):
        return values[:, h * HD : h * HD + 1]

    head_totals = []
    for h in range(H):
        column = r.gd[:, h * HD : h * HD + 1]
        top = column.astype(BF).astype(F32)
        upper = lane((1, 2 * plan.G8)) < plan.G8
        weights = r.oh2[...] * jnp.where(upper, top, column - top).astype(BF)
        summed = dot_tn(weights, r.qf[:, h * M : (h + 1) * M])
        head_totals.append(summed[: plan.G8] + summed[plan.G8 :])
    r.tp[...] = pack_totals(jnp.concatenate(head_totals, 1))
    second = States(
        r.gall, r.gtall, ("gsx", "gtx", "gsz", "gtz", "ggz", "hgz", "ggx", "hgx")
    )
    second.start([r.gg[0], r.gg[1]])
    dn_y = core_sum(dn_core, r.dnp, r.dnc, r.dny, "dy")
    dn_y.start()

    def contract(rows, dup, all_s, h):
        hs = slice(h * M, (h + 1) * M)

        def pair(p, total):
            blocks = state_pair(all_s, p, r.stage_a if plan.big else None)
            right = jnp.concatenate([blocks[0, hs, :], blocks[1, hs, :]], 1)
            return total + dot_nt(masked_pair(rows, dup[h, rows, :], p), right)

        total = jnp.zeros((TILE, M), F32)
        if plan.big:
            return lax.fori_loop(0, n2, pair, total)
        for p in range(n2):
            total = pair(p, total)
        return total

    def feature_back(rows, which, grad_features):
        u = r.qk[which, rows, :]
        weighted = (grad_features * phi(u)).astype(BF)
        both = dot(weighted, r.wb[...])
        return (
            both[:, :L] * SCALE - both[:, L:] * u.astype(F32) * (SCALE * SCALE)
        ).astype(BF)

    def query_back(i):
        rows = rows_of(i, TILE)
        totals = own_totals(rows)
        inv, gd = r.inv[rows, :], r.gd[rows, :]
        parts = [
            contract(rows, r.gad, r.sall, h) * head_column(inv, h)
            + totals[:, h * M : (h + 1) * M] * head_column(gd, h)
            for h in range(H)
        ]
        r.grads[0, rows, :] = feature_back(rows, 0, jnp.concatenate(parts, 1))

    def query_back_pair(i):
        return lambda: loop(2, lambda k: query_back(2 * i + k))

    second.combine(Meanwhile(1, [query_back_pair(i) for i in range(tiles // 2)]))
    for target in chunk_order[: nm - 1]:
        copy(
            r.grads.at[0, rows_of(target, Tm)], r.garr.at[m, 0], "grq", target, mp=target, got=m
        ).start()

    class Reduction:
        def __init__(self, source, rx, rz, out, names, lsem):
            self.source, self.rx, self.rz, self.out = source, rx, rz, out
            self.x, self.z, self.gz, self.gx = names
            self.lsem = lsem

        def block(self, k):
            return self.source(xme * n2 + k)

        def start(self):
            first = self.source(pl.ds((1 - xme) * n2, n2))
            self.sent = copy(first, self.rx, self.x, 0, dp=xpart)
            self.sent.start()

        def scatter(self):
            self.sent.wait()

            def add(k):
                ref = self.block(k)
                ref[...] = (ref[...].astype(F32) + self.rx[k].astype(F32)).astype(BF)

            loop(n2, add)

            def send(k):
                z = lax.rem(zme + 1 + k, n2)
                copy(self.block(z), self.rz.at[zme], self.z, z, dp=2 * z + xme, got=zme).start()

            loop(n2 - 1, send)

        def gather(self):
            own = self.block(zme)

            total = own[...].astype(F32)

            def take(k, total):
                z = lax.rem(zme + 1 + k, n2)
                copy(self.block(z), self.rz.at[z], self.z, z, dp=2 * z + xme).wait()
                return total + self.rz[z].astype(F32)

            if n2 <= 4:
                for k in range(n2 - 1):
                    total = take(k, total)
            else:
                total = lax.fori_loop(0, n2 - 1, take, total)
            own[...] = total.astype(BF)
            spot = self.out.at[xme * n2 + zme]
            self.kept = local(own, spot, self.lsem)
            self.kept.start()

            def send(k):
                z = lax.rem(zme + 1 + k, n2)
                copy(own, spot, self.gz, z, dp=2 * z + xme, got=zme).start()

            loop(n2 - 1, send)

        def spread(self):
            own = self.block(zme)
            self.kept.wait()

            def wait(k):
                z = lax.rem(zme + 1 + k, n2)
                copy(own, self.out.at[xme * n2 + z], self.gz, z, dp=2 * z + xme).wait()

            loop(n2 - 1, wait)
            half = self.out.at[pl.ds(xme * n2, n2)]
            self.last = copy(half, half, self.gx, 0, dp=xpart)
            self.last.start()

        def finish(self):
            half = self.out.at[pl.ds((1 - xme) * n2, n2)]
            copy(half, half, self.gx, 0, dp=xpart).wait_recv()
            self.last.wait_send()

    up = Reduction(
        lambda index: r.upy.at[index], r.upx, r.upz, r.upg_o, ("ux", "uz", "ugz", "ugx"), 7
    )
    dn = Reduction(
        lambda index: r.dny.at[index], r.dnx, r.dnz, r.dng_o, ("dx", "dz", "dgz", "dgx"), 12
    )
    qkv = Reduction(
        lambda index: r.qkvp.at[index], r.qkvx, r.qkvz, r.qkvg_o, ("qx", "qz", "qgz", "qgx"), 8
    )
    y_sum(up_y, r.upp, r.upc, r.upy)
    up.start()
    out_y.start()
    second.onward()
    y_sum(dn_y, r.dnp, r.dnc, r.dny)
    dn.start()
    up.scatter()
    second.finish()

    def key_back(i):
        rows = rows_of(i, TILE)
        totals = own_totals(rows)
        parts = [
            contract(rows, r.vv, r.gall, h) + totals[:, h * M : (h + 1) * M] for h in range(H)
        ]
        r.grads[1, rows, :] = feature_back(rows, 1, jnp.concatenate(parts, 1))
        r.grads[2, rows, :] = select_heads(rows, r.kf[rows, :], r.gall).astype(BF)

    def send_grads(k, target):
        if k < nm - 1:
            spot = rows_of(target, Tm)
            copy(
                r.grads.at[pl.ds(1, 2), spot], r.garr.at[m, pl.ds(1, 2)], "grk", target, mp=target, got=m
            ).start()
        else:
            for a in range(3):
                r.garr[m, a] = r.grads[a, rows_of(m, Tm), :]

    chunks(key_back, send_grads)
    up.gather()
    dn.scatter()

    flat = r.qkvp.reshape(n * plan.rq, L)
    for a in range(3):
        flat[a * D : (a + 1) * D, :] = dot_tn(r.nm[...], r.grads[a]).astype(BF)
    qkv.start()
    out_far = r.out_o.at[rows_of(far, Tm)]
    copy(out_far, out_far, "oy", 0, mp=far).wait_recv()
    out_on = copy(out_far, out_far, "oc", 1, mp=sib)
    out_on.start()

    for target in chunk_order[: nm - 1]:
        copy(r.garr.at[target, 0], r.garr.at[target, 0], "grq", target, mp=target).wait_recv()
        pair = r.garr.at[target, pl.ds(1, 2)]
        copy(pair, pair, "grk", target, mp=target).wait_recv()

    def norm1_back(i):
        rows = rows_of(i, TILE)
        upstream = jnp.zeros((TILE, D), F32)
        for s in range(nm):
            left = jnp.concatenate([r.garr[s, a, rows, :] for a in range(3)], 1)
            right = jnp.concatenate([r.wq_g[s, a] for a in range(3)], 1)
            upstream += dot_nt(left, right)
        upstream = upstream.astype(BF).astype(F32)
        hat, scale = normalised(r.tokv[rows, :].astype(F32))
        r.small[4:5, :] += jnp.sum(upstream * hat, 0, keepdims=True)
        r.small[5:6, :] += jnp.sum(upstream, 0, keepdims=True)
        r.gtv[rows, :] = (r.mid[rows, :] + norm_back(upstream, hat, scale, r.g1[...])).astype(BF)

    loop(Tm // TILE, norm1_back)
    tok_mine = local(r.gtv, r.gtok_o.at[mine], 9)
    tok_y = copy(r.gtv, r.gtok_o.at[mine], "ty", 0, mp=far)
    tok_core = copy(r.gtv, r.gtok_o.at[mine], "tc", 0, mp=sib)
    for c in (tok_y, tok_core, tok_mine):
        c.start()

    small_m = []
    for target in chunk_order[: nm - 1]:
        c = copy(r.small, r.small_m.at[m], "sm", target, mp=target, got=m)
        c.start()
        small_m.append(c)
    dn.gather()
    qkv.scatter()
    up.spread()
    total = r.small[...]
    for target in chunk_order[: nm - 1]:
        copy(r.small, r.small_m.at[target], "sm", target, mp=target).wait_recv()
        total += r.small_m[target]
    for c in small_m:
        c.wait_send()
    r.small_m[m] = total

    def small_send(k):
        j = lax.rem(me + 1 + k, n)
        copy(r.small_m.at[m], r.small_d.at[me], "sd", j, dp=j, got=me).start()

    loop(n - 1, small_send)
    qkv.gather()
    dn.spread()
    qkv.spread()
    r.small_o[...] = r.small_m[m]

    def small_take(k):
        j = lax.rem(me + 1 + k, n)
        copy(r.small_m.at[m], r.small_d.at[j], "sd", j, dp=j).wait()
        r.small_o[...] += r.small_d[j]

    loop(n - 1, small_take)
    r.small_o[6:7, :] = r.small_o[pl.ds(8 + m, 1), :]

    tok_far = r.gtok_o.at[rows_of(far, Tm)]
    copy(tok_far, tok_far, "ty", 0, mp=far).wait_recv()
    tok_on = copy(tok_far, tok_far, "tc", 1, mp=sib)
    tok_on.start()
    up.finish()
    dn.finish()
    qkv.finish()
    for name, here in (("oc", r.out_o), ("tc", r.gtok_o)):
        for index, owner in enumerate((sib, farsib)):
            spot = here.at[rows_of(owner, Tm)]
            copy(spot, spot, name, index, mp=sib).wait_recv()
    for c in (out_y, out_core, out_on, tok_y, tok_core, tok_on):
        c.wait_send()
    for c in (out_mine, tok_mine):
        c.wait()
    for target in chunk_order[: nm - 1]:
        copy(
            r.attb.at[rows_of(target, Tm)], r.arow.at[m], "a2a", target, mp=target
        ).wait_send()
        for i in range(per_chunk):
            grad_copy(target, i).wait_send()
        spot = rows_of(target, Tm)
        copy(r.grads.at[0, spot], r.garr.at[m, 0], "grq", target, mp=target).wait_send()
        copy(
            r.grads.at[pl.ds(1, 2), spot], r.garr.at[m, pl.ds(1, 2)], "grk", target, mp=target
        ).wait_send()


def per_device(
    n,
    nm,
    tokens,
    cotangent,
    bucket,
    cell,
    features,
    qkv_weight,
    out_weight,
    out_bias,
    norm1_gain,
    norm1_bias,
    norm2_gain,
    norm2_bias,
    up_weight,
    up_bias,
    down_weight,
    down_bias,
):
    count, width = tokens.shape
    local, hidden = qkv_weight.shape[2], up_weight.shape[1]
    plan = Plan(n, nm, count, width, local, features.shape[2], hidden)
    spaces = {"vmem": pltpu.VMEM, "hbm": pl.ANY}
    line = lambda v: v.reshape(1, -1)
    grid_ids = (count // LANES, LANES)
    outs = pl.pallas_call(
        functools.partial(layer_kernel, plan),
        out_shape=[jax.ShapeDtypeStruct(s, d) for _, _, s, d in plan.outputs],
        in_specs=[pl.BlockSpec(memory_space=spaces[k]) for _, k in plan.inputs],
        out_specs=[pl.BlockSpec(memory_space=spaces[k]) for _, k, _, _ in plan.outputs],
        scratch_shapes=[pltpu.VMEM(s, d) for _, s, d in plan.scratch]
        + [pltpu.SemaphoreType.DMA((c,)) for c in plan.sems.values() for _ in range(2)]
        + [pltpu.SemaphoreType.DMA((plan.local_sems,))],
        compiler_params=pltpu.CompilerParams(
            collective_id=1, has_side_effects=True, vmem_limit_bytes=63 << 20
        ),
        name="performer_layer",
    )(
        tokens,
        bucket.reshape(grid_ids),
        cell.reshape(grid_ids),
        features,
        qkv_weight,
        line(norm1_gain),
        line(norm1_bias),
        line(out_bias),
        line(norm2_gain),
        line(norm2_bias),
        line(down_bias),
        cotangent,
        out_weight,
        up_weight,
        line(up_bias),
        down_weight,
    )
    output, grad_tokens, up, down, qkv, small = outs[:6]
    up, down = (v.reshape(-1, width) for v in (up, down))
    qkv = qkv.reshape(-1, local)[: 3 * width].reshape(3, width, local)
    return (
        output,
        grad_tokens.astype(F32),
        qkv.astype(F32),
        down[hidden : hidden + local].astype(F32),
        small[3],
        small[4],
        small[5],
        small[1],
        small[2],
        up[:width].astype(F32),
        small[6],
        down[:hidden].astype(F32),
        small[0],
    )


def solution(mesh):
    return jax.shard_map(
        functools.partial(per_device, mesh.shape["dp"], mesh.shape["mp"]),
        mesh=mesh,
        in_specs=(
            P("dp", None),
            P("dp", None),
            P("dp", None),
            P("dp"),
            P(),
            P(None, None, "mp"),
            P("mp", None),
            P(),
            P(),
            P(),
            P(),
            P(),
            P(None, "mp"),
            P("mp"),
            P("mp", None),
            P(),
        ),
        out_specs=(
            P("dp", None),
            P("dp", None),
            P(None, None, "mp"),
            P("mp", None),
            P(),
            P(),
            P(),
            P(),
            P(),
            P(None, "mp"),
            P("mp"),
            P("mp", None),
            P(),
        ),
        check_vma=False,
    )
```

```python
import functools
from types import SimpleNamespace

import jax
import jax.numpy as jnp
from jax import lax
from jax.experimental import pallas as pl
from jax.experimental.pallas import tpu as pltpu
from jax.sharding import PartitionSpec as P

HD = 64
FEATS = 4
STEP = 5
SEG = 2
PAD = 8
SCALE = HD**-0.25
HALF_SQUARE = 0.5 * SCALE * SCALE
EPS = 1e-05

BF = jnp.bfloat16
F32 = jnp.float32
MESH = pl.DeviceIdType.MESH
LANES = 128
TILE = 256


def dot(a, b):
    return jnp.dot(a, b, preferred_element_type=F32)


def dot_nt(a, b):
    return lax.dot_general(a, b, (((1,), (1,)), ((), ())), preferred_element_type=F32)


def dot_tn(a, b):
    return lax.dot_general(a, b, (((0,), (0,)), ((), ())), preferred_element_type=F32)


def lane(shape):
    return lax.broadcasted_iota(jnp.int32, shape, len(shape) - 1)


def roll_half(x):
    return pltpu.roll(x, HD, 1)


def loop(count, body, unroll=False):
    if unroll or count <= 4:
        for i in range(count):
            body(i)
    else:

        def step(i, carry):
            body(i)
            return carry

        lax.fori_loop(0, count, step, 0)


def rows_of(i, size):
    if isinstance(i, int):
        return pl.ds(i * size, size)
    return pl.ds(pl.multiple_of(i * size, size), size)


def normalised(values):
    average = jnp.mean(values, -1, keepdims=True)
    centred = values - average
    spread = jnp.mean(centred * centred, -1, keepdims=True)
    scale = lax.rsqrt(spread + EPS)
    return centred * scale, scale


def norm_back(upstream, hat, scale, gain):
    e = gain * upstream
    return (
        e
        - jnp.mean(e, -1, keepdims=True)
        - hat * jnp.mean(e * hat, -1, keepdims=True)
    ) * scale


def round_up(a, b):
    return (a + b - 1) // b * b


class Plan:
    def __init__(self, n, nm, tokens, width, local, feats, hidden):
        self.n, self.nm, self.T, self.D, self.L, self.M, self.F = (
            n,
            nm,
            tokens,
            width,
            local,
            feats,
            hidden,
        )
        self.H = local // HD
        self.HM = self.H * feats
        self.Tm = tokens // nm
        self.big = n > 8
        self.G8 = n * PAD
        self.rest = hidden + local
        self.tail = self.rest + width * local // width
        self.ru, self.rd, self.rk = (
            round_up((rows + n - 1) // n, 16) for rows in (width, self.tail, 2 * width)
        )
        self.per = self.Tm // TILE
        n2 = n // 2
        T, D, L, HM, Tm = self.T, self.D, self.L, self.HM, self.Tm
        vm = "vmem"
        states = (n, HM, SEG * HD)
        place = "hbm" if self.big else vm
        self.inputs = [
            ("tok", "hbm"),
            ("bkt", vm),
            ("cel", vm),
            ("feat", vm),
            ("wqkv", vm),
            ("g1", vm),
            ("b1", vm),
            ("ob", vm),
            ("g2", vm),
            ("b2", vm),
            ("db", vm),
            ("cot", "hbm"),
            ("ow", "hbm"),
            ("up", "hbm"),
            ("ub", "hbm"),
            ("dn", "hbm"),
        ]
        self.outputs = [
            ("out_o", "hbm", (T, D), BF),
            ("gtok_o", "hbm", (T, D), BF),
            ("upg_o", "hbm", (D, hidden), BF),
            ("dng_o", "hbm", (self.tail, D), BF),
            ("kvg_o", "hbm", (2 * D, L), BF),
            ("small_o", vm, (8, D), F32),
        ]
        big_states = [("sp", states), ("rb", states), ("sall", states), ("gall", states)]
        if self.big:
            self.outputs += [(name, "hbm", shape, BF) for name, shape in big_states]
        self.scratch = [
            ("wcat", (D, 4 * L), BF),
            ("f2", (L, HM), BF),
            ("wb", (HM, 2 * L), BF),
            ("ccb", (T, LANES), BF),
            ("oh2", (T, 2 * self.G8), BF),
            ("nm", (T, D), BF),
            ("qk", (2, T, L), BF),
            ("vv", (2, T, L), BF),
            ("qf", (T, HM), BF),
            ("kf", (T, HM), BF),
            ("ft", (HM, T), BF),
            ("tp", (n, PAD, LANES), F32),
            ("trb", (n, PAD, LANES), F32),
            ("tall", (n, PAD, LANES), F32),
            ("gtall", (n, PAD, LANES), F32),
            ("tot2", (2 * self.G8, HM), BF),
            ("acc", (HM, SEG * HD), F32),
            ("attf", (T, L), F32),
            ("inv", (T, L), F32),
            ("attb", (T, L), BF),
            ("arow", (nm, Tm, L), BF),
            ("wq_g", (nm, 3, D, L), BF),
            ("ow_g", (nm, L, D), BF),
            ("up_g", (nm, D, hidden), BF),
            ("ub_g", (nm, 1, hidden), F32),
            ("dn_g", (nm, hidden, D), BF),
            ("cotv", (Tm, D), BF),
            ("tokv", (Tm, D), BF),
            ("mid", (Tm, D), F32),
            ("nm2", (Tm, D), BF),
            ("act", (nm, Tm, hidden), BF),
            ("gp", (nm, Tm, hidden), BF),
            ("bo", (TILE, D), F32),
            ("gn2", (TILE, D), F32),
            ("gb", (Tm, D), BF),
            ("outv", (Tm, D), BF),
            ("small", (16, D), F32),
            ("small_m", (nm, 16, D), F32),
            ("small_d", (n, 8, D), F32),
            ("small_s", (8, D), F32),
            ("ends", (8, D), F32),
            ("last", (8, LANES), F32),
            ("last_m", (nm, 8, LANES), F32),
            ("last_d", (n, 8, LANES), F32),
            ("upp", (nm, D, hidden), BF),
            ("upc", (2, D, hidden), BF),
            ("upy", (n, self.ru, D), BF),
            ("upx", (n2, self.ru, D), BF),
            ("upz", (n2, self.ru, D), BF),
            ("dnp", (nm, self.rest, D), BF),
            ("dnc", (2, self.rest, D), BF),
            ("dny", (n, self.rd, D), BF),
            ("dnx", (n2, self.rd, D), BF),
            ("dnz", (n2, self.rd, D), BF),
            ("gar", (nm, Tm, L), BF),
            ("gad", (2, T, L), BF),
            ("gg", (2, T, L), BF),
            ("gd", (T, L), F32),
            ("grads", (3, T, L), BF),
            ("garr", (nm, 3, Tm, L), BF),
            ("kvp", (n, self.rk, L), BF),
            ("kvr", (n, self.rk, L), BF),
            ("kvl", (n, self.rk, L), BF),
        ]
        if self.big:
            self.scratch += [("stage_a", (2, HM, SEG * HD), BF), ("stage_b", (2, HM, SEG * HD), BF)]
        else:
            self.scratch += [(name, shape, BF) for name, shape in big_states]
            self.scratch += [("num", (T, LANES), F32), ("gkf", (T, self.M), F32)]
        self.sems = {
            **{name: n2 * self.H for name in ("rsx", "rsz", "agz", "agx", "gsx", "gsz", "ggz", "ggx")},
            **{name: n2 for name in ("rtx", "rtz", "atz", "atx", "gtx", "gtz", "hgz", "hgx")},
            **{name: nm * self.per for name in ("a2a", "gaa", "grk")},
            "grq": nm,
            "wy": 5,
            "wc": 10,
            "uc": 2,
            "uy": 1,
            "ux": n2,
            "uz": n2,
            "ugz": n2,
            "ugx": n2,
            "dc": 2,
            "dy": 1,
            "dx": n2,
            "dz": n2,
            "dgz": n2,
            "dgx": n2,
            "ks": n,
            "kg": n,
            "oy": 1,
            "oc": 2,
            "ty": self.per,
            "tc": 2 * self.per,
            "sm": nm,
            "sd": n,
            "lm": nm,
            "ld": n,
        }
        self.local_sems = 16

    def names(self):
        return (
            [x[0] for x in self.inputs]
            + [x[0] for x in self.outputs]
            + [x[0] for x in self.scratch]
            + [f"{k}_{end}" for k in self.sems for end in ("s", "r")]
            + ["lsem"]
        )


def layer_kernel(plan, *refs):
    r = SimpleNamespace(**dict(zip(plan.names(), refs, strict=True)))
    n, nm, T, D, L, M, HM, Tm, H = (
        plan.n,
        plan.nm,
        plan.T,
        plan.D,
        plan.L,
        plan.M,
        plan.HM,
        plan.Tm,
        plan.H,
    )
    hidden = plan.F
    n2 = n // 2
    tiles = T // TILE
    me, m = lax.axis_index("dp"), lax.axis_index("mp")
    sib = m + 1 - 2 * lax.rem(m, 2)
    far = lax.rem(m + nm // 2, nm)
    farsib = lax.rem(sib + nm // 2, nm)
    xpart = me + 1 - 2 * lax.rem(me, 2)
    xme, zme = lax.rem(me, 2), me // 2

    def sem(name, index):
        return getattr(r, f"{name}_s").at[index], getattr(r, f"{name}_r").at[index]

    def copy(src, dst, name, sent, dp=None, mp=None, got=None):
        send, _ = sem(name, sent)
        _, recv = sem(name, sent if got is None else got)
        return pltpu.make_async_remote_copy(
            src_ref=src,
            dst_ref=dst,
            send_sem=send,
            recv_sem=recv,
            device_id=(me if dp is None else dp, m if mp is None else mp),
            device_id_type=MESH,
        )

    def local(src, dst, index):
        return pltpu.make_async_copy(src, dst, r.lsem.at[index])

    low = lane((1, LANES)) < HD

    barrier = pltpu.get_barrier_semaphore()

    def greet(k):
        pl.semaphore_signal(
            barrier, inc=1, device_id=(lax.rem(me + 1 + k, n), m), device_id_type=MESH
        )

    loop(n - 1, greet)
    for k in range(1, nm):
        pl.semaphore_signal(
            barrier, inc=1, device_id=(me, lax.rem(m + k, nm)), device_id_type=MESH
        )

    mine = rows_of(m, Tm)
    tok_in = local(r.tok, r.nm, 10)
    own_in = [local(r.cot.at[mine], r.cotv, 0), local(r.tok.at[mine], r.tokv, 11)]
    for c in [tok_in, *own_in]:
        c.start()

    r.wcat[:, 0:L] = r.wqkv[0]
    r.wcat[:, L : 2 * L] = r.wqkv[1]
    wv = r.wqkv[2].astype(F32)
    wv_rolled = roll_half(wv)
    r.wcat[:, 2 * L : 3 * L] = jnp.where(low, wv, wv_rolled).astype(BF)
    r.wcat[:, 3 * L : 4 * L] = jnp.where(low, wv_rolled, wv).astype(BF)
    feature_rows = r.feat[STEP % FEATS]
    r.f2[...] = jnp.zeros((L, HM), BF)
    for h in range(H):
        r.f2[h * HD : (h + 1) * HD, h * M : (h + 1) * M] = feature_rows
    r.wb[:, 0:L] = r.f2[...].astype(F32).T.astype(BF)
    head_of_row = lax.broadcasted_iota(jnp.int32, (HM, L), 0) // M
    r.wb[:, L : 2 * L] = jnp.where(head_of_row == lane((HM, L)) // HD, 1.0, 0.0).astype(BF)

    count = T // LANES
    numbers = SEG * r.bkt[...].astype(F32) + r.cel[...].astype(F32)
    numbers = jnp.concatenate([numbers, jnp.zeros((LANES - count, LANES), F32)], 0).T
    for i in range(count):
        rows = pl.ds(i * LANES, LANES)
        column = jnp.broadcast_to(numbers[:, i : i + 1], (LANES, LANES))
        r.ccb[rows, :] = (column - jnp.where(low, 0.0, 1.0)).astype(BF)
        for block in range(2 * plan.G8 // LANES):
            place = (lane((1, LANES)) + block * LANES) % plan.G8
            number = place // PAD * SEG + place % SEG
            r.oh2[rows, block * LANES : (block + 1) * LANES] = jnp.where(
                column == number.astype(F32), 1.0, 0.0
            ).astype(BF)
    part_of_row = lax.broadcasted_iota(jnp.int32, (plan.G8, LANES), 0) % PAD // SEG

    def pack_totals(table):
        packed = jnp.zeros((plan.G8, LANES), F32)
        for q in range(HM // LANES):
            packed += jnp.where(part_of_row == q, table[:, q * LANES : (q + 1) * LANES], 0.0)
        return packed.reshape(n, PAD, LANES)

    def spread_totals(packed):
        packed = packed.reshape(plan.G8, LANES)
        return jnp.concatenate(
            [jnp.where(part_of_row == q, packed, 0.0) for q in range(HM // LANES)], 1
        )

    def phi(u):
        wide = u.astype(F32)
        squares = wide * wide
        first = jnp.sum(jnp.where(low, squares, 0.0), -1, keepdims=True)
        second = jnp.sum(jnp.where(low, 0.0, squares), -1, keepdims=True)
        projected = dot(u, r.f2[...]) * SCALE
        shift = jnp.where(lane((1, HM)) < M, first, second) * HALF_SQUARE
        return jnp.exp(projected - shift)

    tok_in.wait()
    pl.semaphore_wait(barrier, n - 1 + nm - 1)

    def project(i):
        rows = rows_of(i, TILE)
        hat, _ = normalised(r.nm[rows, :].astype(F32))
        normed = (hat * r.g1[...] + r.b1[...]).astype(BF)
        r.nm[rows, :] = normed
        u = dot(normed, r.wcat[:, L:]).astype(BF)
        k = u[:, 0:L]
        r.qk[1, rows, :] = k
        r.vv[0, rows, :], r.vv[1, rows, :] = u[:, L : 2 * L], u[:, 2 * L : 3 * L]
        features = phi(k)
        r.kf[rows, :] = features.astype(BF)
        r.ft[:, rows] = features.T.astype(BF)

    def queries(i):
        rows = rows_of(i, TILE)
        q = dot(r.nm[rows, :], r.wcat[:, 0:L]).astype(BF)
        r.qk[0, rows, :] = q
        r.qf[rows, :] = phi(q).astype(BF)

    shards = [
        (r.ow, r.ow_g),
        (r.up, r.up_g),
        (r.ub, r.ub_g),
        (r.dn, r.dn_g),
        (r.wqkv, r.wq_g),
    ]
    own_copies, y_copies, core_copies = [], [], []
    for i, (src, dst) in enumerate(shards):
        own_copies.append(local(src, dst.at[m], 1 + i))
        y_copies.append(copy(src, dst.at[m], "wy", i, mp=far))
        core_copies.append(copy(src, dst.at[m], "wc", 2 * i, mp=sib))
    for c in own_copies + y_copies + core_copies:
        c.start()
    loop(tiles, project)

    def state_pair(ref, p, stage):
        if plan.big:
            pltpu.sync_copy(ref.at[pl.ds(2 * p, 2)], stage)
            return stage
        return ref.at[pl.ds(2 * p, 2)]

    def masked_pair(rows, dup, p):
        code = r.ccb[rows, :]
        first = jnp.full((1, LANES), 1.0, F32) * (4 * p)
        left = jnp.where(code == first.astype(BF), dup, jnp.zeros_like(dup))
        right = jnp.where(code == (first + 2.0).astype(BF), dup, jnp.zeros_like(dup))
        return jnp.concatenate([left, right], 1)

    everything = pl.ds(0, T)

    def head_rows(h):
        return pl.ds(h * M, M)

    class States:
        def __init__(self, all_s, all_t, names):
            self.all_s, self.all_t = all_s, all_t
            self.x, self.tx, self.z, self.tz, self.gz, self.hz, self.gx, self.hx = names

        def both(self, h, state, totals):
            return [state, totals()] if h == 0 else [state]

        def to_x(self, p, h):
            j, hs = 2 * p + 1 - xme, head_rows(h)
            return self.both(
                h,
                copy(r.sp.at[j, hs], r.rb.at[p, hs], self.x, p * H + h, dp=xpart),
                lambda: copy(r.tp.at[j], r.trb.at[p], self.tx, p, dp=xpart),
            )

        def to_z(self, p, h):
            j, hs = 2 * p + xme, head_rows(h)
            return self.both(
                h,
                copy(
                    r.sp.at[j, hs],
                    r.rb.at[n2 + zme, hs],
                    self.z,
                    p * H + h,
                    dp=j,
                    got=zme * H + h,
                ),
                lambda: copy(r.tp.at[j], r.trb.at[n2 + zme], self.tz, p, dp=j, got=zme),
            )

        def from_z(self, p, h):
            j, hs = 2 * p + xme, head_rows(h)
            return self.both(
                h,
                copy(r.sp.at[j, hs], r.rb.at[n2 + p, hs], self.z, p * H + h, dp=j),
                lambda: copy(r.tp.at[j], r.trb.at[n2 + p], self.tz, p, dp=j),
            )

        def out_z(self, p, h):
            j, hs = 2 * p + xme, head_rows(h)
            s, t = self.all_s.at[me, hs], self.all_t.at[me]
            return self.both(
                h,
                copy(s, s, self.gz, p * H + h, dp=j, got=zme * H + h),
                lambda: copy(t, t, self.hz, p, dp=j, got=zme),
            )

        def in_z(self, p, h):
            j, hs = 2 * p + xme, head_rows(h)
            s, t = self.all_s.at[j, hs], self.all_t.at[j]
            return self.both(
                h,
                copy(s, s, self.gz, p * H + h, dp=j),
                lambda: copy(t, t, self.hz, p, dp=j),
            )

        def out_x(self, p, h, other=False):
            j, hs = 2 * p + (1 - xme if other else xme), head_rows(h)
            s, t = self.all_s.at[j, hs], self.all_t.at[j]
            return self.both(
                h,
                copy(s, s, self.gx, p * H + h, dp=xpart),
                lambda: copy(t, t, self.hx, p, dp=xpart),
            )

        def start(self, dup):
            for h in range(H):

                def pair(kk, h=h):
                    p = lax.rem(zme + 1 + kk, n2)
                    block = dot(r.ft[head_rows(h), :], masked_pair(everything, dup[h], p))
                    sides = block[:, :LANES].astype(BF), block[:, LANES:].astype(BF)
                    for side, values in enumerate(sides):
                        put_state(r.sp, 2 * p + side, h, values)
                    for c in self.to_x(p, h):
                        c.start()

                loop(n2, pair)

        def add_x(self, p, h):
            for c in self.to_x(p, h):
                c.wait_recv()
            j = 2 * p + xme
            if h == 0:
                r.tp[j] += r.trb[p]
            return get_state(r.sp, j, h) + get_state(r.rb, p, h)

        def near(self, h, k):
            p = lax.rem(zme + 1 + k, n2)
            put_state(r.sp, 2 * p + xme, h, self.add_x(p, h).astype(BF))
            for c in self.to_z(p, h):
                c.start()

        def own(self, h):
            r.acc[head_rows(h), :] = self.add_x(zme, h)

        def whole(self, h):
            def take(k):
                p = lax.rem(zme + 1 + k, n2)
                for c in self.from_z(p, h):
                    c.wait_recv()
                r.acc[head_rows(h), :] += get_state(r.rb, n2 + p, h)
                if h == 0:
                    r.tp[me] += r.trb[n2 + p]

            loop(n2 - 1, take)
            if h == 0:
                self.all_t[me] = r.tp[me]
            put_state(self.all_s, me, h, r.acc[head_rows(h), :].astype(BF))

            def send(k):
                for c in self.out_z(lax.rem(zme + 1 + k, n2), h):
                    c.start()

            loop(n2 - 1, send)
            for c in self.out_x(zme, h):
                c.start()

        def onward(self, h, k):
            p = lax.rem(zme + 1 + k, n2)
            for c in self.in_z(p, h):
                c.wait_recv()
            for c in self.out_x(p, h):
                c.start()

        def arrived(self, p, h):
            for c in self.out_x(p, h, other=True):
                c.wait_recv()

        def run(self, between, use, midway):
            others = n2 - 1
            if plan.big:
                for h in range(H):
                    loop(others, functools.partial(self.near, h))
                    self.own(h)
                    self.whole(h)
                between(everything=True)
                midway()
                for h in range(H):
                    loop(others, functools.partial(self.onward, h))
                for h in range(H):
                    loop(n2, lambda p, h=h: self.arrived(p, h))
            else:
                for k in range(others):
                    self.near(0, k)
                    between()
                self.own(0)
                for h in range(1, H):
                    for k in range(others):
                        if k == others - 1:
                            self.whole(h - 1)
                        self.near(h, k)
                        between()
                    self.own(h)
                between(everything=True)
                self.whole(H - 1)
                for k in range(others):
                    self.onward(0, k)
                for h in range(H):
                    for p in range(n2):
                        self.arrived(p, h)
                    if h < H - 1:
                        for k in range(others):
                            self.onward(h + 1, k)
                        use(h)
                        midway()
            for h in range(H):

                def sent(p, h=h):
                    for c in [*self.to_x(p, h), *self.out_x(p, h)]:
                        c.wait_send()

                loop(n2, sent)

                def sent_z(k, h=h):
                    p = lax.rem(zme + 1 + k, n2)
                    for c in [*self.to_z(p, h), *self.out_z(p, h)]:
                        c.wait_send()

                loop(others, sent_z)
            total = spread_totals(self.all_t[...])
            top = total.astype(BF)
            r.tot2[0 : plan.G8, :] = top
            r.tot2[plan.G8 :, :] = (total - top.astype(F32)).astype(BF)

    def put_state(ref, j, h, values):
        if plan.big:
            spot = r.stage_b.at[0, head_rows(h)]
            spot[...] = values
            pltpu.sync_copy(spot, ref.at[j, head_rows(h)])
        else:
            ref[j, head_rows(h), :] = values

    def get_state(ref, j, h):
        if plan.big:
            spot = r.stage_b.at[1, head_rows(h)]
            pltpu.sync_copy(ref.at[j, head_rows(h)], spot)
            return spot[...].astype(F32)
        return ref[j, head_rows(h), :].astype(F32)

    def state_columns(ref, p, h):
        blocks = state_pair(ref, p, r.stage_a if plan.big else None)
        return jnp.concatenate([blocks[0, head_rows(h), :], blocks[1, head_rows(h), :]], 1)

    def pick(code, product, p, rest):
        first = jnp.full((1, LANES), 1.0, F32) * (4 * p)
        rest = jnp.where(code == first, product[:, :LANES], rest)
        return jnp.where(code == first + 2.0, product[:, LANES:], rest)

    def times_state(rows, left, all_s, h):
        code, features = r.ccb[rows, :].astype(F32), left[rows, head_rows(h)]

        def pair(p, total):
            return pick(code, dot(features, state_columns(all_s, p, h)), p, total)

        total = jnp.zeros((TILE, LANES), F32)
        if plan.big:
            return lax.fori_loop(0, n2, pair, total)
        for p in range(n2):
            total = pair(p, total)
        return total

    def own_state(rows, left, all_s):
        ready = [] if plan.big else [r.num[rows, :]]
        heads = ready + [times_state(rows, left, all_s, h) for h in range(len(ready), H)]
        return halves(*(head + roll_half(head) for head in heads))

    def halves(first, second):
        return jnp.where(low, first, second)

    class Meanwhile:
        def __init__(self, each, pieces):
            self.each, self.pieces = each, list(pieces)

        def __call__(self, everything=False):
            many = len(self.pieces) if everything else self.each
            for piece in self.pieces[:many]:
                piece()
            self.pieces = self.pieces[many:]

    def early(left, all_s):
        def run(h):
            def tile(i):
                rows = rows_of(i, TILE)
                r.num[rows, :] = times_state(rows, left, all_s, h)

            loop(tiles, tile)

        return run

    first = States(
        r.sall, r.tall, ("rsx", "rtx", "rsz", "rtz", "agz", "atz", "agx", "atx")
    )
    r.tp[...] = pack_totals(dot_tn(r.oh2[:, : plan.G8], r.kf[...]))
    first.start([r.vv[0], r.vv[1]])

    onward = []

    def weights_on(which):
        for i in which:
            dst = shards[i][1]
            copy(dst.at[far], dst.at[far], "wy", i, mp=far).wait_recv()
            c = copy(dst.at[far], dst.at[far], "wc", 2 * i + 1, mp=sib)
            c.start()
            onward.append(c)

    def turn(source):
        def tile(i):
            rows = rows_of(i, TILE)
            r.ft[:, rows] = source[rows, :].astype(F32).T.astype(BF)

        return lambda: loop(tiles, tile)

    def some(body, start, count):
        return lambda: loop(count, lambda k: body(start + k))

    quarter = tiles // 4
    first.run(
        Meanwhile(1, [some(queries, i * quarter, quarter) for i in range(4)] + [turn(r.qf)]),
        early(r.qf, r.sall),
        lambda: weights_on(range(4)),
    )

    def own_totals(rows):
        return dot(r.oh2[rows, :], r.tot2[...])

    def attend(i):
        rows = rows_of(i, TILE)
        numerator = own_state(rows, r.qf, r.sall)
        product = r.qf[rows, :].astype(F32) * own_totals(rows)
        denominator = halves(
            jnp.sum(product[:, :M], -1, keepdims=True),
            jnp.sum(product[:, M:], -1, keepdims=True),
        )
        inverse = 1.0 / denominator
        attention = numerator / denominator
        r.attf[rows, :] = attention
        r.inv[rows, :] = inverse
        r.attb[rows, :] = attention.astype(BF)

    per = plan.per
    chunk_order = [far, farsib, sib, m]
    others_mp = chunk_order[: nm - 1]

    def swap(src, dst, name, target, i):
        return copy(src, dst, name, target * per + i, mp=target, got=m * per + i)

    def swapped(dst, name, source, i):
        return copy(dst, dst, name, source * per + i, mp=source)

    def attention_copy(target, i):
        return swap(
            r.attb.at[rows_of(target * per + i, TILE)],
            r.arow.at[m, rows_of(i, TILE)],
            "a2a",
            target,
            i,
        )

    for i in range(per):
        for target in others_mp:
            attend(target * per + i)
            attention_copy(target, i).start()
        attend(m * per + i)
        r.arow[m, rows_of(i, TILE), :] = r.attb[rows_of(m * per + i, TILE), :]

    def weights_wait(which):
        for i in which:
            dst = shards[i][1]
            own_copies[i].wait()
            copy(dst.at[sib], dst.at[sib], "wc", 2 * i, mp=sib).wait_recv()
            copy(dst.at[farsib], dst.at[farsib], "wc", 2 * i + 1, mp=sib).wait_recv()
            for c in (y_copies[i], core_copies[i], onward[i]):
                c.wait_send()

    weights_wait(range(4))
    for c in own_in:
        c.wait()

    r.small[...] = jnp.zeros((16, D), F32)

    def units(rows, s):
        up, down = r.up_g[s], r.dn_g[s]
        preact = dot(r.nm2[rows, :], up) + r.ub_g[s]
        spread = 0.5 + 0.5 * lax.erf(preact * (0.5**0.5))
        active = (preact * spread).astype(BF)
        r.act[s, rows, :] = active
        slope = spread + preact * jnp.exp(preact * preact * -0.5) * 0.3989422804014327
        grad = (dot_nt(r.cotv[rows, :], down) * slope).astype(BF)
        r.gp[s, rows, :] = grad
        r.bo[...] += dot(active, down)
        r.gn2[...] += dot_nt(grad, up)
        r.small[pl.ds(8 + s, 1), :] += jnp.sum(grad.astype(F32), 0, keepdims=True)

    gas = r.attb.reshape(nm, Tm, L)

    def grad_copy(target, i):
        rows = rows_of(i, TILE)
        return swap(gas.at[target, rows], r.gar.at[m, rows], "gaa", target, i)

    def middle_rows(i):
        rows = rows_of(i, TILE)
        for target in others_mp:
            swapped(r.arow.at[target, rows], "a2a", target, i).wait_recv()
            attention_copy(target, i).wait_send()
        columns = jnp.concatenate([r.arow[s, rows, :] for s in range(nm)], 1)
        branch = dot(columns, r.ow_g[...].reshape(D, D)).astype(BF).astype(F32)
        middle = r.tokv[rows, :].astype(F32) + branch + r.ob[...]
        hat, scale = normalised(middle)
        normed = hat * r.g2[...] + r.b2[...]
        r.mid[rows, :] = middle
        r.nm2[rows, :] = normed.astype(BF)
        r.bo[...] = jnp.zeros((TILE, D), F32)
        r.gn2[...] = jnp.zeros((TILE, D), F32)
        lax.fori_loop(0, nm, lambda s, carry: (units(rows, s), carry)[1], 0)
        middle = r.mid[rows, :]
        r.outv[rows, :] = (middle + r.bo[...] + r.db[...]).astype(BF)
        hat, scale = normalised(middle)
        upstream = r.gn2[...]
        cotangent = r.cotv[rows, :].astype(F32)
        grad = cotangent + norm_back(upstream, hat, scale, r.g2[...])
        low_grad = grad.astype(BF)
        back = dot_nt(low_grad, r.ow_g[...].reshape(D, D)).astype(BF)
        for s in range(nm):
            gas[s, rows, :] = back[:, s * L : (s + 1) * L]
        for target in others_mp:
            grad_copy(target, i).start()
        r.mid[rows, :] = grad
        r.gb[rows, :] = low_grad
        r.small[0:1, :] += jnp.sum(cotangent, 0, keepdims=True)
        r.small[1:2, :] += jnp.sum(upstream * hat, 0, keepdims=True)
        r.small[2:3, :] += jnp.sum(upstream, 0, keepdims=True)
        r.small[3:4, :] += jnp.sum(grad, 0, keepdims=True)

    lax.fori_loop(0, per, lambda i, carry: (middle_rows(i), carry)[1], 0)
    r.gar[m] = gas[m]

    up_core = [
        copy(r.upp.at[sib], r.upc.at[0], "uc", 0, mp=sib),
        copy(r.upp.at[farsib], r.upc.at[1], "uc", 1, mp=sib),
    ]
    dn_core = [
        copy(r.dnp.at[sib], r.dnc.at[0], "dc", 0, mp=sib),
        copy(r.dnp.at[farsib], r.dnc.at[1], "dc", 1, mp=sib),
    ]

    def up_part(s):
        r.upp[s] = dot_tn(r.nm2[...], r.gp[s]).astype(BF)

    def down_part(s):
        r.dnp[s, 0:hidden, :] = dot_tn(r.act[s], r.cotv[...]).astype(BF)
        r.dnp[s, hidden : hidden + L, :] = dot_tn(r.arow[s], r.gb[...]).astype(BF)

    lax.fori_loop(0, nm, lambda s, carry: (up_part(s), carry)[1], 0)
    for c in up_core:
        c.start()
    lax.fori_loop(0, nm, lambda s, carry: (down_part(s), carry)[1], 0)
    for c in dn_core:
        c.start()

    def flat_rows(ref):
        return ref.reshape(ref.shape[0] * ref.shape[1], ref.shape[2])

    def core_sum(copies, part, other, y, name):
        for c in copies:
            c.wait()
        rows = part.shape[1]

        def add(i):
            strip = rows_of(i, LANES)
            part[far, strip, :] = (
                part[far, strip, :].astype(F32) + other[1, strip, :].astype(F32)
            ).astype(BF)

        loop(rows // LANES, add)
        return copy(part.at[far], flat_rows(y).at[pl.ds(0, rows)], name, 0, mp=far)

    def y_sum(sent, part, other, y):
        sent.wait()
        flat = flat_rows(y)

        def add(i):
            strip = rows_of(i, LANES)
            flat[strip, :] = (
                part[m, strip, :].astype(F32)
                + other[0, strip, :].astype(F32)
                + flat[strip, :].astype(F32)
            ).astype(BF)

        loop(part.shape[1] // LANES, add)

    class Reduction:
        def __init__(self, source, rx, rz, out, names):
            self.source, self.rx, self.rz, self.out = source, rx, rz, out
            self.x, self.z, self.gz, self.gx = names

        def block(self, k):
            return self.source.at[xme * n2 + k]

        def to_x(self, k):
            return copy(self.source.at[(1 - xme) * n2 + k], self.rx.at[k], self.x, k, dp=xpart)

        def start(self):
            loop(n2, lambda k: self.to_x(lax.rem(zme + 1 + k, n2)).start())

        def scatter(self):
            def add(k):
                self.to_x(k).wait()
                ref = self.block(k)
                ref[...] = (ref[...].astype(F32) + self.rx[k].astype(F32)).astype(BF)

            def send(k):
                z = lax.rem(zme + 1 + k, n2)
                add(z)
                copy(self.block(z), self.rz.at[zme], self.z, z, dp=2 * z + xme, got=zme).start()

            loop(n2 - 1, send)
            add(zme)

        def gather(self):
            own = self.block(zme)

            def take(k, total):
                z = lax.rem(zme + 1 + k, n2)
                copy(self.block(z), self.rz.at[z], self.z, z, dp=2 * z + xme).wait()
                return total + self.rz[z].astype(F32)

            total = own[...].astype(F32)
            if n2 <= 4:
                for k in range(n2 - 1):
                    total = take(k, total)
            else:
                total = lax.fori_loop(0, n2 - 1, take, total)
            own[...] = total.astype(BF)
            self.place(xme * n2 + zme, 1)[...] = own[...]
            spot = self.place(xme * n2 + zme, 1)

            def send(k):
                z = lax.rem(zme + 1 + k, n2)
                copy(own, spot, self.gz, z, dp=2 * z + xme, got=zme).start()

            loop(n2 - 1, send)
            self.over_x(zme).start()

        def over_x(self, z, side=None):
            spot = self.place((xme if side is None else side) * n2 + z, 1)
            return copy(spot, spot, self.gx, z, dp=xpart)

        def spread(self):
            own = self.block(zme)

            def onward(k):
                z = lax.rem(zme + 1 + k, n2)
                copy(own, self.place(xme * n2 + z, 1), self.gz, z, dp=2 * z + xme).wait()
                self.over_x(z).start()

            loop(n2 - 1, onward)

        def finish(self):
            def wait(z):
                self.over_x(z, 1 - xme).wait_recv()
                self.over_x(z).wait_send()

            loop(n2, wait)

        def place(self, index, count):
            rows = self.source.shape[1]
            return self.out.at[pl.ds(pl.multiple_of(index * rows, rows), count * rows)]

    up = Reduction(r.upy, r.upx, r.upz, flat_rows(r.upc), ("ux", "uz", "ugz", "ugx"))
    dn = Reduction(r.dny, r.dnx, r.dnz, flat_rows(r.dnc), ("dx", "dz", "dgz", "dgx"))

    class Sums:
        def __init__(self, own, over_m, names):
            self.own, self.over_m, self.names = own, over_m, names

        def start(self):
            for target in others_mp:
                copy(
                    self.own, self.over_m.at[m], self.names[0], target, mp=target, got=m
                ).start()

        def scatter(self, send, over_d, keep):
            total = self.own[...]
            for target in others_mp:
                copy(self.own, self.over_m.at[target], self.names[0], target, mp=target).wait()
                total += self.over_m[target]
            self.send, self.over_d = send, over_d
            self.send[...] = keep(total)

            def go(k):
                j = lax.rem(me + 1 + k, n)
                copy(self.send, over_d.at[me], self.names[1], j, dp=j, got=me).start()

            loop(n - 1, go)

        def gather(self):
            self.total = self.send[...]

            def take(k, total):
                j = lax.rem(me + 1 + k, n)
                copy(self.send, self.over_d.at[j], self.names[1], j, dp=j).wait()
                return total + self.over_d[j]

            return lax.fori_loop(0, n - 1, take, self.send[...])

    small = Sums(r.small, r.small_m, ("sm", "sd"))
    last = Sums(r.last, r.last_m, ("lm", "ld"))
    small.start()
    weights_on([4])
    for i in range(per):
        for target in others_mp:
            swapped(r.gar.at[target, rows_of(i, TILE)], "gaa", target, i).wait_recv()
    up_y = core_sum(up_core, r.upp, r.upc, r.upy, "uy")
    up_y.start()

    def grad_rows(i):
        rows = rows_of(i, TILE)
        s = i // per
        inner = rows_of(i - s * per, TILE)
        grad = r.gar[s, inner, :].astype(F32)
        inv = r.inv[rows, :]
        scaled = grad * inv
        g_roll, s_roll = roll_half(grad), roll_half(scaled)
        r.gad[0, rows, :] = halves(grad, g_roll).astype(BF)
        r.gad[1, rows, :] = halves(g_roll, grad).astype(BF)
        r.gg[0, rows, :] = halves(scaled, s_roll).astype(BF)
        r.gg[1, rows, :] = halves(s_roll, scaled).astype(BF)
        product = scaled * r.attf[rows, :]
        r.gd[rows, :] = -halves(
            jnp.sum(jnp.where(low, product, 0.0), -1, keepdims=True),
            jnp.sum(jnp.where(low, 0.0, product), -1, keepdims=True),
        )

    loop(tiles, grad_rows)

    def head_column(values, h):
        return values[:, h * HD : h * HD + 1]

    head_totals = []
    for h in range(H):
        column = r.gd[:, h * HD : h * HD + 1]
        top = column.astype(BF).astype(F32)
        upper = lane((1, 2 * plan.G8)) < plan.G8
        weights = r.oh2[...] * jnp.where(upper, top, column - top).astype(BF)
        summed = dot_tn(weights, r.qf[:, h * M : (h + 1) * M])
        head_totals.append(summed[: plan.G8] + summed[plan.G8 :])
    r.tp[...] = pack_totals(jnp.concatenate(head_totals, 1))
    dn_y = core_sum(dn_core, r.dnp, r.dnc, r.dny, "dy")
    dn_y.start()
    second = States(
        r.gall, r.gtall, ("gsx", "gtx", "gsz", "gtz", "ggz", "hgz", "ggx", "hgx")
    )
    second.start([r.gg[0], r.gg[1]])

    def contract(rows, dup, all_s, h):
        def pair(p, total):
            return total + dot_nt(masked_pair(rows, dup[h, rows, :], p), state_columns(all_s, p, h))

        total = jnp.zeros((TILE, M), F32)
        if plan.big:
            return lax.fori_loop(0, n2, pair, total)
        for p in range(n2):
            total = pair(p, total)
        return total

    def early_keys(h):
        def tile(i):
            rows = rows_of(i, TILE)
            r.gkf[rows, :] = contract(rows, r.vv, r.gall, h)

        loop(tiles, tile)
        early(r.kf, r.gall)(h)

    def feature_back(rows, which, grad_features):
        u = r.qk[which, rows, :]
        weighted = (grad_features * phi(u)).astype(BF)
        both = dot(weighted, r.wb[...])
        return (
            both[:, :L] * SCALE - both[:, L:] * u.astype(F32) * (SCALE * SCALE)
        ).astype(BF)

    def query_back(i):
        rows = rows_of(i, TILE)
        totals = own_totals(rows)
        inv, gd = r.inv[rows, :], r.gd[rows, :]
        parts = [
            contract(rows, r.gad, r.sall, h) * head_column(inv, h)
            + totals[:, h * M : (h + 1) * M] * head_column(gd, h)
            for h in range(H)
        ]
        r.grads[0, rows, :] = feature_back(rows, 0, jnp.concatenate(parts, 1))

    def own_unit_sums(total):
        rows = lax.broadcasted_iota(jnp.int32, (16, 1), 0)
        units_row = jnp.sum(jnp.where(rows == 8 + m, total, 0.0), 0, keepdims=True)
        return jnp.concatenate([total[0:4], units_row, jnp.zeros((3, D), F32)], 0)

    def small_scatter():
        small.scatter(r.small_s, r.small_d, own_unit_sums)

    def send_query_grads():
        for target in others_mp:
            copy(
                r.grads.at[0, rows_of(target, Tm)], r.garr.at[m, 0], "grq", target, mp=target, got=m
            ).start()

    def query_projection():
        part = dot(r.ft[...], r.grads[0]).astype(BF)
        flat = flat_rows(r.dny)
        for c in range(D // L):
            flat[plan.rest : plan.tail, c * L : (c + 1) * L] = part[c * L : (c + 1) * L, :]

    gtv = r.nm2
    out_land, tok_land = flat_rows(r.dn_g), flat_rows(r.up_g)
    out_y = copy(r.outv, out_land.at[mine], "oy", 0, mp=far)
    out_core = copy(r.outv, out_land.at[mine], "oc", 0, mp=sib)

    def start_up():
        y_sum(up_y, r.upp, r.upc, r.upy)
        up.start()

    def midway():
        y_sum(dn_y, r.dnp, r.dnc, r.dny)
        dn.start()
        out_y.start()
        out_core.start()
        up.scatter()

    def together(*bodies):
        def run():
            for body in bodies:
                body()

        return run

    second.run(
        Meanwhile(
            1,
            [
                some(query_back, 0, quarter),
                some(query_back, quarter, quarter),
                some(query_back, 2 * quarter, quarter),
                together(some(query_back, 3 * quarter, quarter), send_query_grads),
                turn(r.nm),
                together(query_projection, start_up, small_scatter),
            ],
        ),
        early_keys,
        midway,
    )
    dn.scatter()
    out_land[mine, :] = r.outv[...]
    def key_back(i):
        rows = rows_of(i, TILE)
        totals = own_totals(rows)
        ready = [] if plan.big else [r.gkf[rows, :]]
        parts = ready + [contract(rows, r.vv, r.gall, h) for h in range(len(ready), H)]
        gkf = jnp.concatenate(parts, 1)
        r.grads[1, rows, :] = feature_back(rows, 1, gkf + totals)
        r.grads[2, rows, :] = own_state(rows, r.kf, r.gall).astype(BF)

    both = pl.ds(1, 2)

    def key_copy(target, i):
        return swap(
            r.grads.at[both, rows_of(target * per + i, TILE)],
            r.garr.at[m, both, rows_of(i, TILE)],
            "grk",
            target,
            i,
        )

    for i in range(per):
        for target in others_mp:
            key_back(target * per + i)
            key_copy(target, i).start()
        if i == per // 2:
            up.gather()
        key_back(m * per + i)
        inner, spot = rows_of(i, TILE), rows_of(m * per + i, TILE)
        for a in range(3):
            r.garr[m, a, inner, :] = r.grads[a, spot, :]

    part = dot(r.ft[...], jnp.concatenate([r.grads[1], r.grads[2]], 1)).astype(BF)
    flat = flat_rows(r.kvp)
    flat[0:D, :] = part[:, :L]
    flat[D : 2 * D, :] = part[:, L:]

    def kv_send(k):
        j = lax.rem(me + 1 + k, n)
        copy(r.kvp.at[j], r.kvr.at[me], "ks", j, dp=j, got=me).start()

    loop(n - 1, kv_send)

    out_far = out_land.at[rows_of(far, Tm)]
    copy(out_far, out_far, "oy", 0, mp=far).wait_recv()
    out_on = copy(out_far, out_far, "oc", 1, mp=sib)
    out_on.start()

    for target in others_mp:
        copy(r.garr.at[target, 0], r.garr.at[target, 0], "grq", target, mp=target).wait_recv()
    weights_wait([4])
    r.ends[...] = jnp.zeros((8, D), F32)
    tok_sent = []

    quarters = D // LANES

    def send_ends():
        for row in range(2):
            for q in range(quarters):
                spot = row * quarters + q
                r.last[spot : spot + 1, :] = r.ends[row : row + 1, q * LANES : (q + 1) * LANES]
        last.start()

    def norm1_back(i):
        rows = rows_of(i, TILE)
        for target in others_mp:
            swapped(r.garr.at[target, both, rows], "grk", target, i).wait_recv()
        upstream = jnp.zeros((TILE, D), F32)
        for s in range(nm):
            left = jnp.concatenate([r.garr[s, a, rows, :] for a in range(3)], 1)
            right = jnp.concatenate([r.wq_g[s, a] for a in range(3)], 1)
            upstream += dot_nt(left, right)
        upstream = upstream.astype(BF).astype(F32)
        hat, scale = normalised(r.tokv[rows, :].astype(F32))
        gtv[rows, :] = (r.mid[rows, :] + norm_back(upstream, hat, scale, r.g1[...])).astype(BF)
        r.ends[0:1, :] += jnp.sum(upstream * hat, 0, keepdims=True)
        r.ends[1:2, :] += jnp.sum(upstream, 0, keepdims=True)
        if i == per - 1:
            send_ends()
        spot = tok_land.at[rows_of(m * per + i, TILE)]
        copies = [
            copy(gtv.at[rows], spot, "ty", i, mp=far),
            copy(gtv.at[rows], spot, "tc", 2 * i, mp=sib),
        ]
        for c in copies:
            c.start()
        tok_sent.append(copies)

    for i in range(per):
        norm1_back(i)
        if i == 0:
            dn.gather()
            up.spread()
    tok_land[mine, :] = gtv[...]

    def kv_sum():
        total = r.kvp[me].astype(F32)

        def take(k, total):
            j = lax.rem(me + 1 + k, n)
            copy(r.kvp.at[j], r.kvr.at[j], "ks", j, dp=j).wait()
            return total + r.kvr[j].astype(F32)

        r.kvp[me] = lax.fori_loop(0, n - 1, take, total).astype(BF)

    kv_sum()
    last.scatter(r.last, r.last_d, lambda total: total)
    kv_spot = r.kvl.at[me]
    r.kvl[me] = r.kvp[me]

    def kv_spread(k):
        j = lax.rem(me + 1 + k, n)
        copy(r.kvp.at[me], kv_spot, "kg", j, dp=j, got=me).start()

    loop(n - 1, kv_spread)
    dn.spread()
    tok_on = []

    def tok_forward(i):
        spot = tok_land.at[rows_of(far * per + i, TILE)]
        copy(spot, spot, "ty", i, mp=far).wait_recv()
        c = copy(spot, spot, "tc", 2 * i + 1, mp=sib)
        c.start()
        tok_on.append(c)

    sums = small.gather()
    ends = last.gather()
    r.small_o[0:4, :] = sums[0:4]
    for row in range(2):
        for q in range(quarters):
            spot = row * quarters + q
            r.small_o[4 + row : 5 + row, q * LANES : (q + 1) * LANES] = ends[spot : spot + 1]
    r.small_o[6:7, :] = sums[4:5]

    written = []

    def write(src, dst):
        c = local(src, dst, len(written))
        c.start()
        written.append(c)

    def kv_wait(k):
        j = lax.rem(me + 1 + k, n)
        copy(r.kvp.at[me], r.kvl.at[j], "kg", j, dp=j).wait()

    for index, owner in enumerate((sib, farsib)):
        spot = out_land.at[rows_of(owner, Tm)]
        copy(spot, spot, "oc", index, mp=sib).wait_recv()
    write(out_land, r.out_o)
    for i in range(per):
        tok_forward(i)
    up.finish()
    write(up.out.at[pl.ds(0, D)], r.upg_o)
    loop(n - 1, kv_wait)
    write(flat_rows(r.kvl).at[pl.ds(0, 2 * D)], r.kvg_o)
    for i in range(per):
        for index, owner in enumerate((sib, farsib)):
            spot = tok_land.at[rows_of(owner * per + i, TILE)]
            copy(spot, spot, "tc", 2 * i + index, mp=sib).wait_recv()
    write(tok_land, r.gtok_o)
    dn.finish()
    write(dn.out.at[pl.ds(0, plan.tail)], r.dng_o)
    for y, core in tok_sent:
        y.wait_send()
        core.wait_send()
    for c in (out_y, out_core, out_on, *tok_on):
        c.wait_send()
    for c in written:
        c.wait()
    for target in others_mp:
        for i in range(per):
            for c in (grad_copy(target, i), key_copy(target, i)):
                c.wait_send()
        copy(r.grads.at[0, rows_of(target, Tm)], r.garr.at[m, 0], "grq", target, mp=target).wait_send()


def widen_kernel(plan, *refs):
    (output, tokens, up, down, kv, small), refs = refs[:6], refs[6:]
    (out_o, tok_o, qkv_o, ow_o, ob_o, g1_o, b1_o, g2_o, b2_o, up_o, ub_o, dn_o, db_o), refs = (
        refs[:13],
        refs[13:],
    )
    tok_v, out_v, up_v, dn_v, kv_v, tok_w, up_w, dn_w, ow_w, qkv_w, sem_in, sem_out = refs
    D, L, hidden, T = plan.D, plan.L, plan.F, plan.T
    pieces = 4
    size = T // pieces
    reads = [
        pltpu.make_async_copy(a, b, sem_in.at[i])
        for i, (a, b) in enumerate([(up, up_v), (down, dn_v), (kv, kv_v), (output, out_v)])
    ]
    token_reads = [
        pltpu.make_async_copy(
            tokens.at[pl.ds(i * size, size)], tok_v.at[pl.ds(i * size, size)], sem_in.at[4 + i]
        )
        for i in range(pieces)
    ]
    for c in token_reads + reads:
        c.start()
    for row, ref in ((3, ob_o), (4, g1_o), (5, b1_o), (1, g2_o), (2, b2_o), (6, ub_o), (0, db_o)):
        ref[...] = small[row : row + 1, :]
    writes = []

    def send(src, dst):
        c = pltpu.make_async_copy(src, dst, sem_out.at[len(writes)])
        c.start()
        writes.append(c)

    for i in range(pieces):
        token_reads[i].wait()
        rows = pl.ds(i * size, size)
        tok_w[rows, :] = tok_v[rows, :].astype(F32)
        send(tok_w.at[rows], tok_o.at[rows])
    for c in reads:
        c.wait()
    send(out_v, out_o)
    up_w[...] = up_v[...].astype(F32)
    send(up_w, up_o)
    dn_w[...] = dn_v[0:hidden, :].astype(F32)
    send(dn_w, dn_o)
    ow_w[...] = dn_v[hidden : hidden + L, :].astype(F32)
    send(ow_w, ow_o)
    for c in range(D // L):
        qkv_w[0, c * L : (c + 1) * L, :] = dn_v[
            plan.rest : plan.tail, c * L : (c + 1) * L
        ].astype(F32)
    qkv_w[1] = kv_v[0:D, :].astype(F32)
    qkv_w[2] = kv_v[D : 2 * D, :].astype(F32)
    send(qkv_w, qkv_o)
    for c in writes:
        c.wait()


def widen(plan, *gathered):
    D, L, hidden, T = plan.D, plan.L, plan.F, plan.T
    line = ("vmem", (1, D))
    outs = [
        ("hbm", (T, D)),
        ("hbm", (T, D)),
        ("hbm", (3, D, L)),
        ("hbm", (L, D)),
        *[line] * 5,
        ("hbm", (D, hidden)),
        ("vmem", (1, hidden)),
        ("hbm", (hidden, D)),
        line,
    ]
    spaces = {"vmem": pltpu.VMEM, "hbm": pl.ANY}
    results = pl.pallas_call(
        functools.partial(widen_kernel, plan),
        out_shape=[
            jax.ShapeDtypeStruct(shape, BF if i == 0 else F32) for i, (_, shape) in enumerate(outs)
        ],
        in_specs=[pl.BlockSpec(memory_space=pl.ANY)] * 5 + [pl.BlockSpec(memory_space=pltpu.VMEM)],
        out_specs=[pl.BlockSpec(memory_space=spaces[kind]) for kind, _ in outs],
        scratch_shapes=[
            pltpu.VMEM((T, D), BF),
            pltpu.VMEM((T, D), BF),
            pltpu.VMEM((D, hidden), BF),
            pltpu.VMEM((plan.tail, D), BF),
            pltpu.VMEM((2 * D, L), BF),
            pltpu.VMEM((T, D), F32),
            pltpu.VMEM((D, hidden), F32),
            pltpu.VMEM((hidden, D), F32),
            pltpu.VMEM((L, D), F32),
            pltpu.VMEM((3, D, L), F32),
            pltpu.SemaphoreType.DMA((8,)),
            pltpu.SemaphoreType.DMA((16,)),
        ],
        compiler_params=pltpu.CompilerParams(vmem_limit_bytes=60 << 20),
        name="widen",
    )(*gathered)
    return tuple(v.reshape(-1) if v.shape[0] == 1 else v for v in results)


def per_device(
    n,
    nm,
    tokens,
    cotangent,
    bucket,
    cell,
    features,
    qkv_weight,
    out_weight,
    out_bias,
    norm1_gain,
    norm1_bias,
    norm2_gain,
    norm2_bias,
    up_weight,
    up_bias,
    down_weight,
    down_bias,
):
    count, width = tokens.shape
    local, hidden = qkv_weight.shape[2], up_weight.shape[1]
    plan = Plan(n, nm, count, width, local, features.shape[2], hidden)
    spaces = {"vmem": pltpu.VMEM, "hbm": pl.ANY}
    line = lambda v: v.reshape(1, -1)
    grid_ids = (count // LANES, LANES)
    outs = pl.pallas_call(
        functools.partial(layer_kernel, plan),
        out_shape=[jax.ShapeDtypeStruct(s, d) for _, _, s, d in plan.outputs],
        in_specs=[pl.BlockSpec(memory_space=spaces[k]) for _, k in plan.inputs],
        out_specs=[pl.BlockSpec(memory_space=spaces[k]) for _, k, _, _ in plan.outputs],
        scratch_shapes=[pltpu.VMEM(s, d) for _, s, d in plan.scratch]
        + [pltpu.SemaphoreType.DMA((c,)) for c in plan.sems.values() for _ in range(2)]
        + [pltpu.SemaphoreType.DMA((plan.local_sems,))],
        compiler_params=pltpu.CompilerParams(
            collective_id=1, has_side_effects=True, vmem_limit_bytes=63 << 20
        ),
        name="performer_layer",
    )(
        tokens,
        bucket.reshape(grid_ids),
        cell.reshape(grid_ids),
        features,
        qkv_weight,
        line(norm1_gain),
        line(norm1_bias),
        line(out_bias),
        line(norm2_gain),
        line(norm2_bias),
        line(down_bias),
        cotangent,
        out_weight,
        up_weight,
        line(up_bias),
        down_weight,
    )
    return widen(plan, *outs[:6])


def solution(mesh):
    return jax.shard_map(
        functools.partial(per_device, mesh.shape["dp"], mesh.shape["mp"]),
        mesh=mesh,
        in_specs=(
            P("dp", None),
            P("dp", None),
            P("dp", None),
            P("dp"),
            P(),
            P(None, None, "mp"),
            P("mp", None),
            P(),
            P(),
            P(),
            P(),
            P(),
            P(None, "mp"),
            P("mp"),
            P("mp", None),
            P(),
        ),
        out_specs=(
            P("dp", None),
            P("dp", None),
            P(None, None, "mp"),
            P("mp", None),
            P(),
            P(),
            P(),
            P(),
            P(),
            P(None, "mp"),
            P("mp"),
            P("mp", None),
            P(),
        ),
        check_vma=False,
    )
```

```python
import functools
from types import SimpleNamespace

import jax
import jax.numpy as jnp
from jax import lax
from jax.experimental import pallas as pl
from jax.experimental.pallas import tpu as pltpu
from jax.sharding import PartitionSpec as P

HD = 64
FEATS = 4
STEP = 5
SEG = 2
PAD = 8
SCALE = HD**-0.25
HALF_SQUARE = 0.5 * SCALE * SCALE
EPS = 1e-05

BF = jnp.bfloat16
F32 = jnp.float32
MESH = pl.DeviceIdType.MESH
LANES = 128
TILE = 256


def dot(a, b):
    return jnp.dot(a, b, preferred_element_type=F32)


def dot_nt(a, b):
    return lax.dot_general(a, b, (((1,), (1,)), ((), ())), preferred_element_type=F32)


def dot_tn(a, b):
    return lax.dot_general(a, b, (((0,), (0,)), ((), ())), preferred_element_type=F32)


def lane(shape):
    return lax.broadcasted_iota(jnp.int32, shape, len(shape) - 1)


def roll_half(x):
    return pltpu.roll(x, HD, 1)


def loop(count, body, unroll=False):
    if unroll or count <= 3:
        for i in range(count):
            body(i)
    else:

        def step(i, carry):
            body(i)
            return carry

        lax.fori_loop(0, count, step, 0)


def rows_of(i, size):
    if isinstance(i, int):
        return pl.ds(i * size, size)
    return pl.ds(pl.multiple_of(i * size, size), size)


def normalised(values):
    average = jnp.mean(values, -1, keepdims=True)
    centred = values - average
    spread = jnp.mean(centred * centred, -1, keepdims=True)
    scale = lax.rsqrt(spread + EPS)
    return centred * scale, scale


def norm_back(upstream, hat, scale, gain):
    e = gain * upstream
    return (
        e
        - jnp.mean(e, -1, keepdims=True)
        - hat * jnp.mean(e * hat, -1, keepdims=True)
    ) * scale


def round_up(a, b):
    return (a + b - 1) // b * b


class Plan:
    def __init__(self, n, nm, tokens, width, local, feats, hidden):
        self.n, self.nm, self.T, self.D, self.L, self.M, self.F = (
            n,
            nm,
            tokens,
            width,
            local,
            feats,
            hidden,
        )
        self.H = local // HD
        self.HM = self.H * feats
        self.Tm = tokens // nm
        self.big = n > 8
        self.G8 = n * PAD
        self.rest = hidden + local
        self.tail = self.rest + width * local // width
        self.ru, self.rd, self.rk = (
            round_up((rows + n - 1) // n, 16) for rows in (width, self.tail, 2 * width)
        )
        self.per = self.Tm // TILE
        n2 = n // 2
        T, D, L, HM, Tm = self.T, self.D, self.L, self.HM, self.Tm
        vm = "vmem"
        states = (n, HM, SEG * HD)
        place = "hbm" if self.big else vm
        self.inputs = [
            ("tok", "hbm"),
            ("bkt", vm),
            ("cel", vm),
            ("feat", vm),
            ("wqkv", vm),
            ("g1", vm),
            ("b1", vm),
            ("ob", vm),
            ("g2", vm),
            ("b2", vm),
            ("db", vm),
            ("cot", "hbm"),
            ("ow", "hbm"),
            ("up", "hbm"),
            ("ub", "hbm"),
            ("dn", "hbm"),
        ]
        self.outputs = [
            ("out_o", "hbm", (T, D), BF),
            ("gtok_o", "hbm", (T, D), BF),
            ("upg_o", "hbm", (D, hidden), BF),
            ("dng_o", "hbm", (self.tail, D), BF),
            ("kvg_o", "hbm", (2 * D, L), BF),
            ("small_o", vm, (8, D), F32),
        ]
        big_states = [("sp", states), ("rb", states), ("sall", states), ("gall", states)]
        if self.big:
            self.outputs += [(name, "hbm", shape, BF) for name, shape in big_states]
        self.scratch = [
            ("wcat", (D, 4 * L), BF),
            ("f2", (L, HM), BF),
            ("wb", (HM, 2 * L), BF),
            ("ccb", (T, LANES), BF),
            ("oh2", (T, 2 * self.G8), BF),
            ("nm", (T, D), BF),
            ("qk", (2, T, L), BF),
            ("vv", (2, T, L), BF),
            ("qf", (T, HM), BF),
            ("kf", (T, HM), BF),
            ("ft", (HM, T), BF),
            ("tp", (n, PAD, LANES), F32),
            ("trb", (n, PAD, LANES), F32),
            ("tall", (n, PAD, LANES), F32),
            ("gtall", (n, PAD, LANES), F32),
            ("tot2", (2 * self.G8, HM), BF),
            ("acc", (HM, SEG * HD), F32),
            ("attf", (T, L), F32),
            ("inv", (T, L), F32),
            ("attb", (T, L), BF),
            ("arow", (nm, Tm, L), BF),
            ("wq_g", (nm, 3, D, L), BF),
            ("ow_g", (nm, L, D), BF),
            ("up_g", (nm, D, hidden), BF),
            ("ub_g", (nm, 1, hidden), F32),
            ("dn_g", (nm, hidden, D), BF),
            ("cotv", (Tm, D), BF),
            ("tokv", (Tm, D), BF),
            ("mid", (Tm, D), F32),
            ("nm2", (Tm, D), BF),
            ("act", (nm, Tm, hidden), BF),
            ("gp", (nm, Tm, hidden), BF),
            ("bo", (TILE, D), F32),
            ("gn2", (TILE, D), F32),
            ("gb", (Tm, D), BF),
            ("outv", (Tm, D), BF),
            ("small", (16, D), F32),
            ("small_m", (nm, 16, D), F32),
            ("small_d", (n, 8, D), F32),
            ("small_s", (8, D), F32),
            ("ends", (8, D), F32),
            ("last", (8, LANES), F32),
            ("last_m", (nm, 8, LANES), F32),
            ("last_d", (n, 8, LANES), F32),
            ("upp", (nm, D, hidden), BF),
            ("upc", (2, D, hidden), BF),
            ("upy", (n, self.ru, D), BF),
            ("upx", (n2, self.ru, D), BF),
            ("upz", (n2, self.ru, D), BF),
            ("dnp", (nm, self.rest, D), BF),
            ("dnc", (2, self.rest, D), BF),
            ("dny", (n, self.rd, D), BF),
            ("dnx", (n2, self.rd, D), BF),
            ("dnz", (n2, self.rd, D), BF),
            ("gar", (nm, Tm, L), BF),
            ("gad", (2, T, L), BF),
            ("gg", (2, T, L), BF),
            ("gd", (T, L), F32),
            ("grads", (3, T, L), BF),
            ("garr", (nm, 3, Tm, L), BF),
            ("kvp", (n, self.rk, L), BF),
            ("kvr", (n, self.rk, L), BF),
            ("kvl", (n, self.rk, L), BF),
        ]
        if self.big:
            self.scratch += [("stage_a", (2, HM, SEG * HD), BF), ("stage_b", (2, HM, SEG * HD), BF)]
        else:
            self.scratch += [(name, shape, BF) for name, shape in big_states]
            self.scratch += [("num", (T, LANES), F32), ("gkf", (T, self.M), F32)]
        self.sems = {
            **{name: n2 * self.H for name in ("rsx", "rsz", "agz", "agx", "gsx", "gsz", "ggz", "ggx")},
            **{name: n2 for name in ("rtx", "rtz", "atz", "atx", "gtx", "gtz", "hgz", "hgx")},
            **{name: nm * self.per for name in ("a2a", "gaa", "grk")},
            "grq": nm,
            "wy": 5,
            "wc": 10,
            "uc": 2,
            "uy": 1,
            "ux": n2,
            "uz": n2,
            "ugz": n2,
            "ugx": n2,
            "dc": 2,
            "dy": 1,
            "dx": n2,
            "dz": n2,
            "dgz": n2,
            "dgx": n2,
            "ks": n,
            "kg": n,
            "oy": 1,
            "oc": 2,
            "ty": self.per,
            "tc": 2 * self.per,
            "sm": nm,
            "sd": n,
            "lm": nm,
            "ld": n,
        }
        self.local_sems = 16

    def names(self):
        return (
            [x[0] for x in self.inputs]
            + [x[0] for x in self.outputs]
            + [x[0] for x in self.scratch]
            + [f"{k}_{end}" for k in self.sems for end in ("s", "r")]
            + ["lsem"]
        )


def layer_kernel(plan, *refs):
    r = SimpleNamespace(**dict(zip(plan.names(), refs, strict=True)))
    n, nm, T, D, L, M, HM, Tm, H = (
        plan.n,
        plan.nm,
        plan.T,
        plan.D,
        plan.L,
        plan.M,
        plan.HM,
        plan.Tm,
        plan.H,
    )
    hidden = plan.F
    n2 = n // 2
    tiles = T // TILE
    me, m = lax.axis_index("dp"), lax.axis_index("mp")
    sib = m + 1 - 2 * lax.rem(m, 2)
    far = lax.rem(m + nm // 2, nm)
    farsib = lax.rem(sib + nm // 2, nm)
    xpart = me + 1 - 2 * lax.rem(me, 2)
    xme, zme = lax.rem(me, 2), me // 2

    def sem(name, index):
        return getattr(r, f"{name}_s").at[index], getattr(r, f"{name}_r").at[index]

    def copy(src, dst, name, sent, dp=None, mp=None, got=None):
        send, _ = sem(name, sent)
        _, recv = sem(name, sent if got is None else got)
        return pltpu.make_async_remote_copy(
            src_ref=src,
            dst_ref=dst,
            send_sem=send,
            recv_sem=recv,
            device_id=(me if dp is None else dp, m if mp is None else mp),
            device_id_type=MESH,
        )

    def local(src, dst, index):
        return pltpu.make_async_copy(src, dst, r.lsem.at[index])

    low = lane((1, LANES)) < HD

    barrier = pltpu.get_barrier_semaphore()

    def greet(k):
        pl.semaphore_signal(
            barrier, inc=1, device_id=(lax.rem(me + 1 + k, n), m), device_id_type=MESH
        )

    loop(n - 1, greet)
    for k in range(1, nm):
        pl.semaphore_signal(
            barrier, inc=1, device_id=(me, lax.rem(m + k, nm)), device_id_type=MESH
        )

    mine = rows_of(m, Tm)
    tok_in = local(r.tok, r.nm, 10)
    own_in = [local(r.cot.at[mine], r.cotv, 0), local(r.tok.at[mine], r.tokv, 11)]
    for c in [tok_in, *own_in]:
        c.start()

    r.wcat[:, 0:L] = r.wqkv[0]
    r.wcat[:, L : 2 * L] = r.wqkv[1]
    wv = r.wqkv[2].astype(F32)
    wv_rolled = roll_half(wv)
    r.wcat[:, 2 * L : 3 * L] = jnp.where(low, wv, wv_rolled).astype(BF)
    r.wcat[:, 3 * L : 4 * L] = jnp.where(low, wv_rolled, wv).astype(BF)
    feature_rows = r.feat[STEP % FEATS]
    r.f2[...] = jnp.zeros((L, HM), BF)
    for h in range(H):
        r.f2[h * HD : (h + 1) * HD, h * M : (h + 1) * M] = feature_rows
    r.wb[:, 0:L] = r.f2[...].astype(F32).T.astype(BF)
    head_of_row = lax.broadcasted_iota(jnp.int32, (HM, L), 0) // M
    r.wb[:, L : 2 * L] = jnp.where(head_of_row == lane((HM, L)) // HD, 1.0, 0.0).astype(BF)

    count = T // LANES
    numbers = SEG * r.bkt[...].astype(F32) + r.cel[...].astype(F32)
    numbers = jnp.concatenate([numbers, jnp.zeros((LANES - count, LANES), F32)], 0).T
    for i in range(count):
        rows = pl.ds(i * LANES, LANES)
        column = jnp.broadcast_to(numbers[:, i : i + 1], (LANES, LANES))
        r.ccb[rows, :] = (column - jnp.where(low, 0.0, 1.0)).astype(BF)
        for block in range(2 * plan.G8 // LANES):
            place = (lane((1, LANES)) + block * LANES) % plan.G8
            number = place // PAD * SEG + place % SEG
            r.oh2[rows, block * LANES : (block + 1) * LANES] = jnp.where(
                column == number.astype(F32), 1.0, 0.0
            ).astype(BF)
    part_of_row = lax.broadcasted_iota(jnp.int32, (plan.G8, LANES), 0) % PAD // SEG

    def pack_totals(table):
        packed = jnp.zeros((plan.G8, LANES), F32)
        for q in range(HM // LANES):
            packed += jnp.where(part_of_row == q, table[:, q * LANES : (q + 1) * LANES], 0.0)
        return packed.reshape(n, PAD, LANES)

    def spread_totals(packed):
        packed = packed.reshape(plan.G8, LANES)
        return jnp.concatenate(
            [jnp.where(part_of_row == q, packed, 0.0) for q in range(HM // LANES)], 1
        )

    def phi(u):
        wide = u.astype(F32)
        squares = wide * wide
        first = jnp.sum(jnp.where(low, squares, 0.0), -1, keepdims=True)
        second = jnp.sum(jnp.where(low, 0.0, squares), -1, keepdims=True)
        projected = dot(u, r.f2[...]) * SCALE
        shift = jnp.where(lane((1, HM)) < M, first, second) * HALF_SQUARE
        return jnp.exp(projected - shift)

    tok_in.wait()
    pl.semaphore_wait(barrier, n - 1 + nm - 1)

    def project(i):
        rows = rows_of(i, TILE)
        hat, _ = normalised(r.nm[rows, :].astype(F32))
        normed = (hat * r.g1[...] + r.b1[...]).astype(BF)
        r.nm[rows, :] = normed
        u = dot(normed, r.wcat[:, L:]).astype(BF)
        k = u[:, 0:L]
        r.qk[1, rows, :] = k
        r.vv[0, rows, :], r.vv[1, rows, :] = u[:, L : 2 * L], u[:, 2 * L : 3 * L]
        features = phi(k)
        r.kf[rows, :] = features.astype(BF)
        r.ft[:, rows] = features.T.astype(BF)

    def queries(i):
        rows = rows_of(i, TILE)
        q = dot(r.nm[rows, :], r.wcat[:, 0:L]).astype(BF)
        r.qk[0, rows, :] = q
        r.qf[rows, :] = phi(q).astype(BF)

    shards = [
        (r.ow, r.ow_g),
        (r.up, r.up_g),
        (r.ub, r.ub_g),
        (r.dn, r.dn_g),
        (r.wqkv, r.wq_g),
    ]
    own_copies, y_copies, core_copies = [], [], []
    for i, (src, dst) in enumerate(shards):
        own_copies.append(local(src, dst.at[m], 1 + i))
        y_copies.append(copy(src, dst.at[m], "wy", i, mp=far))
        core_copies.append(copy(src, dst.at[m], "wc", 2 * i, mp=sib))
    for c in own_copies + y_copies + core_copies:
        c.start()
    loop(tiles, project)

    def state_pair(ref, p, stage):
        if plan.big:
            pltpu.sync_copy(ref.at[pl.ds(2 * p, 2)], stage)
            return stage
        return ref.at[pl.ds(2 * p, 2)]

    def masked_pair(rows, dup, p):
        code = r.ccb[rows, :]
        first = jnp.full((1, LANES), 1.0, F32) * (4 * p)
        left = jnp.where(code == first.astype(BF), dup, jnp.zeros_like(dup))
        right = jnp.where(code == (first + 2.0).astype(BF), dup, jnp.zeros_like(dup))
        return jnp.concatenate([left, right], 1)

    everything = pl.ds(0, T)

    def head_rows(h):
        return pl.ds(h * M, M)

    class States:
        def __init__(self, all_s, all_t, names):
            self.all_s, self.all_t = all_s, all_t
            self.x, self.tx, self.z, self.tz, self.gz, self.hz, self.gx, self.hx = names

        def both(self, h, state, totals):
            return [state, totals()] if h == 0 else [state]

        def to_x(self, p, h):
            j, hs = 2 * p + 1 - xme, head_rows(h)
            return self.both(
                h,
                copy(r.sp.at[j, hs], r.rb.at[p, hs], self.x, p * H + h, dp=xpart),
                lambda: copy(r.tp.at[j], r.trb.at[p], self.tx, p, dp=xpart),
            )

        def to_z(self, p, h):
            j, hs = 2 * p + xme, head_rows(h)
            return self.both(
                h,
                copy(
                    r.sp.at[j, hs],
                    r.rb.at[n2 + zme, hs],
                    self.z,
                    p * H + h,
                    dp=j,
                    got=zme * H + h,
                ),
                lambda: copy(r.tp.at[j], r.trb.at[n2 + zme], self.tz, p, dp=j, got=zme),
            )

        def from_z(self, p, h):
            j, hs = 2 * p + xme, head_rows(h)
            return self.both(
                h,
                copy(r.sp.at[j, hs], r.rb.at[n2 + p, hs], self.z, p * H + h, dp=j),
                lambda: copy(r.tp.at[j], r.trb.at[n2 + p], self.tz, p, dp=j),
            )

        def out_z(self, p, h):
            j, hs = 2 * p + xme, head_rows(h)
            s, t = self.all_s.at[me, hs], self.all_t.at[me]
            return self.both(
                h,
                copy(s, s, self.gz, p * H + h, dp=j, got=zme * H + h),
                lambda: copy(t, t, self.hz, p, dp=j, got=zme),
            )

        def in_z(self, p, h):
            j, hs = 2 * p + xme, head_rows(h)
            s, t = self.all_s.at[j, hs], self.all_t.at[j]
            return self.both(
                h,
                copy(s, s, self.gz, p * H + h, dp=j),
                lambda: copy(t, t, self.hz, p, dp=j),
            )

        def out_x(self, p, h, other=False):
            j, hs = 2 * p + (1 - xme if other else xme), head_rows(h)
            s, t = self.all_s.at[j, hs], self.all_t.at[j]
            return self.both(
                h,
                copy(s, s, self.gx, p * H + h, dp=xpart),
                lambda: copy(t, t, self.hx, p, dp=xpart),
            )

        def start(self, dup):
            for h in range(H):

                def pair(kk, h=h):
                    p = lax.rem(zme + 1 + kk, n2)
                    block = dot(r.ft[head_rows(h), :], masked_pair(everything, dup[h], p))
                    sides = block[:, :LANES].astype(BF), block[:, LANES:].astype(BF)
                    for side, values in enumerate(sides):
                        put_state(r.sp, 2 * p + side, h, values)
                    for c in self.to_x(p, h):
                        c.start()

                loop(n2, pair)

        def add_x(self, p, h):
            for c in self.to_x(p, h):
                c.wait_recv()
            j = 2 * p + xme
            if h == 0:
                r.tp[j] += r.trb[p]
            return get_state(r.sp, j, h) + get_state(r.rb, p, h)

        def near(self, h, k):
            p = lax.rem(zme + 1 + k, n2)
            put_state(r.sp, 2 * p + xme, h, self.add_x(p, h).astype(BF))
            for c in self.to_z(p, h):
                c.start()

        def own(self, h):
            r.acc[head_rows(h), :] = self.add_x(zme, h)

        def whole(self, h):
            def take(k):
                p = lax.rem(zme + 1 + k, n2)
                for c in self.from_z(p, h):
                    c.wait_recv()
                r.acc[head_rows(h), :] += get_state(r.rb, n2 + p, h)
                if h == 0:
                    r.tp[me] += r.trb[n2 + p]

            loop(n2 - 1, take)
            if h == 0:
                self.all_t[me] = r.tp[me]
            put_state(self.all_s, me, h, r.acc[head_rows(h), :].astype(BF))

            def send(k):
                for c in self.out_z(lax.rem(zme + 1 + k, n2), h):
                    c.start()

            loop(n2 - 1, send)
            for c in self.out_x(zme, h):
                c.start()

        def onward(self, h, k):
            p = lax.rem(zme + 1 + k, n2)
            for c in self.in_z(p, h):
                c.wait_recv()
            for c in self.out_x(p, h):
                c.start()

        def arrived(self, p, h):
            for c in self.out_x(p, h, other=True):
                c.wait_recv()

        def run(self, between, use, midway):
            others = n2 - 1
            if plan.big:
                for h in range(H):
                    loop(others, functools.partial(self.near, h))
                    self.own(h)
                    self.whole(h)
                between(everything=True)
                midway()
                for h in range(H):
                    loop(others, functools.partial(self.onward, h))
                for h in range(H):
                    loop(n2, lambda p, h=h: self.arrived(p, h))
            else:
                for k in range(others):
                    self.near(0, k)
                    between()
                self.own(0)
                for h in range(1, H):
                    for k in range(others):
                        if k == others - 1:
                            self.whole(h - 1)
                        self.near(h, k)
                        between()
                    self.own(h)
                between(everything=True)
                self.whole(H - 1)
                for k in range(others):
                    self.onward(0, k)
                for h in range(H):
                    for p in range(n2):
                        self.arrived(p, h)
                    if h < H - 1:
                        for k in range(others):
                            self.onward(h + 1, k)
                        use(h)
                        midway()
            for h in range(H):

                def sent(p, h=h):
                    for c in [*self.to_x(p, h), *self.out_x(p, h)]:
                        c.wait_send()

                loop(n2, sent)

                def sent_z(k, h=h):
                    p = lax.rem(zme + 1 + k, n2)
                    for c in [*self.to_z(p, h), *self.out_z(p, h)]:
                        c.wait_send()

                loop(others, sent_z)
            total = spread_totals(self.all_t[...])
            top = total.astype(BF)
            r.tot2[0 : plan.G8, :] = top
            r.tot2[plan.G8 :, :] = (total - top.astype(F32)).astype(BF)

    def put_state(ref, j, h, values):
        if plan.big:
            spot = r.stage_b.at[0, head_rows(h)]
            spot[...] = values
            pltpu.sync_copy(spot, ref.at[j, head_rows(h)])
        else:
            ref[j, head_rows(h), :] = values

    def get_state(ref, j, h):
        if plan.big:
            spot = r.stage_b.at[1, head_rows(h)]
            pltpu.sync_copy(ref.at[j, head_rows(h)], spot)
            return spot[...].astype(F32)
        return ref[j, head_rows(h), :].astype(F32)

    def state_columns(ref, p, h):
        blocks = state_pair(ref, p, r.stage_a if plan.big else None)
        return jnp.concatenate([blocks[0, head_rows(h), :], blocks[1, head_rows(h), :]], 1)

    def pick(code, product, p, rest):
        first = jnp.full((1, LANES), 1.0, F32) * (4 * p)
        rest = jnp.where(code == first, product[:, :LANES], rest)
        return jnp.where(code == first + 2.0, product[:, LANES:], rest)

    def times_state(rows, left, all_s, h):
        code, features = r.ccb[rows, :].astype(F32), left[rows, head_rows(h)]

        def pair(p, total):
            return pick(code, dot(features, state_columns(all_s, p, h)), p, total)

        total = jnp.zeros((TILE, LANES), F32)
        if plan.big:
            return lax.fori_loop(0, n2, pair, total)
        for p in range(n2):
            total = pair(p, total)
        return total

    def own_state(rows, left, all_s):
        ready = [] if plan.big else [r.num[rows, :]]
        heads = ready + [times_state(rows, left, all_s, h) for h in range(len(ready), H)]
        return halves(*(head + roll_half(head) for head in heads))

    def halves(first, second):
        return jnp.where(low, first, second)

    class Meanwhile:
        def __init__(self, each, pieces):
            self.each, self.pieces = each, list(pieces)

        def __call__(self, everything=False):
            many = len(self.pieces) if everything else self.each
            for piece in self.pieces[:many]:
                piece()
            self.pieces = self.pieces[many:]

    def early(left, all_s):
        def run(h):
            def tile(i):
                rows = rows_of(i, TILE)
                r.num[rows, :] = times_state(rows, left, all_s, h)

            loop(tiles, tile)

        return run

    first = States(
        r.sall, r.tall, ("rsx", "rtx", "rsz", "rtz", "agz", "atz", "agx", "atx")
    )
    r.tp[...] = pack_totals(dot_tn(r.oh2[:, : plan.G8], r.kf[...]))
    first.start([r.vv[0], r.vv[1]])

    onward = []

    def weights_on(which):
        for i in which:
            dst = shards[i][1]
            copy(dst.at[far], dst.at[far], "wy", i, mp=far).wait_recv()
            c = copy(dst.at[far], dst.at[far], "wc", 2 * i + 1, mp=sib)
            c.start()
            onward.append(c)

    def turn(source):
        def tile(i):
            rows = rows_of(i, TILE)
            r.ft[:, rows] = source[rows, :].astype(F32).T.astype(BF)

        return lambda: loop(tiles, tile)

    def some(body, start, count):
        return lambda: lax.fori_loop(start, start + count, lambda k, carry: (body(k), carry)[1], 0)

    quarter = tiles // 4
    first.run(
        Meanwhile(1, [some(queries, i * quarter, quarter) for i in range(4)] + [turn(r.qf)]),
        early(r.qf, r.sall),
        lambda: weights_on(range(4)),
    )

    def own_totals(rows):
        return dot(r.oh2[rows, :], r.tot2[...])

    def attend(i):
        rows = rows_of(i, TILE)
        numerator = own_state(rows, r.qf, r.sall)
        product = r.qf[rows, :].astype(F32) * own_totals(rows)
        denominator = halves(
            jnp.sum(product[:, :M], -1, keepdims=True),
            jnp.sum(product[:, M:], -1, keepdims=True),
        )
        inverse = 1.0 / denominator
        attention = numerator / denominator
        r.attf[rows, :] = attention
        r.inv[rows, :] = inverse
        r.attb[rows, :] = attention.astype(BF)

    per = plan.per
    chunk_order = [far, farsib, sib, m]
    others_mp = chunk_order[: nm - 1]

    def swap(src, dst, name, target, i):
        return copy(src, dst, name, target * per + i, mp=target, got=m * per + i)

    def swapped(dst, name, source, i):
        return copy(dst, dst, name, source * per + i, mp=source)

    def attention_copy(target, i):
        return swap(
            r.attb.at[rows_of(target * per + i, TILE)],
            r.arow.at[m, rows_of(i, TILE)],
            "a2a",
            target,
            i,
        )

    def each_tile(body, after, middle=None):
        def step(q, carry):
            i, k = q // nm, lax.rem(q, nm)
            start = lax.rem(m + (1 - k // 2) * (nm // 2), nm)
            target = start + lax.rem((k + 1) // 2, 2) * (1 - 2 * lax.rem(start, 2))
            body(target * per + i)
            pl.when(k < nm - 1)(lambda: after(target, i).start())
            return carry

        half = per // 2 * nm
        lax.fori_loop(0, half, step, 0)
        if middle is not None:
            middle()
        lax.fori_loop(half, per * nm, step, 0)

    each_tile(attend, attention_copy)
    r.arow[m] = r.attb[rows_of(m, Tm), :]

    def weights_wait(which):
        for i in which:
            dst = shards[i][1]
            own_copies[i].wait()
            copy(dst.at[sib], dst.at[sib], "wc", 2 * i, mp=sib).wait_recv()
            copy(dst.at[farsib], dst.at[farsib], "wc", 2 * i + 1, mp=sib).wait_recv()
            for c in (y_copies[i], core_copies[i], onward[i]):
                c.wait_send()

    weights_wait(range(4))
    for c in own_in:
        c.wait()

    r.small[...] = jnp.zeros((16, D), F32)

    def units(rows, s):
        up, down = r.up_g[s], r.dn_g[s]
        preact = dot(r.nm2[rows, :], up) + r.ub_g[s]
        spread = 0.5 + 0.5 * lax.erf(preact * (0.5**0.5))
        active = (preact * spread).astype(BF)
        r.act[s, rows, :] = active
        slope = spread + preact * jnp.exp(preact * preact * -0.5) * 0.3989422804014327
        grad = (dot_nt(r.cotv[rows, :], down) * slope).astype(BF)
        r.gp[s, rows, :] = grad
        r.bo[...] += dot(active, down)
        r.gn2[...] += dot_nt(grad, up)
        r.small[pl.ds(8 + s, 1), :] += jnp.sum(grad.astype(F32), 0, keepdims=True)

    gas = r.attb.reshape(nm, Tm, L)

    def grad_copy(target, i):
        rows = rows_of(i, TILE)
        return swap(gas.at[target, rows], r.gar.at[m, rows], "gaa", target, i)

    def middle_rows(i):
        rows = rows_of(i, TILE)
        for target in others_mp:
            swapped(r.arow.at[target, rows], "a2a", target, i).wait_recv()
            attention_copy(target, i).wait_send()
        columns = jnp.concatenate([r.arow[s, rows, :] for s in range(nm)], 1)
        branch = dot(columns, r.ow_g[...].reshape(D, D)).astype(BF).astype(F32)
        middle = r.tokv[rows, :].astype(F32) + branch + r.ob[...]
        hat, scale = normalised(middle)
        normed = hat * r.g2[...] + r.b2[...]
        r.mid[rows, :] = middle
        r.nm2[rows, :] = normed.astype(BF)
        r.bo[...] = jnp.zeros((TILE, D), F32)
        r.gn2[...] = jnp.zeros((TILE, D), F32)
        lax.fori_loop(0, nm, lambda s, carry: (units(rows, s), carry)[1], 0)
        middle = r.mid[rows, :]
        r.outv[rows, :] = (middle + r.bo[...] + r.db[...]).astype(BF)
        hat, scale = normalised(middle)
        upstream = r.gn2[...]
        cotangent = r.cotv[rows, :].astype(F32)
        grad = cotangent + norm_back(upstream, hat, scale, r.g2[...])
        low_grad = grad.astype(BF)
        back = dot_nt(low_grad, r.ow_g[...].reshape(D, D)).astype(BF)
        for s in range(nm):
            gas[s, rows, :] = back[:, s * L : (s + 1) * L]
        for target in others_mp:
            grad_copy(target, i).start()
        r.mid[rows, :] = grad
        r.gb[rows, :] = low_grad
        r.small[0:1, :] += jnp.sum(cotangent, 0, keepdims=True)
        r.small[1:2, :] += jnp.sum(upstream * hat, 0, keepdims=True)
        r.small[2:3, :] += jnp.sum(upstream, 0, keepdims=True)
        r.small[3:4, :] += jnp.sum(grad, 0, keepdims=True)

    lax.fori_loop(0, per, lambda i, carry: (middle_rows(i), carry)[1], 0)
    r.gar[m] = gas[m]

    up_core = [
        copy(r.upp.at[sib], r.upc.at[0], "uc", 0, mp=sib),
        copy(r.upp.at[farsib], r.upc.at[1], "uc", 1, mp=sib),
    ]
    dn_core = [
        copy(r.dnp.at[sib], r.dnc.at[0], "dc", 0, mp=sib),
        copy(r.dnp.at[farsib], r.dnc.at[1], "dc", 1, mp=sib),
    ]

    def up_part(s):
        r.upp[s] = dot_tn(r.nm2[...], r.gp[s]).astype(BF)

    def down_part(s):
        r.dnp[s, 0:hidden, :] = dot_tn(r.act[s], r.cotv[...]).astype(BF)
        r.dnp[s, hidden : hidden + L, :] = dot_tn(r.arow[s], r.gb[...]).astype(BF)

    lax.fori_loop(0, nm, lambda s, carry: (up_part(s), carry)[1], 0)
    for c in up_core:
        c.start()
    lax.fori_loop(0, nm, lambda s, carry: (down_part(s), carry)[1], 0)
    for c in dn_core:
        c.start()

    def flat_rows(ref):
        return ref.reshape(ref.shape[0] * ref.shape[1], ref.shape[2])

    def core_sum(copies, part, other, y, name):
        for c in copies:
            c.wait()
        rows = part.shape[1]

        def add(i):
            strip = rows_of(i, LANES)
            part[far, strip, :] = (
                part[far, strip, :].astype(F32) + other[1, strip, :].astype(F32)
            ).astype(BF)

        loop(rows // LANES, add)
        return copy(part.at[far], flat_rows(y).at[pl.ds(0, rows)], name, 0, mp=far)

    def y_sum(sent, part, other, y):
        sent.wait()
        flat = flat_rows(y)

        def add(i):
            strip = rows_of(i, LANES)
            flat[strip, :] = (
                part[m, strip, :].astype(F32)
                + other[0, strip, :].astype(F32)
                + flat[strip, :].astype(F32)
            ).astype(BF)

        loop(part.shape[1] // LANES, add)

    class Reduction:
        def __init__(self, source, rx, rz, out, names):
            self.source, self.rx, self.rz, self.out = source, rx, rz, out
            self.x, self.z, self.gz, self.gx = names

        def block(self, k):
            return self.source.at[xme * n2 + k]

        def to_x(self, k):
            return copy(self.source.at[(1 - xme) * n2 + k], self.rx.at[k], self.x, k, dp=xpart)

        def start(self):
            loop(n2, lambda k: self.to_x(lax.rem(zme + 1 + k, n2)).start())

        def scatter(self):
            def add(k):
                self.to_x(k).wait()
                ref = self.block(k)
                ref[...] = (ref[...].astype(F32) + self.rx[k].astype(F32)).astype(BF)

            def send(k):
                z = lax.rem(zme + 1 + k, n2)
                add(z)
                copy(self.block(z), self.rz.at[zme], self.z, z, dp=2 * z + xme, got=zme).start()

            loop(n2 - 1, send)
            add(zme)

        def gather(self):
            own = self.block(zme)

            def take(k, total):
                z = lax.rem(zme + 1 + k, n2)
                copy(self.block(z), self.rz.at[z], self.z, z, dp=2 * z + xme).wait()
                return total + self.rz[z].astype(F32)

            total = own[...].astype(F32)
            if n2 <= 4:
                for k in range(n2 - 1):
                    total = take(k, total)
            else:
                total = lax.fori_loop(0, n2 - 1, take, total)
            own[...] = total.astype(BF)
            self.place(xme * n2 + zme, 1)[...] = own[...]
            spot = self.place(xme * n2 + zme, 1)

            def send(k):
                z = lax.rem(zme + 1 + k, n2)
                copy(own, spot, self.gz, z, dp=2 * z + xme, got=zme).start()

            loop(n2 - 1, send)
            self.over_x(zme).start()

        def over_x(self, z, side=None):
            spot = self.place((xme if side is None else side) * n2 + z, 1)
            return copy(spot, spot, self.gx, z, dp=xpart)

        def spread(self):
            own = self.block(zme)

            def onward(k):
                z = lax.rem(zme + 1 + k, n2)
                copy(own, self.place(xme * n2 + z, 1), self.gz, z, dp=2 * z + xme).wait()
                self.over_x(z).start()

            loop(n2 - 1, onward)

        def finish(self):
            def wait(z):
                self.over_x(z, 1 - xme).wait_recv()
                self.over_x(z).wait_send()

            loop(n2, wait)

        def place(self, index, count):
            rows = self.source.shape[1]
            return self.out.at[pl.ds(pl.multiple_of(index * rows, rows), count * rows)]

    up = Reduction(r.upy, r.upx, r.upz, flat_rows(r.upc), ("ux", "uz", "ugz", "ugx"))
    dn = Reduction(r.dny, r.dnx, r.dnz, flat_rows(r.dnc), ("dx", "dz", "dgz", "dgx"))

    class Sums:
        def __init__(self, own, over_m, names):
            self.own, self.over_m, self.names = own, over_m, names

        def start(self):
            for target in others_mp:
                copy(
                    self.own, self.over_m.at[m], self.names[0], target, mp=target, got=m
                ).start()

        def scatter(self, send, over_d, keep):
            total = self.own[...]
            for target in others_mp:
                copy(self.own, self.over_m.at[target], self.names[0], target, mp=target).wait()
                total += self.over_m[target]
            self.send, self.over_d = send, over_d
            self.send[...] = keep(total)

            def go(k):
                j = lax.rem(me + 1 + k, n)
                copy(self.send, over_d.at[me], self.names[1], j, dp=j, got=me).start()

            loop(n - 1, go)

        def gather(self):
            self.total = self.send[...]

            def take(k, total):
                j = lax.rem(me + 1 + k, n)
                copy(self.send, self.over_d.at[j], self.names[1], j, dp=j).wait()
                return total + self.over_d[j]

            return lax.fori_loop(0, n - 1, take, self.send[...])

    small = Sums(r.small, r.small_m, ("sm", "sd"))
    last = Sums(r.last, r.last_m, ("lm", "ld"))
    small.start()
    weights_on([4])
    for i in range(per):
        for target in others_mp:
            swapped(r.gar.at[target, rows_of(i, TILE)], "gaa", target, i).wait_recv()
    up_y = core_sum(up_core, r.upp, r.upc, r.upy, "uy")
    up_y.start()

    def grad_rows(i):
        rows = rows_of(i, TILE)
        s = i // per
        inner = rows_of(i - s * per, TILE)
        grad = r.gar[s, inner, :].astype(F32)
        inv = r.inv[rows, :]
        scaled = grad * inv
        g_roll, s_roll = roll_half(grad), roll_half(scaled)
        r.gad[0, rows, :] = halves(grad, g_roll).astype(BF)
        r.gad[1, rows, :] = halves(g_roll, grad).astype(BF)
        r.gg[0, rows, :] = halves(scaled, s_roll).astype(BF)
        r.gg[1, rows, :] = halves(s_roll, scaled).astype(BF)
        product = scaled * r.attf[rows, :]
        r.gd[rows, :] = -halves(
            jnp.sum(jnp.where(low, product, 0.0), -1, keepdims=True),
            jnp.sum(jnp.where(low, 0.0, product), -1, keepdims=True),
        )

    loop(tiles, grad_rows)

    def head_column(values, h):
        return values[:, h * HD : h * HD + 1]

    head_totals = []
    for h in range(H):
        column = r.gd[:, h * HD : h * HD + 1]
        top = column.astype(BF).astype(F32)
        upper = lane((1, 2 * plan.G8)) < plan.G8
        weights = r.oh2[...] * jnp.where(upper, top, column - top).astype(BF)
        summed = dot_tn(weights, r.qf[:, h * M : (h + 1) * M])
        head_totals.append(summed[: plan.G8] + summed[plan.G8 :])
    r.tp[...] = pack_totals(jnp.concatenate(head_totals, 1))
    dn_y = core_sum(dn_core, r.dnp, r.dnc, r.dny, "dy")
    dn_y.start()
    second = States(
        r.gall, r.gtall, ("gsx", "gtx", "gsz", "gtz", "ggz", "hgz", "ggx", "hgx")
    )
    second.start([r.gg[0], r.gg[1]])

    def contract(rows, dup, all_s, h):
        def pair(p, total):
            return total + dot_nt(masked_pair(rows, dup[h, rows, :], p), state_columns(all_s, p, h))

        total = jnp.zeros((TILE, M), F32)
        if plan.big:
            return lax.fori_loop(0, n2, pair, total)
        for p in range(n2):
            total = pair(p, total)
        return total

    def early_keys(h):
        def tile(i):
            rows = rows_of(i, TILE)
            r.gkf[rows, :] = contract(rows, r.vv, r.gall, h)

        loop(tiles, tile)
        early(r.kf, r.gall)(h)

    def feature_back(rows, which, grad_features):
        u = r.qk[which, rows, :]
        weighted = (grad_features * phi(u)).astype(BF)
        both = dot(weighted, r.wb[...])
        return (
            both[:, :L] * SCALE - both[:, L:] * u.astype(F32) * (SCALE * SCALE)
        ).astype(BF)

    def query_back(i):
        rows = rows_of(i, TILE)
        totals = own_totals(rows)
        inv, gd = r.inv[rows, :], r.gd[rows, :]
        parts = [
            contract(rows, r.gad, r.sall, h) * head_column(inv, h)
            + totals[:, h * M : (h + 1) * M] * head_column(gd, h)
            for h in range(H)
        ]
        r.grads[0, rows, :] = feature_back(rows, 0, jnp.concatenate(parts, 1))

    def own_unit_sums(total):
        rows = lax.broadcasted_iota(jnp.int32, (16, 1), 0)
        units_row = jnp.sum(jnp.where(rows == 8 + m, total, 0.0), 0, keepdims=True)
        return jnp.concatenate([total[0:4], units_row, jnp.zeros((3, D), F32)], 0)

    def small_scatter():
        small.scatter(r.small_s, r.small_d, own_unit_sums)

    def send_query_grads():
        for target in others_mp:
            copy(
                r.grads.at[0, rows_of(target, Tm)], r.garr.at[m, 0], "grq", target, mp=target, got=m
            ).start()

    def query_projection():
        part = dot(r.ft[...], r.grads[0]).astype(BF)
        flat = flat_rows(r.dny)
        for c in range(D // L):
            flat[plan.rest : plan.tail, c * L : (c + 1) * L] = part[c * L : (c + 1) * L, :]

    gtv = r.nm2
    out_land, tok_land = flat_rows(r.dn_g), flat_rows(r.up_g)
    out_y = copy(r.outv, out_land.at[mine], "oy", 0, mp=far)
    out_core = copy(r.outv, out_land.at[mine], "oc", 0, mp=sib)

    def start_up():
        y_sum(up_y, r.upp, r.upc, r.upy)
        up.start()

    def midway():
        y_sum(dn_y, r.dnp, r.dnc, r.dny)
        dn.start()
        out_y.start()
        out_core.start()
        up.scatter()

    def together(*bodies):
        def run():
            for body in bodies:
                body()

        return run

    second.run(
        Meanwhile(
            1,
            [
                some(query_back, 0, quarter),
                some(query_back, quarter, quarter),
                some(query_back, 2 * quarter, quarter),
                together(some(query_back, 3 * quarter, quarter), send_query_grads),
                turn(r.nm),
                together(query_projection, start_up, small_scatter),
            ],
        ),
        early_keys,
        midway,
    )
    dn.scatter()
    out_land[mine, :] = r.outv[...]
    def key_back(i):
        rows = rows_of(i, TILE)
        totals = own_totals(rows)
        ready = [] if plan.big else [r.gkf[rows, :]]
        parts = ready + [contract(rows, r.vv, r.gall, h) for h in range(len(ready), H)]
        gkf = jnp.concatenate(parts, 1)
        r.grads[1, rows, :] = feature_back(rows, 1, gkf + totals)
        r.grads[2, rows, :] = own_state(rows, r.kf, r.gall).astype(BF)

    both = pl.ds(1, 2)

    def key_copy(target, i):
        return swap(
            r.grads.at[both, rows_of(target * per + i, TILE)],
            r.garr.at[m, both, rows_of(i, TILE)],
            "grk",
            target,
            i,
        )

    each_tile(key_back, key_copy, up.gather)
    for a in range(3):
        r.garr[m, a] = r.grads[a, rows_of(m, Tm), :]

    part = dot(r.ft[...], jnp.concatenate([r.grads[1], r.grads[2]], 1)).astype(BF)
    flat = flat_rows(r.kvp)
    flat[0:D, :] = part[:, :L]
    flat[D : 2 * D, :] = part[:, L:]

    def kv_send(k):
        j = lax.rem(me + 1 + k, n)
        copy(r.kvp.at[j], r.kvr.at[me], "ks", j, dp=j, got=me).start()

    loop(n - 1, kv_send)

    out_far = out_land.at[rows_of(far, Tm)]
    copy(out_far, out_far, "oy", 0, mp=far).wait_recv()
    out_on = copy(out_far, out_far, "oc", 1, mp=sib)
    out_on.start()

    for target in others_mp:
        copy(r.garr.at[target, 0], r.garr.at[target, 0], "grq", target, mp=target).wait_recv()
    weights_wait([4])
    r.ends[...] = jnp.zeros((8, D), F32)
    tok_sent = []

    quarters = D // LANES

    def send_ends():
        for row in range(2):
            for q in range(quarters):
                spot = row * quarters + q
                r.last[spot : spot + 1, :] = r.ends[row : row + 1, q * LANES : (q + 1) * LANES]
        last.start()

    def norm1_back(i):
        rows = rows_of(i, TILE)
        for target in others_mp:
            swapped(r.garr.at[target, both, rows], "grk", target, i).wait_recv()
        upstream = jnp.zeros((TILE, D), F32)
        for s in range(nm):
            left = jnp.concatenate([r.garr[s, a, rows, :] for a in range(3)], 1)
            right = jnp.concatenate([r.wq_g[s, a] for a in range(3)], 1)
            upstream += dot_nt(left, right)
        upstream = upstream.astype(BF).astype(F32)
        hat, scale = normalised(r.tokv[rows, :].astype(F32))
        gtv[rows, :] = (r.mid[rows, :] + norm_back(upstream, hat, scale, r.g1[...])).astype(BF)
        r.ends[0:1, :] += jnp.sum(upstream * hat, 0, keepdims=True)
        r.ends[1:2, :] += jnp.sum(upstream, 0, keepdims=True)
        if i == per - 1:
            send_ends()
        spot = tok_land.at[rows_of(m * per + i, TILE)]
        copies = [
            copy(gtv.at[rows], spot, "ty", i, mp=far),
            copy(gtv.at[rows], spot, "tc", 2 * i, mp=sib),
        ]
        for c in copies:
            c.start()
        tok_sent.append(copies)

    for i in range(per):
        norm1_back(i)
        if i == 0:
            dn.gather()
            up.spread()
    tok_land[mine, :] = gtv[...]

    def kv_sum():
        total = r.kvp[me].astype(F32)

        def take(k, total):
            j = lax.rem(me + 1 + k, n)
            copy(r.kvp.at[j], r.kvr.at[j], "ks", j, dp=j).wait()
            return total + r.kvr[j].astype(F32)

        r.kvp[me] = lax.fori_loop(0, n - 1, take, total).astype(BF)

    kv_sum()
    last.scatter(r.last, r.last_d, lambda total: total)
    kv_spot = r.kvl.at[me]
    r.kvl[me] = r.kvp[me]

    def kv_spread(k):
        j = lax.rem(me + 1 + k, n)
        copy(r.kvp.at[me], kv_spot, "kg", j, dp=j, got=me).start()

    loop(n - 1, kv_spread)
    dn.spread()
    tok_on = []

    def tok_forward(i):
        spot = tok_land.at[rows_of(far * per + i, TILE)]
        copy(spot, spot, "ty", i, mp=far).wait_recv()
        c = copy(spot, spot, "tc", 2 * i + 1, mp=sib)
        c.start()
        tok_on.append(c)

    sums = small.gather()
    ends = last.gather()
    r.small_o[0:4, :] = sums[0:4]
    for row in range(2):
        for q in range(quarters):
            spot = row * quarters + q
            r.small_o[4 + row : 5 + row, q * LANES : (q + 1) * LANES] = ends[spot : spot + 1]
    r.small_o[6:7, :] = sums[4:5]

    written = []

    def write(src, dst):
        c = local(src, dst, len(written))
        c.start()
        written.append(c)

    def kv_wait(k):
        j = lax.rem(me + 1 + k, n)
        copy(r.kvp.at[me], r.kvl.at[j], "kg", j, dp=j).wait()

    for index, owner in enumerate((sib, farsib)):
        spot = out_land.at[rows_of(owner, Tm)]
        copy(spot, spot, "oc", index, mp=sib).wait_recv()
    write(out_land, r.out_o)
    for i in range(per):
        tok_forward(i)
    up.finish()
    write(up.out.at[pl.ds(0, D)], r.upg_o)
    loop(n - 1, kv_wait)
    write(flat_rows(r.kvl).at[pl.ds(0, 2 * D)], r.kvg_o)
    for i in range(per):
        for index, owner in enumerate((sib, farsib)):
            spot = tok_land.at[rows_of(owner * per + i, TILE)]
            copy(spot, spot, "tc", 2 * i + index, mp=sib).wait_recv()
    write(tok_land, r.gtok_o)
    dn.finish()
    write(dn.out.at[pl.ds(0, plan.tail)], r.dng_o)
    for y, core in tok_sent:
        y.wait_send()
        core.wait_send()
    for c in (out_y, out_core, out_on, *tok_on):
        c.wait_send()
    for c in written:
        c.wait()
    for target in others_mp:
        for i in range(per):
            for c in (grad_copy(target, i), key_copy(target, i)):
                c.wait_send()
        copy(r.grads.at[0, rows_of(target, Tm)], r.garr.at[m, 0], "grq", target, mp=target).wait_send()


def widen_kernel(plan, *refs):
    (output, tokens, up, down, kv, small), refs = refs[:6], refs[6:]
    (out_o, tok_o, qkv_o, ow_o, ob_o, g1_o, b1_o, g2_o, b2_o, up_o, ub_o, dn_o, db_o), refs = (
        refs[:13],
        refs[13:],
    )
    tok_v, out_v, up_v, dn_v, kv_v, tok_w, up_w, dn_w, ow_w, qkv_w, sem_in, sem_out = refs
    D, L, hidden, T = plan.D, plan.L, plan.F, plan.T
    pieces = 4
    size = T // pieces
    reads = [
        pltpu.make_async_copy(a, b, sem_in.at[i])
        for i, (a, b) in enumerate([(up, up_v), (down, dn_v), (kv, kv_v), (output, out_v)])
    ]
    token_reads = [
        pltpu.make_async_copy(
            tokens.at[pl.ds(i * size, size)], tok_v.at[pl.ds(i * size, size)], sem_in.at[4 + i]
        )
        for i in range(pieces)
    ]
    for c in token_reads + reads:
        c.start()
    for row, ref in ((3, ob_o), (4, g1_o), (5, b1_o), (1, g2_o), (2, b2_o), (6, ub_o), (0, db_o)):
        ref[...] = small[row : row + 1, :]
    writes = []

    def send(src, dst):
        c = pltpu.make_async_copy(src, dst, sem_out.at[len(writes)])
        c.start()
        writes.append(c)

    for i in range(pieces):
        token_reads[i].wait()
        rows = pl.ds(i * size, size)
        tok_w[rows, :] = tok_v[rows, :].astype(F32)
        send(tok_w.at[rows], tok_o.at[rows])
    for c in reads:
        c.wait()
    send(out_v, out_o)
    up_w[...] = up_v[...].astype(F32)
    send(up_w, up_o)
    dn_w[...] = dn_v[0:hidden, :].astype(F32)
    send(dn_w, dn_o)
    ow_w[...] = dn_v[hidden : hidden + L, :].astype(F32)
    send(ow_w, ow_o)
    for c in range(D // L):
        qkv_w[0, c * L : (c + 1) * L, :] = dn_v[
            plan.rest : plan.tail, c * L : (c + 1) * L
        ].astype(F32)
    qkv_w[1] = kv_v[0:D, :].astype(F32)
    qkv_w[2] = kv_v[D : 2 * D, :].astype(F32)
    send(qkv_w, qkv_o)
    for c in writes:
        c.wait()


def widen(plan, *gathered):
    D, L, hidden, T = plan.D, plan.L, plan.F, plan.T
    line = ("vmem", (1, D))
    outs = [
        ("hbm", (T, D)),
        ("hbm", (T, D)),
        ("hbm", (3, D, L)),
        ("hbm", (L, D)),
        *[line] * 5,
        ("hbm", (D, hidden)),
        ("vmem", (1, hidden)),
        ("hbm", (hidden, D)),
        line,
    ]
    spaces = {"vmem": pltpu.VMEM, "hbm": pl.ANY}
    results = pl.pallas_call(
        functools.partial(widen_kernel, plan),
        out_shape=[
            jax.ShapeDtypeStruct(shape, BF if i == 0 else F32) for i, (_, shape) in enumerate(outs)
        ],
        in_specs=[pl.BlockSpec(memory_space=pl.ANY)] * 5 + [pl.BlockSpec(memory_space=pltpu.VMEM)],
        out_specs=[pl.BlockSpec(memory_space=spaces[kind]) for kind, _ in outs],
        scratch_shapes=[
            pltpu.VMEM((T, D), BF),
            pltpu.VMEM((T, D), BF),
            pltpu.VMEM((D, hidden), BF),
            pltpu.VMEM((plan.tail, D), BF),
            pltpu.VMEM((2 * D, L), BF),
            pltpu.VMEM((T, D), F32),
            pltpu.VMEM((D, hidden), F32),
            pltpu.VMEM((hidden, D), F32),
            pltpu.VMEM((L, D), F32),
            pltpu.VMEM((3, D, L), F32),
            pltpu.SemaphoreType.DMA((8,)),
            pltpu.SemaphoreType.DMA((16,)),
        ],
        compiler_params=pltpu.CompilerParams(vmem_limit_bytes=60 << 20),
        name="widen",
    )(*gathered)
    return tuple(v.reshape(-1) if v.shape[0] == 1 else v for v in results)


def per_device(
    n,
    nm,
    tokens,
    cotangent,
    bucket,
    cell,
    features,
    qkv_weight,
    out_weight,
    out_bias,
    norm1_gain,
    norm1_bias,
    norm2_gain,
    norm2_bias,
    up_weight,
    up_bias,
    down_weight,
    down_bias,
):
    count, width = tokens.shape
    local, hidden = qkv_weight.shape[2], up_weight.shape[1]
    plan = Plan(n, nm, count, width, local, features.shape[2], hidden)
    spaces = {"vmem": pltpu.VMEM, "hbm": pl.ANY}
    line = lambda v: v.reshape(1, -1)
    grid_ids = (count // LANES, LANES)
    outs = pl.pallas_call(
        functools.partial(layer_kernel, plan),
        out_shape=[jax.ShapeDtypeStruct(s, d) for _, _, s, d in plan.outputs],
        in_specs=[pl.BlockSpec(memory_space=spaces[k]) for _, k in plan.inputs],
        out_specs=[pl.BlockSpec(memory_space=spaces[k]) for _, k, _, _ in plan.outputs],
        scratch_shapes=[pltpu.VMEM(s, d) for _, s, d in plan.scratch]
        + [pltpu.SemaphoreType.DMA((c,)) for c in plan.sems.values() for _ in range(2)]
        + [pltpu.SemaphoreType.DMA((plan.local_sems,))],
        compiler_params=pltpu.CompilerParams(
            collective_id=1, has_side_effects=True, vmem_limit_bytes=63 << 20
        ),
        name="performer_layer",
    )(
        tokens,
        bucket.reshape(grid_ids),
        cell.reshape(grid_ids),
        features,
        qkv_weight,
        line(norm1_gain),
        line(norm1_bias),
        line(out_bias),
        line(norm2_gain),
        line(norm2_bias),
        line(down_bias),
        cotangent,
        out_weight,
        up_weight,
        line(up_bias),
        down_weight,
    )
    return widen(plan, *outs[:6])


def solution(mesh):
    return jax.shard_map(
        functools.partial(per_device, mesh.shape["dp"], mesh.shape["mp"]),
        mesh=mesh,
        in_specs=(
            P("dp", None),
            P("dp", None),
            P("dp", None),
            P("dp"),
            P(),
            P(None, None, "mp"),
            P("mp", None),
            P(),
            P(),
            P(),
            P(),
            P(),
            P(None, "mp"),
            P("mp"),
            P("mp", None),
            P(),
        ),
        out_specs=(
            P("dp", None),
            P("dp", None),
            P(None, None, "mp"),
            P("mp", None),
            P(),
            P(),
            P(),
            P(),
            P(),
            P(None, "mp"),
            P("mp"),
            P("mp", None),
            P(),
        ),
        check_vma=False,
    )
```

```python
import functools
from types import SimpleNamespace

import jax
import jax.numpy as jnp
from jax import lax
from jax.experimental import pallas as pl
from jax.experimental.pallas import tpu as pltpu
from jax.sharding import PartitionSpec as P

HD = 64
FEATS = 4
STEP = 5
SEG = 2
PAD = 8
SCALE = HD**-0.25
HALF_SQUARE = 0.5 * SCALE * SCALE
EPS = 1e-05

BF = jnp.bfloat16
F32 = jnp.float32
MESH = pl.DeviceIdType.MESH
LANES = 128
TILE = 256


def dot(a, b):
    return jnp.dot(a, b, preferred_element_type=F32)


def dot_nt(a, b):
    return lax.dot_general(a, b, (((1,), (1,)), ((), ())), preferred_element_type=F32)


def dot_tn(a, b):
    return lax.dot_general(a, b, (((0,), (0,)), ((), ())), preferred_element_type=F32)


def lane(shape):
    return lax.broadcasted_iota(jnp.int32, shape, len(shape) - 1)


def roll_half(x):
    return pltpu.roll(x, HD, 1)


def loop(count, body, unroll=False):
    if unroll or count <= 3:
        for i in range(count):
            body(i)
    else:

        def step(i, carry):
            body(i)
            return carry

        lax.fori_loop(0, count, step, 0)


def rows_of(i, size):
    if isinstance(i, int):
        return pl.ds(i * size, size)
    return pl.ds(pl.multiple_of(i * size, size), size)


def normalised(values):
    average = jnp.mean(values, -1, keepdims=True)
    centred = values - average
    spread = jnp.mean(centred * centred, -1, keepdims=True)
    scale = lax.rsqrt(spread + EPS)
    return centred * scale, scale


def norm_back(upstream, hat, scale, gain):
    e = gain * upstream
    return (
        e
        - jnp.mean(e, -1, keepdims=True)
        - hat * jnp.mean(e * hat, -1, keepdims=True)
    ) * scale


def round_up(a, b):
    return (a + b - 1) // b * b


class Plan:
    def __init__(self, n, nm, tokens, width, local, feats, hidden):
        self.n, self.nm, self.T, self.D, self.L, self.M, self.F = (
            n,
            nm,
            tokens,
            width,
            local,
            feats,
            hidden,
        )
        self.H = local // HD
        self.HM = self.H * feats
        self.Tm = tokens // nm
        self.big = n > 8
        self.G8 = n * PAD
        self.rest = hidden + local
        self.tail = self.rest + width * local // width
        self.ru, self.rd, self.rk = (
            round_up((rows + n - 1) // n, 16) for rows in (width, self.tail, 2 * width)
        )
        self.per = self.Tm // TILE
        n2 = n // 2
        T, D, L, HM, Tm = self.T, self.D, self.L, self.HM, self.Tm
        vm = "vmem"
        states = (n, HM, SEG * HD)
        place = "hbm" if self.big else vm
        self.inputs = [
            ("tok", "hbm"),
            ("bkt", vm),
            ("cel", vm),
            ("feat", vm),
            ("wqkv", vm),
            ("g1", vm),
            ("b1", vm),
            ("ob", vm),
            ("g2", vm),
            ("b2", vm),
            ("db", vm),
            ("cot", "hbm"),
            ("ow", "hbm"),
            ("up", "hbm"),
            ("ub", "hbm"),
            ("dn", "hbm"),
        ]
        self.outputs = [
            ("out_o", "hbm", (T, D), BF),
            ("gtok_o", "hbm", (T, D), BF),
            ("upg_o", "hbm", (D, hidden), BF),
            ("dng_o", "hbm", (self.tail, D), BF),
            ("kvg_o", "hbm", (2 * D, L), BF),
            ("small_o", vm, (8, D), F32),
        ]
        big_states = [("sp", states), ("rb", states), ("sall", states), ("gall", states)]
        if self.big:
            self.outputs += [(name, "hbm", shape, BF) for name, shape in big_states]
        self.scratch = [
            ("wcat", (D, 4 * L), BF),
            ("f2", (L, HM), BF),
            ("wb", (HM, 2 * L), BF),
            ("ccb", (T, LANES), BF),
            ("oh2", (T, 2 * self.G8), BF),
            ("nm", (T, D), BF),
            ("qk", (2, T, L), BF),
            ("vv", (2, T, L), BF),
            ("qf", (T, HM), BF),
            ("kf", (T, HM), BF),
            ("ft", (HM, T), BF),
            ("tp", (n, PAD, LANES), F32),
            ("trb", (n, PAD, LANES), F32),
            ("tall", (n, PAD, LANES), F32),
            ("gtall", (n, PAD, LANES), F32),
            ("tot2", (2 * self.G8, HM), BF),
            ("acc", (HM, SEG * HD), F32),
            ("attf", (T, L), F32),
            ("inv", (T, L), F32),
            ("attb", (T, L), BF),
            ("arow", (nm, Tm, L), BF),
            ("wq_g", (nm, 3, D, L), BF),
            ("ow_g", (nm, L, D), BF),
            ("up_g", (nm, D, hidden), BF),
            ("ub_g", (nm, 1, hidden), F32),
            ("dn_g", (nm, hidden, D), BF),
            ("cotv", (Tm, D), BF),
            ("tokv", (Tm, D), BF),
            ("mid", (Tm, D), F32),
            ("nm2", (Tm, D), BF),
            ("act", (nm, Tm, hidden), BF),
            ("gp", (nm, Tm, hidden), BF),
            ("bo", (TILE, D), F32),
            ("gn2", (TILE, D), F32),
            ("gb", (Tm, D), BF),
            ("outv", (Tm, D), BF),
            ("small", (16, D), F32),
            ("small_m", (nm, 16, D), F32),
            ("small_d", (n, 8, D), F32),
            ("small_s", (8, D), F32),
            ("ends", (8, D), F32),
            ("last", (8, LANES), F32),
            ("last_m", (nm, 8, LANES), F32),
            ("last_d", (n, 8, LANES), F32),
            ("upp", (nm, D, hidden), BF),
            ("upc", (2, D, hidden), BF),
            ("upy", (n, self.ru, D), BF),
            ("upx", (n2, self.ru, D), BF),
            ("upz", (n2, self.ru, D), BF),
            ("dnp", (nm, self.rest, D), BF),
            ("dnc", (2, self.rest, D), BF),
            ("dny", (n, self.rd, D), BF),
            ("dnx", (n2, self.rd, D), BF),
            ("dnz", (n2, self.rd, D), BF),
            ("gar", (nm, Tm, L), BF),
            ("gad", (2, T, L), BF),
            ("gg", (2, T, L), BF),
            ("gd", (T, L), F32),
            ("grads", (3, T, L), BF),
            ("garr", (nm, 3, Tm, L), BF),
            ("kvp", (n, self.rk, L), BF),
            ("kvr", (n, self.rk, L), BF),
            ("kvl", (n, self.rk, L), BF),
        ]
        if self.big:
            self.scratch += [("stage_a", (2, HM, SEG * HD), BF), ("stage_b", (2, HM, SEG * HD), BF)]
        else:
            self.scratch += [(name, shape, BF) for name, shape in big_states]
            self.scratch += [("num", (T, LANES), F32), ("gkf", (T, self.M), F32)]
        self.sems = {
            **{name: n2 * self.H for name in ("rsx", "rsz", "agz", "agx", "gsx", "gsz", "ggz", "ggx")},
            **{name: n2 for name in ("rtx", "rtz", "atz", "atx", "gtx", "gtz", "hgz", "hgx")},
            **{name: nm * self.per for name in ("a2a", "gaa", "grk")},
            "grq": nm,
            "wy": 5,
            "wc": 10,
            "uc": 2,
            "uy": 1,
            "ux": n2,
            "uz": n2,
            "ugz": n2,
            "ugx": n2,
            "dc": 2,
            "dy": 1,
            "dx": n2,
            "dz": n2,
            "dgz": n2,
            "dgx": n2,
            "ks": n,
            "kg": n,
            "oy": 1,
            "oc": 2,
            "ty": self.per,
            "tc": 2 * self.per,
            "sm": nm,
            "sd": n,
            "lm": nm,
            "ld": n,
        }
        self.local_sems = 24

    def names(self):
        return (
            [x[0] for x in self.inputs]
            + [x[0] for x in self.outputs]
            + [x[0] for x in self.scratch]
            + [f"{k}_{end}" for k in self.sems for end in ("s", "r")]
            + ["lsem"]
        )


def layer_kernel(plan, *refs):
    r = SimpleNamespace(**dict(zip(plan.names(), refs, strict=True)))
    n, nm, T, D, L, M, HM, Tm, H = (
        plan.n,
        plan.nm,
        plan.T,
        plan.D,
        plan.L,
        plan.M,
        plan.HM,
        plan.Tm,
        plan.H,
    )
    hidden = plan.F
    n2 = n // 2
    tiles = T // TILE
    wide = TILE if plan.big else 2 * TILE
    me, m = lax.axis_index("dp"), lax.axis_index("mp")
    sib = m + 1 - 2 * lax.rem(m, 2)
    far = lax.rem(m + nm // 2, nm)
    farsib = lax.rem(sib + nm // 2, nm)
    xpart = me + 1 - 2 * lax.rem(me, 2)
    xme, zme = lax.rem(me, 2), me // 2

    def sem(name, index):
        return getattr(r, f"{name}_s").at[index], getattr(r, f"{name}_r").at[index]

    def copy(src, dst, name, sent, dp=None, mp=None, got=None):
        send, _ = sem(name, sent)
        _, recv = sem(name, sent if got is None else got)
        return pltpu.make_async_remote_copy(
            src_ref=src,
            dst_ref=dst,
            send_sem=send,
            recv_sem=recv,
            device_id=(me if dp is None else dp, m if mp is None else mp),
            device_id_type=MESH,
        )

    def local(src, dst, index):
        return pltpu.make_async_copy(src, dst, r.lsem.at[index])

    low = lane((1, LANES)) < HD

    barrier = pltpu.get_barrier_semaphore()

    def greet(k):
        pl.semaphore_signal(
            barrier, inc=1, device_id=(lax.rem(me + 1 + k, n), m), device_id_type=MESH
        )

    loop(n - 1, greet)
    for k in range(1, nm):
        pl.semaphore_signal(
            barrier, inc=1, device_id=(me, lax.rem(m + k, nm)), device_id_type=MESH
        )

    mine = rows_of(m, Tm)
    wides, len_shards = T // wide, 5

    def tok_in(i):
        rows = rows_of(i, wide)
        return local(r.tok.at[rows], r.nm.at[rows], 1 + len_shards + i)

    own_in = [local(r.cot.at[mine], r.cotv, 0), local(r.tok.at[mine], r.tokv, 1 + len_shards + wides)]
    for c in [tok_in(i) for i in range(wides)] + own_in:
        c.start()

    r.wcat[:, 0:L] = r.wqkv[0]
    r.wcat[:, L : 2 * L] = r.wqkv[1]
    wv = r.wqkv[2].astype(F32)
    wv_rolled = roll_half(wv)
    r.wcat[:, 2 * L : 3 * L] = jnp.where(low, wv, wv_rolled).astype(BF)
    r.wcat[:, 3 * L : 4 * L] = jnp.where(low, wv_rolled, wv).astype(BF)
    feature_rows = r.feat[STEP % FEATS]
    r.f2[...] = jnp.zeros((L, HM), BF)
    for h in range(H):
        r.f2[h * HD : (h + 1) * HD, h * M : (h + 1) * M] = feature_rows
    r.wb[:, 0:L] = r.f2[...].astype(F32).T.astype(BF)
    head_of_row = lax.broadcasted_iota(jnp.int32, (HM, L), 0) // M
    r.wb[:, L : 2 * L] = jnp.where(head_of_row == lane((HM, L)) // HD, 1.0, 0.0).astype(BF)

    count = T // LANES
    numbers = SEG * r.bkt[...].astype(F32) + r.cel[...].astype(F32)
    numbers = jnp.concatenate([numbers, jnp.zeros((LANES - count, LANES), F32)], 0).T
    for i in range(count):
        rows = pl.ds(i * LANES, LANES)
        column = jnp.broadcast_to(numbers[:, i : i + 1], (LANES, LANES))
        r.ccb[rows, :] = (column - jnp.where(low, 0.0, 1.0)).astype(BF)
        for block in range(2 * plan.G8 // LANES):
            place = (lane((1, LANES)) + block * LANES) % plan.G8
            number = place // PAD * SEG + place % SEG
            r.oh2[rows, block * LANES : (block + 1) * LANES] = jnp.where(
                column == number.astype(F32), 1.0, 0.0
            ).astype(BF)
    part_of_row = lax.broadcasted_iota(jnp.int32, (plan.G8, LANES), 0) % PAD // SEG

    def pack_totals(table):
        packed = jnp.zeros((plan.G8, LANES), F32)
        for q in range(HM // LANES):
            packed += jnp.where(part_of_row == q, table[:, q * LANES : (q + 1) * LANES], 0.0)
        return packed.reshape(n, PAD, LANES)

    def spread_totals(packed):
        packed = packed.reshape(plan.G8, LANES)
        return jnp.concatenate(
            [jnp.where(part_of_row == q, packed, 0.0) for q in range(HM // LANES)], 1
        )

    def phi(u):
        wide = u.astype(F32)
        squares = wide * wide
        first = jnp.sum(jnp.where(low, squares, 0.0), -1, keepdims=True)
        second = jnp.sum(jnp.where(low, 0.0, squares), -1, keepdims=True)
        projected = dot(u, r.f2[...]) * SCALE
        shift = jnp.where(lane((1, HM)) < M, first, second) * HALF_SQUARE
        return jnp.exp(projected - shift)

    pl.semaphore_wait(barrier, n - 1 + nm - 1)

    def project(i):
        rows = rows_of(i, wide)
        tok_in(i).wait()
        hat, _ = normalised(r.nm[rows, :].astype(F32))
        normed = (hat * r.g1[...] + r.b1[...]).astype(BF)
        r.nm[rows, :] = normed
        u = dot(normed, r.wcat[:, L:]).astype(BF)
        k = u[:, 0:L]
        r.qk[1, rows, :] = k
        r.vv[0, rows, :], r.vv[1, rows, :] = u[:, L : 2 * L], u[:, 2 * L : 3 * L]
        features = phi(k).astype(BF)
        r.kf[rows, :] = features
        r.ft[:, rows] = features.T

    def queries(i):
        rows = rows_of(i, wide)
        q = dot(r.nm[rows, :], r.wcat[:, 0:L]).astype(BF)
        r.qk[0, rows, :] = q
        r.qf[rows, :] = phi(q).astype(BF)

    shards = [
        (r.ow, r.ow_g),
        (r.up, r.up_g),
        (r.ub, r.ub_g),
        (r.dn, r.dn_g),
        (r.wqkv, r.wq_g),
    ]
    own_copies, y_copies, core_copies = [], [], []
    for i, (src, dst) in enumerate(shards):
        own_copies.append(local(src, dst.at[m], 1 + i))
        y_copies.append(copy(src, dst.at[m], "wy", i, mp=far))
        core_copies.append(copy(src, dst.at[m], "wc", 2 * i, mp=sib))
    for c in own_copies + y_copies + core_copies:
        c.start()
    lax.fori_loop(0, wides, lambda i, carry: (project(i), carry)[1], 0)

    def state_pair(ref, p, stage):
        if plan.big:
            pltpu.sync_copy(ref.at[pl.ds(2 * p, 2)], stage)
            return stage
        return ref.at[pl.ds(2 * p, 2)]

    def masked_pair(rows, dup, p):
        code = r.ccb[rows, :]
        first = jnp.full((1, LANES), 1.0, F32) * (4 * p)
        left = jnp.where(code == first.astype(BF), dup, jnp.zeros_like(dup))
        right = jnp.where(code == (first + 2.0).astype(BF), dup, jnp.zeros_like(dup))
        return jnp.concatenate([left, right], 1)

    everything = pl.ds(0, T)

    def head_rows(h):
        return pl.ds(h * M, M) if isinstance(h, int) else pl.ds(pl.multiple_of(h * M, M), M)

    def at_first(h, body):
        if isinstance(h, int):
            if h == 0:
                body()
        else:
            pl.when(h == 0)(body)

    class Pair:
        def __init__(self, h, state, totals):
            self.h, self.state, self.totals = h, state, totals

        def start(self):
            self.state.start()
            at_first(self.h, lambda: self.totals().start())

        def wait_recv(self):
            self.state.wait_recv()
            at_first(self.h, lambda: self.totals().wait_recv())

        def wait_send(self):
            self.state.wait_send()
            at_first(self.h, lambda: self.totals().wait_send())

    class States:
        def __init__(self, all_s, all_t, names):
            self.all_s, self.all_t = all_s, all_t
            self.x, self.tx, self.z, self.tz, self.gz, self.hz, self.gx, self.hx = names

        def both(self, h, state, totals):
            return Pair(h, state, totals)

        def to_x(self, p, h):
            j, hs = 2 * p + 1 - xme, head_rows(h)
            return self.both(
                h,
                copy(r.sp.at[j, hs], r.rb.at[p, hs], self.x, p * H + h, dp=xpart),
                lambda: copy(r.tp.at[j], r.trb.at[p], self.tx, p, dp=xpart),
            )

        def to_z(self, p, h):
            j, hs = 2 * p + xme, head_rows(h)
            return self.both(
                h,
                copy(
                    r.sp.at[j, hs],
                    r.rb.at[n2 + zme, hs],
                    self.z,
                    p * H + h,
                    dp=j,
                    got=zme * H + h,
                ),
                lambda: copy(r.tp.at[j], r.trb.at[n2 + zme], self.tz, p, dp=j, got=zme),
            )

        def from_z(self, p, h):
            j, hs = 2 * p + xme, head_rows(h)
            return self.both(
                h,
                copy(r.sp.at[j, hs], r.rb.at[n2 + p, hs], self.z, p * H + h, dp=j),
                lambda: copy(r.tp.at[j], r.trb.at[n2 + p], self.tz, p, dp=j),
            )

        def out_z(self, p, h):
            j, hs = 2 * p + xme, head_rows(h)
            s, t = self.all_s.at[me, hs], self.all_t.at[me]
            return self.both(
                h,
                copy(s, s, self.gz, p * H + h, dp=j, got=zme * H + h),
                lambda: copy(t, t, self.hz, p, dp=j, got=zme),
            )

        def in_z(self, p, h):
            j, hs = 2 * p + xme, head_rows(h)
            s, t = self.all_s.at[j, hs], self.all_t.at[j]
            return self.both(
                h,
                copy(s, s, self.gz, p * H + h, dp=j),
                lambda: copy(t, t, self.hz, p, dp=j),
            )

        def out_x(self, p, h, other=False):
            j, hs = 2 * p + (1 - xme if other else xme), head_rows(h)
            s, t = self.all_s.at[j, hs], self.all_t.at[j]
            return self.both(
                h,
                copy(s, s, self.gx, p * H + h, dp=xpart),
                lambda: copy(t, t, self.hx, p, dp=xpart),
            )

        def start(self, dup):
            def pair(q, carry):
                h, p = q // n2, lax.rem(zme + 1 + lax.rem(q, n2), n2)
                block = dot(r.ft[head_rows(h), :], masked_pair(everything, dup[h], p))
                put_state(r.sp, 2 * p, h, block[:, :LANES].astype(BF))
                put_state(r.sp, 2 * p + 1, h, block[:, LANES:].astype(BF))
                self.to_x(p, h).start()
                return carry

            lax.fori_loop(0, H * n2, pair, 0)

        def add_x(self, p, h):
            self.to_x(p, h).wait_recv()
            j = 2 * p + xme

            def totals():
                r.tp[j] += r.trb[p]

            at_first(h, totals)
            return get_state(r.sp, j, h) + get_state(r.rb, p, h)

        def near(self, h, k):
            p = lax.rem(zme + 1 + k, n2)
            put_state(r.sp, 2 * p + xme, h, self.add_x(p, h).astype(BF))
            self.to_z(p, h).start()

        def own(self, h):
            r.acc[head_rows(h), :] = self.add_x(zme, h)

        def whole(self, h):
            def take(k):
                p = lax.rem(zme + 1 + k, n2)
                self.from_z(p, h).wait_recv()
                r.acc[head_rows(h), :] += get_state(r.rb, n2 + p, h)
                if h == 0:
                    r.tp[me] += r.trb[n2 + p]

            loop(n2 - 1, take)
            if h == 0:
                self.all_t[me] = r.tp[me]
            put_state(self.all_s, me, h, r.acc[head_rows(h), :].astype(BF))

            def send(k):
                self.out_z(lax.rem(zme + 1 + k, n2), h).start()

            loop(n2 - 1, send)
            self.out_x(zme, h).start()

        def onward(self, h, k):
            p = lax.rem(zme + 1 + k, n2)
            self.in_z(p, h).wait_recv()
            self.out_x(p, h).start()

        def arrived(self, p, h):
            self.out_x(p, h, other=True).wait_recv()

        def run(self, work, rest, use, midway):
            others = n2 - 1
            steps = H * others

            def step(q, carry):
                h, k = q // others, lax.rem(q, others)
                pl.when(q == steps - 1)(lambda: self.whole(0))
                self.near(h, k)
                work(q)
                pl.when(k == others - 1)(lambda: self.own(h))
                return carry

            lax.fori_loop(0, steps, step, 0)
            rest()
            self.whole(H - 1)
            loop(others, lambda k: self.onward(0, k))
            for h in range(H):
                loop(n2, lambda p, h=h: self.arrived(p, h))
                if h < H - 1:
                    loop(others, lambda k, h=h: self.onward(h + 1, k))
                    use(h)
                    midway()
            for h in range(H):

                def sent(p, h=h):
                    self.to_x(p, h).wait_send()
                    self.out_x(p, h).wait_send()

                loop(n2, sent)

                def sent_z(k, h=h):
                    p = lax.rem(zme + 1 + k, n2)
                    self.to_z(p, h).wait_send()
                    self.out_z(p, h).wait_send()

                loop(others, sent_z)
            total = spread_totals(self.all_t[...])
            top = total.astype(BF)
            r.tot2[0 : plan.G8, :] = top
            r.tot2[plan.G8 :, :] = (total - top.astype(F32)).astype(BF)

    def put_state(ref, j, h, values):
        if plan.big:
            spot = r.stage_b.at[0, head_rows(h)]
            spot[...] = values
            pltpu.sync_copy(spot, ref.at[j, head_rows(h)])
        else:
            ref[j, head_rows(h), :] = values

    def get_state(ref, j, h):
        if plan.big:
            spot = r.stage_b.at[1, head_rows(h)]
            pltpu.sync_copy(ref.at[j, head_rows(h)], spot)
            return spot[...].astype(F32)
        return ref[j, head_rows(h), :].astype(F32)

    def state_columns(ref, p, h):
        blocks = state_pair(ref, p, r.stage_a if plan.big else None)
        return jnp.concatenate([blocks[0, head_rows(h), :], blocks[1, head_rows(h), :]], 1)

    def pick(code, product, p, rest):
        first = jnp.full((1, LANES), 1.0, F32) * (4 * p)
        rest = jnp.where(code == first, product[:, :LANES], rest)
        return jnp.where(code == first + 2.0, product[:, LANES:], rest)

    def times_state(rows, left, all_s, h):
        code, features = r.ccb[rows, :].astype(F32), left[rows, head_rows(h)]

        def pair(p, total):
            return pick(code, dot(features, state_columns(all_s, p, h)), p, total)

        total = jnp.zeros((rows.size, LANES), F32)
        if plan.big:
            return lax.fori_loop(0, n2, pair, total)
        for p in range(n2):
            total = pair(p, total)
        return total

    def own_state(rows, left, all_s):
        ready = [] if plan.big else [r.num[rows, :]]
        heads = ready + [times_state(rows, left, all_s, h) for h in range(len(ready), H)]
        return halves(*(head + roll_half(head) for head in heads))

    def halves(first, second):
        return jnp.where(low, first, second)

    def early(left, all_s):
        def run(h):
            if plan.big:
                return

            def tile(i, carry):
                rows = rows_of(i, wide)
                r.num[rows, :] = times_state(rows, left, all_s, h)
                return carry

            lax.fori_loop(0, wides, tile, 0)

        return run

    first = States(
        r.sall, r.tall, ("rsx", "rtx", "rsz", "rtz", "agz", "atz", "agx", "atx")
    )
    r.tp[...] = pack_totals(dot_tn(r.oh2[:, : plan.G8], r.kf[...]))
    first.start(r.vv)

    onward = []

    def weights_on(which):
        for i in which:
            dst = shards[i][1]
            copy(dst.at[far], dst.at[far], "wy", i, mp=far).wait_recv()
            c = copy(dst.at[far], dst.at[far], "wc", 2 * i + 1, mp=sib)
            c.start()
            onward.append(c)

    def turn(source):
        def tile(i):
            rows = rows_of(i, TILE)
            r.ft[:, rows] = source[rows, :].T

        return lambda: loop(tiles, tile)

    def in_quarters(body, size):
        quarter = T // size // 4

        def work(q):
            def tile(i, carry):
                body(q * quarter + i)
                return carry

            pl.when(q < 4)(lambda: (lax.fori_loop(0, quarter, tile, 0), None)[1])

        return work

    first.run(
        in_quarters(queries, wide),
        turn(r.qf),
        early(r.qf, r.sall),
        lambda: weights_on(range(4)),
    )

    def own_totals(rows):
        return dot(r.oh2[rows, :], r.tot2[...])

    def attend(i):
        rows = rows_of(i, TILE)
        numerator = own_state(rows, r.qf, r.sall)
        product = r.qf[rows, :].astype(F32) * own_totals(rows)
        denominator = halves(
            jnp.sum(product[:, :M], -1, keepdims=True),
            jnp.sum(product[:, M:], -1, keepdims=True),
        )
        inverse = 1.0 / denominator
        attention = numerator / denominator
        r.attf[rows, :] = attention
        r.inv[rows, :] = inverse
        r.attb[rows, :] = attention.astype(BF)

    per = plan.per
    chunk_order = [far, farsib, sib, m]
    others_mp = chunk_order[: nm - 1]

    def swap(src, dst, name, target, i):
        return copy(src, dst, name, target * per + i, mp=target, got=m * per + i)

    def swapped(dst, name, source, i):
        return copy(dst, dst, name, source * per + i, mp=source)

    def attention_copy(target, i):
        return swap(
            r.attb.at[rows_of(target * per + i, TILE)],
            r.arow.at[m, rows_of(i, TILE)],
            "a2a",
            target,
            i,
        )

    def each_tile(body, after, middle=None):
        def step(q, carry):
            i, k = q // nm, lax.rem(q, nm)
            start = lax.rem(m + (1 - k // 2) * (nm // 2), nm)
            target = start + lax.rem((k + 1) // 2, 2) * (1 - 2 * lax.rem(start, 2))
            body(target * per + i)
            pl.when(k < nm - 1)(lambda: after(target, i).start())
            return carry

        half = per // 2 * nm
        lax.fori_loop(0, half, step, 0)
        if middle is not None:
            middle()
        lax.fori_loop(half, per * nm, step, 0)

    each_tile(attend, attention_copy)
    r.arow[m] = r.attb[rows_of(m, Tm), :]

    def weights_wait(which):
        for i in which:
            dst = shards[i][1]
            own_copies[i].wait()
            copy(dst.at[sib], dst.at[sib], "wc", 2 * i, mp=sib).wait_recv()
            copy(dst.at[farsib], dst.at[farsib], "wc", 2 * i + 1, mp=sib).wait_recv()
            for c in (y_copies[i], core_copies[i], onward[i]):
                c.wait_send()

    weights_wait(range(4))
    for c in own_in:
        c.wait()

    r.small[...] = jnp.zeros((16, D), F32)

    def units(rows, s):
        up, down = r.up_g[s], r.dn_g[s]
        preact = dot(r.nm2[rows, :], up) + r.ub_g[s]
        spread = 0.5 + 0.5 * lax.erf(preact * (0.5**0.5))
        active = (preact * spread).astype(BF)
        r.act[s, rows, :] = active
        slope = spread + preact * jnp.exp(preact * preact * -0.5) * 0.3989422804014327
        grad = (dot_nt(r.cotv[rows, :], down) * slope).astype(BF)
        r.gp[s, rows, :] = grad
        r.bo[...] += dot(active, down)
        r.gn2[...] += dot_nt(grad, up)
        r.small[pl.ds(8 + s, 1), :] += jnp.sum(grad.astype(F32), 0, keepdims=True)

    gas = r.attb.reshape(nm, Tm, L)

    def grad_copy(target, i):
        rows = rows_of(i, TILE)
        return swap(gas.at[target, rows], r.gar.at[m, rows], "gaa", target, i)

    def middle_rows(i):
        rows = rows_of(i, TILE)
        for target in others_mp:
            swapped(r.arow.at[target, rows], "a2a", target, i).wait_recv()
            attention_copy(target, i).wait_send()
        columns = jnp.concatenate([r.arow[s, rows, :] for s in range(nm)], 1)
        branch = dot(columns, r.ow_g[...].reshape(D, D)).astype(BF).astype(F32)
        middle = r.tokv[rows, :].astype(F32) + branch + r.ob[...]
        hat, scale = normalised(middle)
        normed = hat * r.g2[...] + r.b2[...]
        r.mid[rows, :] = middle
        r.nm2[rows, :] = normed.astype(BF)
        r.bo[...] = jnp.zeros((TILE, D), F32)
        r.gn2[...] = jnp.zeros((TILE, D), F32)
        lax.fori_loop(0, nm, lambda s, carry: (units(rows, s), carry)[1], 0)
        middle = r.mid[rows, :]
        r.outv[rows, :] = (middle + r.bo[...] + r.db[...]).astype(BF)
        hat, scale = normalised(middle)
        upstream = r.gn2[...]
        cotangent = r.cotv[rows, :].astype(F32)
        grad = cotangent + norm_back(upstream, hat, scale, r.g2[...])
        low_grad = grad.astype(BF)
        back = dot_nt(low_grad, r.ow_g[...].reshape(D, D)).astype(BF)
        for s in range(nm):
            gas[s, rows, :] = back[:, s * L : (s + 1) * L]
        for target in others_mp:
            grad_copy(target, i).start()
        r.mid[rows, :] = grad
        r.gb[rows, :] = low_grad
        r.small[0:1, :] += jnp.sum(cotangent, 0, keepdims=True)
        r.small[1:2, :] += jnp.sum(upstream * hat, 0, keepdims=True)
        r.small[2:3, :] += jnp.sum(upstream, 0, keepdims=True)
        r.small[3:4, :] += jnp.sum(grad, 0, keepdims=True)

    lax.fori_loop(0, per, lambda i, carry: (middle_rows(i), carry)[1], 0)
    r.gar[m] = gas[m]

    up_core = [
        copy(r.upp.at[sib], r.upc.at[0], "uc", 0, mp=sib),
        copy(r.upp.at[farsib], r.upc.at[1], "uc", 1, mp=sib),
    ]
    dn_core = [
        copy(r.dnp.at[sib], r.dnc.at[0], "dc", 0, mp=sib),
        copy(r.dnp.at[farsib], r.dnc.at[1], "dc", 1, mp=sib),
    ]

    def up_part(s):
        r.upp[s] = dot_tn(r.nm2[...], r.gp[s]).astype(BF)

    def down_part(s):
        r.dnp[s, 0:hidden, :] = dot_tn(r.act[s], r.cotv[...]).astype(BF)
        r.dnp[s, hidden : hidden + L, :] = dot_tn(r.arow[s], r.gb[...]).astype(BF)

    lax.fori_loop(0, nm, lambda s, carry: (up_part(s), carry)[1], 0)
    for c in up_core:
        c.start()
    lax.fori_loop(0, nm, lambda s, carry: (down_part(s), carry)[1], 0)
    for c in dn_core:
        c.start()

    def flat_rows(ref):
        return ref.reshape(ref.shape[0] * ref.shape[1], ref.shape[2])

    def core_sum(copies, part, other, y, name):
        for c in copies:
            c.wait()
        rows = part.shape[1]

        def add(i):
            strip = rows_of(i, LANES)
            part[far, strip, :] = (
                part[far, strip, :].astype(F32) + other[1, strip, :].astype(F32)
            ).astype(BF)

        loop(rows // LANES, add)
        return copy(part.at[far], flat_rows(y).at[pl.ds(0, rows)], name, 0, mp=far)

    def y_sum(sent, part, other, y):
        sent.wait()
        flat = flat_rows(y)

        def add(i):
            strip = rows_of(i, LANES)
            flat[strip, :] = (
                part[m, strip, :].astype(F32)
                + other[0, strip, :].astype(F32)
                + flat[strip, :].astype(F32)
            ).astype(BF)

        loop(part.shape[1] // LANES, add)

    class Reduction:
        def __init__(self, source, rx, rz, out, names):
            self.source, self.rx, self.rz, self.out = source, rx, rz, out
            self.x, self.z, self.gz, self.gx = names

        def block(self, k):
            return self.source.at[xme * n2 + k]

        def to_x(self, k):
            return copy(self.source.at[(1 - xme) * n2 + k], self.rx.at[k], self.x, k, dp=xpart)

        def start(self):
            loop(n2, lambda k: self.to_x(lax.rem(zme + 1 + k, n2)).start())

        def scatter(self):
            def add(k):
                self.to_x(k).wait()
                ref = self.block(k)
                ref[...] = (ref[...].astype(F32) + self.rx[k].astype(F32)).astype(BF)

            def send(k):
                z = lax.rem(zme + 1 + k, n2)
                add(z)
                copy(self.block(z), self.rz.at[zme], self.z, z, dp=2 * z + xme, got=zme).start()

            loop(n2 - 1, send)
            add(zme)

        def gather(self):
            own = self.block(zme)

            def take(k, total):
                z = lax.rem(zme + 1 + k, n2)
                copy(self.block(z), self.rz.at[z], self.z, z, dp=2 * z + xme).wait()
                return total + self.rz[z].astype(F32)

            total = own[...].astype(F32)
            if n2 <= 4:
                for k in range(n2 - 1):
                    total = take(k, total)
            else:
                total = lax.fori_loop(0, n2 - 1, take, total)
            own[...] = total.astype(BF)
            self.place(xme * n2 + zme, 1)[...] = own[...]
            spot = self.place(xme * n2 + zme, 1)

            def send(k):
                z = lax.rem(zme + 1 + k, n2)
                copy(own, spot, self.gz, z, dp=2 * z + xme, got=zme).start()

            loop(n2 - 1, send)
            self.over_x(zme).start()

        def over_x(self, z, side=None):
            spot = self.place((xme if side is None else side) * n2 + z, 1)
            return copy(spot, spot, self.gx, z, dp=xpart)

        def spread(self):
            own = self.block(zme)

            def onward(k):
                z = lax.rem(zme + 1 + k, n2)
                copy(own, self.place(xme * n2 + z, 1), self.gz, z, dp=2 * z + xme).wait()
                self.over_x(z).start()

            loop(n2 - 1, onward)

        def finish(self):
            def wait(z):
                self.over_x(z, 1 - xme).wait_recv()
                self.over_x(z).wait_send()

            loop(n2, wait)

        def place(self, index, count):
            rows = self.source.shape[1]
            return self.out.at[pl.ds(pl.multiple_of(index * rows, rows), count * rows)]

    up = Reduction(r.upy, r.upx, r.upz, flat_rows(r.upc), ("ux", "uz", "ugz", "ugx"))
    dn = Reduction(r.dny, r.dnx, r.dnz, flat_rows(r.dnc), ("dx", "dz", "dgz", "dgx"))

    class Sums:
        def __init__(self, own, over_m, names):
            self.own, self.over_m, self.names = own, over_m, names

        def start(self):
            for target in others_mp:
                copy(
                    self.own, self.over_m.at[m], self.names[0], target, mp=target, got=m
                ).start()

        def scatter(self, send, over_d, keep):
            total = self.own[...]
            for target in others_mp:
                copy(self.own, self.over_m.at[target], self.names[0], target, mp=target).wait()
                total += self.over_m[target]
            self.send, self.over_d = send, over_d
            self.send[...] = keep(total)

            def go(k):
                j = lax.rem(me + 1 + k, n)
                copy(self.send, over_d.at[me], self.names[1], j, dp=j, got=me).start()

            loop(n - 1, go)

        def gather(self):
            self.total = self.send[...]

            def take(k, total):
                j = lax.rem(me + 1 + k, n)
                copy(self.send, self.over_d.at[j], self.names[1], j, dp=j).wait()
                return total + self.over_d[j]

            return lax.fori_loop(0, n - 1, take, self.send[...])

    small = Sums(r.small, r.small_m, ("sm", "sd"))
    last = Sums(r.last, r.last_m, ("lm", "ld"))
    small.start()
    weights_on([4])
    for i in range(per):
        for target in others_mp:
            swapped(r.gar.at[target, rows_of(i, TILE)], "gaa", target, i).wait_recv()
    up_y = core_sum(up_core, r.upp, r.upc, r.upy, "uy")
    up_y.start()

    def grad_rows(i):
        rows = rows_of(i, wide)
        s = i // (Tm // wide)
        inner = rows_of(i - s * (Tm // wide), wide)
        grad = r.gar[s, inner, :].astype(F32)
        inv = r.inv[rows, :]
        scaled = grad * inv
        g_roll, s_roll = roll_half(grad), roll_half(scaled)
        r.gad[0, rows, :] = halves(grad, g_roll).astype(BF)
        r.gad[1, rows, :] = halves(g_roll, grad).astype(BF)
        r.gg[0, rows, :] = halves(scaled, s_roll).astype(BF)
        r.gg[1, rows, :] = halves(s_roll, scaled).astype(BF)
        product = scaled * r.attf[rows, :]
        r.gd[rows, :] = -halves(
            jnp.sum(jnp.where(low, product, 0.0), -1, keepdims=True),
            jnp.sum(jnp.where(low, 0.0, product), -1, keepdims=True),
        )

    lax.fori_loop(0, wides, lambda i, carry: (grad_rows(i), carry)[1], 0)

    def head_column(values, h):
        return values[:, h * HD : h * HD + 1]

    head_totals = []
    for h in range(H):
        column = r.gd[:, h * HD : h * HD + 1]
        top = column.astype(BF).astype(F32)
        upper = lane((1, 2 * plan.G8)) < plan.G8
        weights = r.oh2[...] * jnp.where(upper, top, column - top).astype(BF)
        summed = dot_tn(weights, r.qf[:, h * M : (h + 1) * M])
        head_totals.append(summed[: plan.G8] + summed[plan.G8 :])
    r.tp[...] = pack_totals(jnp.concatenate(head_totals, 1))
    dn_y = core_sum(dn_core, r.dnp, r.dnc, r.dny, "dy")
    dn_y.start()
    second = States(
        r.gall, r.gtall, ("gsx", "gtx", "gsz", "gtz", "ggz", "hgz", "ggx", "hgx")
    )
    second.start(r.gg)

    def contract(rows, dup, all_s, h):
        def pair(p, total):
            return total + dot_nt(masked_pair(rows, dup[h, rows, :], p), state_columns(all_s, p, h))

        total = jnp.zeros((rows.size, M), F32)
        if plan.big:
            return lax.fori_loop(0, n2, pair, total)
        for p in range(n2):
            total = pair(p, total)
        return total

    def early_keys(h):
        if plan.big:
            return

        def tile(i, carry):
            rows = rows_of(i, wide)
            r.gkf[rows, :] = contract(rows, r.vv, r.gall, h)
            return carry

        lax.fori_loop(0, wides, tile, 0)
        early(r.kf, r.gall)(h)

    def feature_back(rows, which, grad_features):
        u = r.qk[which, rows, :]
        weighted = (grad_features * phi(u)).astype(BF)
        both = dot(weighted, r.wb[...])
        return (
            both[:, :L] * SCALE - both[:, L:] * u.astype(F32) * (SCALE * SCALE)
        ).astype(BF)

    def query_back(i):
        rows = rows_of(i, wide)
        totals = own_totals(rows)
        inv, gd = r.inv[rows, :], r.gd[rows, :]
        parts = [
            contract(rows, r.gad, r.sall, h) * head_column(inv, h)
            + totals[:, h * M : (h + 1) * M] * head_column(gd, h)
            for h in range(H)
        ]
        r.grads[0, rows, :] = feature_back(rows, 0, jnp.concatenate(parts, 1))

    def own_unit_sums(total):
        rows = lax.broadcasted_iota(jnp.int32, (16, 1), 0)
        units_row = jnp.sum(jnp.where(rows == 8 + m, total, 0.0), 0, keepdims=True)
        return jnp.concatenate([total[0:4], units_row, jnp.zeros((3, D), F32)], 0)

    def small_scatter():
        small.scatter(r.small_s, r.small_d, own_unit_sums)

    def send_query_grads():
        for target in others_mp:
            copy(
                r.grads.at[0, rows_of(target, Tm)], r.garr.at[m, 0], "grq", target, mp=target, got=m
            ).start()

    def query_projection():
        part = dot(r.ft[...], r.grads[0]).astype(BF)
        flat = flat_rows(r.dny)
        for c in range(D // L):
            flat[plan.rest : plan.tail, c * L : (c + 1) * L] = part[c * L : (c + 1) * L, :]

    gtv = r.nm2
    out_land, tok_land = flat_rows(r.dn_g), flat_rows(r.up_g)
    out_y = copy(r.outv, out_land.at[mine], "oy", 0, mp=far)
    out_core = copy(r.outv, out_land.at[mine], "oc", 0, mp=sib)

    def start_up():
        y_sum(up_y, r.upp, r.upc, r.upy)
        up.start()

    def midway():
        y_sum(dn_y, r.dnp, r.dnc, r.dny)
        dn.start()
        out_y.start()
        out_core.start()
        up.scatter()

    def after_queries():
        send_query_grads()
        turn(r.nm)()
        query_projection()
        start_up()
        small_scatter()

    second.run(in_quarters(query_back, wide), after_queries, early_keys, midway)
    dn.scatter()
    out_land[mine, :] = r.outv[...]

    def key_back(i):
        rows = rows_of(i, TILE)
        totals = own_totals(rows)
        ready = [] if plan.big else [r.gkf[rows, :]]
        parts = ready + [contract(rows, r.vv, r.gall, h) for h in range(len(ready), H)]
        gkf = jnp.concatenate(parts, 1)
        r.grads[1, rows, :] = feature_back(rows, 1, gkf + totals)
        r.grads[2, rows, :] = own_state(rows, r.kf, r.gall).astype(BF)

    both = pl.ds(1, 2)

    def key_copy(target, i):
        return swap(
            r.grads.at[both, rows_of(target * per + i, TILE)],
            r.garr.at[m, both, rows_of(i, TILE)],
            "grk",
            target,
            i,
        )

    each_tile(key_back, key_copy, up.gather)
    for a in range(3):
        r.garr[m, a] = r.grads[a, rows_of(m, Tm), :]

    part = dot(r.ft[...], jnp.concatenate([r.grads[1], r.grads[2]], 1)).astype(BF)
    flat = flat_rows(r.kvp)
    flat[0:D, :] = part[:, :L]
    flat[D : 2 * D, :] = part[:, L:]

    def kv_send(k):
        j = lax.rem(me + 1 + k, n)
        copy(r.kvp.at[j], r.kvr.at[me], "ks", j, dp=j, got=me).start()

    loop(n - 1, kv_send)

    out_far = out_land.at[rows_of(far, Tm)]
    copy(out_far, out_far, "oy", 0, mp=far).wait_recv()
    out_on = copy(out_far, out_far, "oc", 1, mp=sib)
    out_on.start()

    for target in others_mp:
        copy(r.garr.at[target, 0], r.garr.at[target, 0], "grq", target, mp=target).wait_recv()
    weights_wait([4])
    r.ends[...] = jnp.zeros((8, D), F32)

    quarters = D // LANES

    def send_ends():
        for row in range(2):
            for q in range(quarters):
                spot = row * quarters + q
                r.last[spot : spot + 1, :] = r.ends[row : row + 1, q * LANES : (q + 1) * LANES]
        last.start()

    def norm1_back(i):
        rows = rows_of(i, TILE)
        for target in others_mp:
            swapped(r.garr.at[target, both, rows], "grk", target, i).wait_recv()
        upstream = jnp.zeros((TILE, D), F32)
        for s in range(nm):
            left = jnp.concatenate([r.garr[s, a, rows, :] for a in range(3)], 1)
            right = jnp.concatenate([r.wq_g[s, a] for a in range(3)], 1)
            upstream += dot_nt(left, right)
        upstream = upstream.astype(BF).astype(F32)
        hat, scale = normalised(r.tokv[rows, :].astype(F32))
        gtv[rows, :] = (r.mid[rows, :] + norm_back(upstream, hat, scale, r.g1[...])).astype(BF)
        r.ends[0:1, :] += jnp.sum(upstream * hat, 0, keepdims=True)
        r.ends[1:2, :] += jnp.sum(upstream, 0, keepdims=True)
        pl.when(i == per - 1)(send_ends)
        for c in tok_copies(i):
            c.start()

        @pl.when(i == 0)
        def _():
            dn.gather()
            up.spread()

    def tok_copies(i):
        rows = rows_of(i, TILE)
        spot = tok_land.at[rows_of(m * per + i, TILE)]
        return (
            copy(gtv.at[rows], spot, "ty", i, mp=far),
            copy(gtv.at[rows], spot, "tc", 2 * i, mp=sib),
        )

    lax.fori_loop(0, per, lambda i, carry: (norm1_back(i), carry)[1], 0)
    tok_land[mine, :] = gtv[...]

    def kv_sum():
        total = r.kvp[me].astype(F32)

        def take(k, total):
            j = lax.rem(me + 1 + k, n)
            copy(r.kvp.at[j], r.kvr.at[j], "ks", j, dp=j).wait()
            return total + r.kvr[j].astype(F32)

        r.kvp[me] = lax.fori_loop(0, n - 1, take, total).astype(BF)

    kv_sum()
    last.scatter(r.last, r.last_d, lambda total: total)
    kv_spot = r.kvl.at[me]
    r.kvl[me] = r.kvp[me]

    def kv_spread(k):
        j = lax.rem(me + 1 + k, n)
        copy(r.kvp.at[me], kv_spot, "kg", j, dp=j, got=me).start()

    loop(n - 1, kv_spread)
    dn.spread()
    tok_on = []

    def tok_forward(i):
        spot = tok_land.at[rows_of(far * per + i, TILE)]
        copy(spot, spot, "ty", i, mp=far).wait_recv()
        c = copy(spot, spot, "tc", 2 * i + 1, mp=sib)
        c.start()
        tok_on.append(c)

    sums = small.gather()
    ends = last.gather()
    r.small_o[0:4, :] = sums[0:4]
    for row in range(2):
        for q in range(quarters):
            spot = row * quarters + q
            r.small_o[4 + row : 5 + row, q * LANES : (q + 1) * LANES] = ends[spot : spot + 1]
    r.small_o[6:7, :] = sums[4:5]

    written = []

    def write(src, dst):
        c = local(src, dst, len(written))
        c.start()
        written.append(c)

    def kv_wait(k):
        j = lax.rem(me + 1 + k, n)
        copy(r.kvp.at[me], r.kvl.at[j], "kg", j, dp=j).wait()

    for index, owner in enumerate((sib, farsib)):
        spot = out_land.at[rows_of(owner, Tm)]
        copy(spot, spot, "oc", index, mp=sib).wait_recv()
    write(out_land, r.out_o)
    for i in range(per):
        tok_forward(i)
    up.finish()
    write(up.out.at[pl.ds(0, D)], r.upg_o)
    loop(n - 1, kv_wait)
    write(flat_rows(r.kvl).at[pl.ds(0, 2 * D)], r.kvg_o)
    for i in range(per):
        for index, owner in enumerate((sib, farsib)):
            spot = tok_land.at[rows_of(owner * per + i, TILE)]
            copy(spot, spot, "tc", 2 * i + index, mp=sib).wait_recv()
    write(tok_land, r.gtok_o)
    dn.finish()
    write(dn.out.at[pl.ds(0, plan.tail)], r.dng_o)
    for i in range(per):
        for c in tok_copies(i):
            c.wait_send()
    for c in (out_y, out_core, out_on, *tok_on):
        c.wait_send()
    for c in written:
        c.wait()
    for target in others_mp:
        for i in range(per):
            for c in (grad_copy(target, i), key_copy(target, i)):
                c.wait_send()
        copy(r.grads.at[0, rows_of(target, Tm)], r.garr.at[m, 0], "grq", target, mp=target).wait_send()


def widen_kernel(plan, *refs):
    (output, tokens, up, down, kv, small), refs = refs[:6], refs[6:]
    (out_o, tok_o, qkv_o, ow_o, ob_o, g1_o, b1_o, g2_o, b2_o, up_o, ub_o, dn_o, db_o), refs = (
        refs[:13],
        refs[13:],
    )
    tok_v, out_v, up_v, dn_v, kv_v, tok_w, up_w, dn_w, ow_w, qkv_w, sem_in, sem_out = refs
    D, L, hidden, T = plan.D, plan.L, plan.F, plan.T
    pieces = 8
    size = T // pieces
    reads = [
        pltpu.make_async_copy(a, b, sem_in.at[i])
        for i, (a, b) in enumerate([(up, up_v), (down, dn_v), (kv, kv_v), (output, out_v)])
    ]
    token_reads = [
        pltpu.make_async_copy(
            tokens.at[pl.ds(i * size, size)], tok_v.at[pl.ds(i * size, size)], sem_in.at[4 + i]
        )
        for i in range(pieces)
    ]
    for c in token_reads + reads:
        c.start()
    for row, ref in ((3, ob_o), (4, g1_o), (5, b1_o), (1, g2_o), (2, b2_o), (6, ub_o), (0, db_o)):
        ref[...] = small[row : row + 1, :]
    writes = []

    def send(src, dst):
        c = pltpu.make_async_copy(src, dst, sem_out.at[len(writes)])
        c.start()
        writes.append(c)

    for i in range(pieces):
        token_reads[i].wait()
        if i == 1:
            reads[3].wait()
            for part in range(2):
                through = pl.ds(part * (T // 2), T // 2)
                send(out_v.at[through], out_o.at[through])
        rows = pl.ds(i * size, size)
        tok_w[rows, :] = tok_v[rows, :].astype(F32)
        send(tok_w.at[rows], tok_o.at[rows])
    for c in reads[:3]:
        c.wait()
    up_w[...] = up_v[...].astype(F32)
    send(up_w, up_o)
    dn_w[...] = dn_v[0:hidden, :].astype(F32)
    send(dn_w, dn_o)
    ow_w[...] = dn_v[hidden : hidden + L, :].astype(F32)
    send(ow_w, ow_o)
    for c in range(D // L):
        qkv_w[0, c * L : (c + 1) * L, :] = dn_v[
            plan.rest : plan.tail, c * L : (c + 1) * L
        ].astype(F32)
    qkv_w[1] = kv_v[0:D, :].astype(F32)
    qkv_w[2] = kv_v[D : 2 * D, :].astype(F32)
    send(qkv_w, qkv_o)
    for c in writes:
        c.wait()


def widen(plan, *gathered):
    D, L, hidden, T = plan.D, plan.L, plan.F, plan.T
    line = ("vmem", (1, D))
    outs = [
        ("hbm", (T, D)),
        ("hbm", (T, D)),
        ("hbm", (3, D, L)),
        ("hbm", (L, D)),
        *[line] * 5,
        ("hbm", (D, hidden)),
        ("vmem", (1, hidden)),
        ("hbm", (hidden, D)),
        line,
    ]
    spaces = {"vmem": pltpu.VMEM, "hbm": pl.ANY}
    results = pl.pallas_call(
        functools.partial(widen_kernel, plan),
        out_shape=[
            jax.ShapeDtypeStruct(shape, BF if i == 0 else F32) for i, (_, shape) in enumerate(outs)
        ],
        in_specs=[pl.BlockSpec(memory_space=pl.ANY)] * 5 + [pl.BlockSpec(memory_space=pltpu.VMEM)],
        out_specs=[pl.BlockSpec(memory_space=spaces[kind]) for kind, _ in outs],
        scratch_shapes=[
            pltpu.VMEM((T, D), BF),
            pltpu.VMEM((T, D), BF),
            pltpu.VMEM((D, hidden), BF),
            pltpu.VMEM((plan.tail, D), BF),
            pltpu.VMEM((2 * D, L), BF),
            pltpu.VMEM((T, D), F32),
            pltpu.VMEM((D, hidden), F32),
            pltpu.VMEM((hidden, D), F32),
            pltpu.VMEM((L, D), F32),
            pltpu.VMEM((3, D, L), F32),
            pltpu.SemaphoreType.DMA((16,)),
            pltpu.SemaphoreType.DMA((24,)),
        ],
        compiler_params=pltpu.CompilerParams(vmem_limit_bytes=60 << 20),
        name="widen",
    )(*gathered)
    return tuple(v.reshape(-1) if v.shape[0] == 1 else v for v in results)


def per_device(
    n,
    nm,
    tokens,
    cotangent,
    bucket,
    cell,
    features,
    qkv_weight,
    out_weight,
    out_bias,
    norm1_gain,
    norm1_bias,
    norm2_gain,
    norm2_bias,
    up_weight,
    up_bias,
    down_weight,
    down_bias,
):
    count, width = tokens.shape
    local, hidden = qkv_weight.shape[2], up_weight.shape[1]
    plan = Plan(n, nm, count, width, local, features.shape[2], hidden)
    spaces = {"vmem": pltpu.VMEM, "hbm": pl.ANY}
    line = lambda v: v.reshape(1, -1)
    grid_ids = (count // LANES, LANES)
    outs = pl.pallas_call(
        functools.partial(layer_kernel, plan),
        out_shape=[jax.ShapeDtypeStruct(s, d) for _, _, s, d in plan.outputs],
        in_specs=[pl.BlockSpec(memory_space=spaces[k]) for _, k in plan.inputs],
        out_specs=[pl.BlockSpec(memory_space=spaces[k]) for _, k, _, _ in plan.outputs],
        scratch_shapes=[pltpu.VMEM(s, d) for _, s, d in plan.scratch]
        + [pltpu.SemaphoreType.DMA((c,)) for c in plan.sems.values() for _ in range(2)]
        + [pltpu.SemaphoreType.DMA((plan.local_sems,))],
        compiler_params=pltpu.CompilerParams(
            collective_id=1, has_side_effects=True, vmem_limit_bytes=63 << 20
        ),
        name="performer_layer",
    )(
        tokens,
        bucket.reshape(grid_ids),
        cell.reshape(grid_ids),
        features,
        qkv_weight,
        line(norm1_gain),
        line(norm1_bias),
        line(out_bias),
        line(norm2_gain),
        line(norm2_bias),
        line(down_bias),
        cotangent,
        out_weight,
        up_weight,
        line(up_bias),
        down_weight,
    )
    return widen(plan, *outs[:6])


def solution(mesh):
    return jax.shard_map(
        functools.partial(per_device, mesh.shape["dp"], mesh.shape["mp"]),
        mesh=mesh,
        in_specs=(
            P("dp", None),
            P("dp", None),
            P("dp", None),
            P("dp"),
            P(),
            P(None, None, "mp"),
            P("mp", None),
            P(),
            P(),
            P(),
            P(),
            P(),
            P(None, "mp"),
            P("mp"),
            P("mp", None),
            P(),
        ),
        out_specs=(
            P("dp", None),
            P("dp", None),
            P(None, None, "mp"),
            P("mp", None),
            P(),
            P(),
            P(),
            P(),
            P(),
            P(None, "mp"),
            P("mp"),
            P("mp", None),
            P(),
        ),
        check_vma=False,
    )
```

```python
import functools
from types import SimpleNamespace

import jax
import jax.numpy as jnp
from jax import lax
from jax.experimental import pallas as pl
from jax.experimental.pallas import tpu as pltpu
from jax.sharding import PartitionSpec as P

HD = 64
FEATS = 4
STEP = 5
SEG = 2
PAD = 8
SCALE = HD**-0.25
HALF_SQUARE = 0.5 * SCALE * SCALE
EPS = 1e-05

BF = jnp.bfloat16
F32 = jnp.float32
MESH = pl.DeviceIdType.MESH
LANES = 128
TILE = 256


def dot(a, b):
    return jnp.dot(a, b, preferred_element_type=F32)


def dot_nt(a, b):
    return lax.dot_general(a, b, (((1,), (1,)), ((), ())), preferred_element_type=F32)


def dot_tn(a, b):
    return lax.dot_general(a, b, (((0,), (0,)), ((), ())), preferred_element_type=F32)


def lane(shape):
    return lax.broadcasted_iota(jnp.int32, shape, len(shape) - 1)


def roll_half(x):
    return pltpu.roll(x, HD, 1)


def loop(count, body, unroll=False):
    if unroll or count <= 3:
        for i in range(count):
            body(i)
    else:

        def step(i, carry):
            body(i)
            return carry

        lax.fori_loop(0, count, step, 0)


def rows_of(i, size):
    if isinstance(i, int):
        return pl.ds(i * size, size)
    return pl.ds(pl.multiple_of(i * size, size), size)


def normalised(values):
    average = jnp.mean(values, -1, keepdims=True)
    centred = values - average
    spread = jnp.mean(centred * centred, -1, keepdims=True)
    scale = lax.rsqrt(spread + EPS)
    return centred * scale, scale


def norm_back(upstream, hat, scale, gain):
    e = gain * upstream
    return (
        e
        - jnp.mean(e, -1, keepdims=True)
        - hat * jnp.mean(e * hat, -1, keepdims=True)
    ) * scale


def round_up(a, b):
    return (a + b - 1) // b * b


class Plan:
    def __init__(self, n, nm, tokens, width, local, feats, hidden):
        self.n, self.nm, self.T, self.D, self.L, self.M, self.F = (
            n,
            nm,
            tokens,
            width,
            local,
            feats,
            hidden,
        )
        self.H = local // HD
        self.HM = self.H * feats
        self.Tm = tokens // nm
        self.big = n > 8
        self.G8 = n * PAD
        self.rest = hidden + local
        self.tail = self.rest + width * local // width
        self.ru, self.rd, self.rk = (
            round_up((rows + n - 1) // n, 16) for rows in (width, self.tail, 2 * width)
        )
        self.per = self.Tm // TILE
        n2 = n // 2
        T, D, L, HM, Tm = self.T, self.D, self.L, self.HM, self.Tm
        vm = "vmem"
        states = (n, HM, SEG * HD)
        place = "hbm" if self.big else vm
        self.inputs = [
            ("tok", "hbm"),
            ("bkt", vm),
            ("cel", vm),
            ("feat", vm),
            ("wqkv", vm),
            ("g1", vm),
            ("b1", vm),
            ("ob", vm),
            ("g2", vm),
            ("b2", vm),
            ("db", vm),
            ("cot", "hbm"),
            ("ow", "hbm"),
            ("up", "hbm"),
            ("ub", "hbm"),
            ("dn", "hbm"),
        ]
        self.outputs = [
            ("out_o", "hbm", (T, D), BF),
            ("gtok_o", "hbm", (T, D), BF),
            ("upg_o", "hbm", (D, hidden), BF),
            ("dng_o", "hbm", (self.tail, D), BF),
            ("kvg_o", "hbm", (2 * D, L), BF),
            ("small_o", vm, (8, D), F32),
        ]
        big_states = [("sp", states), ("rb", states), ("sall", states), ("gall", states)]
        if self.big:
            self.outputs += [(name, "hbm", shape, BF) for name, shape in big_states]
        self.scratch = [
            ("wcat", (D, 4 * L), BF),
            ("f2", (L, HM), BF),
            ("wb", (HM, 2 * L), BF),
            ("ccb", (T, LANES), BF),
            ("oh2", (T, 2 * self.G8), BF),
            ("nm", (T, D), BF),
            ("qk", (2, T, L), BF),
            ("vv", (2, T, L), BF),
            ("qf", (T, HM), BF),
            ("kf", (T, HM), BF),
            ("ft", (HM, T), BF),
            ("tp", (n, PAD, LANES), F32),
            ("trb", (n, PAD, LANES), F32),
            ("tall", (n, PAD, LANES), F32),
            ("gtall", (n, PAD, LANES), F32),
            ("tot2", (2 * self.G8, HM), BF),
            ("acc", (HM, SEG * HD), F32),
            ("attf", (T, L), F32),
            ("inv", (T, L), F32),
            ("attb", (T, L), BF),
            ("arow", (nm, Tm, L), BF),
            ("wq_g", (nm, 3, D, L), BF),
            ("ow_g", (nm, L, D), BF),
            ("up_g", (nm, D, hidden), BF),
            ("ub_g", (nm, 1, hidden), F32),
            ("dn_g", (nm, hidden, D), BF),
            ("cotv", (Tm, D), BF),
            ("tokv", (Tm, D), BF),
            ("mid", (Tm, D), F32),
            ("nm2", (Tm, D), BF),
            ("act", (nm, Tm, hidden), BF),
            ("gp", (nm, Tm, hidden), BF),
            ("bo", (TILE, D), F32),
            ("gn2", (TILE, D), F32),
            ("gb", (Tm, D), BF),
            ("outv", (Tm, D), BF),
            ("small", (16, D), F32),
            ("small_m", (nm, 16, D), F32),
            ("small_d", (n, 8, D), F32),
            ("small_s", (8, D), F32),
            ("ends", (8, D), F32),
            ("last", (8, LANES), F32),
            ("last_m", (nm, 8, LANES), F32),
            ("last_d", (n, 8, LANES), F32),
            ("upp", (nm, D, hidden), BF),
            ("upc", (2, D, hidden), BF),
            ("upy", (n, self.ru, D), BF),
            ("upx", (n2, self.ru, D), BF),
            ("upz", (n2, self.ru, D), BF),
            ("dnp", (nm, self.rest, D), BF),
            ("dnc", (2, self.rest, D), BF),
            ("dny", (n, self.rd, D), BF),
            ("dnx", (n2, self.rd, D), BF),
            ("dnz", (n2, self.rd, D), BF),
            ("gar", (nm, Tm, L), BF),
            ("gad", (2, T, L), BF),
            ("gg", (2, T, L), BF),
            ("gd", (T, L), F32),
            ("grads", (3, T, L), BF),
            ("garr", (nm, 3, Tm, L), BF),
            ("kvp", (n, self.rk, L), BF),
            ("kvr", (n, self.rk, L), BF),
            ("kvl", (n, self.rk, L), BF),
        ]
        if self.big:
            self.scratch += [("stage_a", (2, HM, SEG * HD), BF), ("stage_b", (2, HM, SEG * HD), BF)]
        else:
            self.scratch += [(name, shape, BF) for name, shape in big_states]
            self.scratch += [("num", (T, LANES), F32), ("gkf", (T, self.M), F32)]
        self.sems = {
            **{name: n2 * self.H for name in ("rsx", "rsz", "agz", "agx", "gsx", "gsz", "ggz", "ggx")},
            **{name: n2 for name in ("rtx", "rtz", "atz", "atx", "gtx", "gtz", "hgz", "hgx")},
            **{name: nm * self.per for name in ("a2a", "gaa", "grk")},
            "grq": nm,
            "wy": 5,
            "wc": 10,
            "uc": 2,
            "uy": 1,
            "ux": n2,
            "uz": n2,
            "ugz": n2,
            "ugx": n2,
            "dc": 2,
            "dy": 1,
            "dx": n2,
            "dz": n2,
            "dgz": n2,
            "dgx": n2,
            "ks": n,
            "kg": n,
            "oy": 1,
            "oc": 2,
            "ty": self.per,
            "tc": 2 * self.per,
            "sm": nm,
            "sd": n,
            "lm": nm,
            "ld": n,
        }
        self.local_sems = 24

    def names(self):
        return (
            [x[0] for x in self.inputs]
            + [x[0] for x in self.outputs]
            + [x[0] for x in self.scratch]
            + [f"{k}_{end}" for k in self.sems for end in ("s", "r")]
            + ["lsem"]
        )


def layer_kernel(plan, *refs):
    r = SimpleNamespace(**dict(zip(plan.names(), refs, strict=True)))
    n, nm, T, D, L, M, HM, Tm, H = (
        plan.n,
        plan.nm,
        plan.T,
        plan.D,
        plan.L,
        plan.M,
        plan.HM,
        plan.Tm,
        plan.H,
    )
    hidden = plan.F
    n2 = n // 2
    tiles = T // TILE
    wide = TILE if plan.big else 2 * TILE
    me, m = lax.axis_index("dp"), lax.axis_index("mp")
    sib = m + 1 - 2 * lax.rem(m, 2)
    far = lax.rem(m + nm // 2, nm)
    farsib = lax.rem(sib + nm // 2, nm)
    xpart = me + 1 - 2 * lax.rem(me, 2)
    xme, zme = lax.rem(me, 2), me // 2

    def sem(name, index):
        return getattr(r, f"{name}_s").at[index], getattr(r, f"{name}_r").at[index]

    def copy(src, dst, name, sent, dp=None, mp=None, got=None):
        send, _ = sem(name, sent)
        _, recv = sem(name, sent if got is None else got)
        return pltpu.make_async_remote_copy(
            src_ref=src,
            dst_ref=dst,
            send_sem=send,
            recv_sem=recv,
            device_id=(me if dp is None else dp, m if mp is None else mp),
            device_id_type=MESH,
        )

    def local(src, dst, index):
        return pltpu.make_async_copy(src, dst, r.lsem.at[index])

    low = lane((1, LANES)) < HD

    barrier = pltpu.get_barrier_semaphore()

    def greet(k):
        pl.semaphore_signal(
            barrier, inc=1, device_id=(lax.rem(me + 1 + k, n), m), device_id_type=MESH
        )

    loop(n - 1, greet)
    for k in range(1, nm):
        pl.semaphore_signal(
            barrier, inc=1, device_id=(me, lax.rem(m + k, nm)), device_id_type=MESH
        )

    mine = rows_of(m, Tm)
    wides, len_shards = T // wide, 5

    def tok_in(i):
        rows = rows_of(i, wide)
        return local(r.tok.at[rows], r.nm.at[rows], 1 + len_shards + i)

    own_in = [local(r.cot.at[mine], r.cotv, 0), local(r.tok.at[mine], r.tokv, 1 + len_shards + wides)]
    for c in [tok_in(i) for i in range(wides)] + own_in:
        c.start()

    r.wcat[:, 0:L] = r.wqkv[0]
    r.wcat[:, L : 2 * L] = r.wqkv[1]
    wv = r.wqkv[2].astype(F32)
    wv_rolled = roll_half(wv)
    r.wcat[:, 2 * L : 3 * L] = jnp.where(low, wv, wv_rolled).astype(BF)
    r.wcat[:, 3 * L : 4 * L] = jnp.where(low, wv_rolled, wv).astype(BF)
    feature_rows = r.feat[STEP % FEATS]
    r.f2[...] = jnp.zeros((L, HM), BF)
    for h in range(H):
        r.f2[h * HD : (h + 1) * HD, h * M : (h + 1) * M] = feature_rows
    r.wb[:, 0:L] = r.f2[...].astype(F32).T.astype(BF)
    head_of_row = lax.broadcasted_iota(jnp.int32, (HM, L), 0) // M
    r.wb[:, L : 2 * L] = jnp.where(head_of_row == lane((HM, L)) // HD, 1.0, 0.0).astype(BF)

    count = T // LANES
    numbers = SEG * r.bkt[...].astype(F32) + r.cel[...].astype(F32)
    numbers = jnp.concatenate([numbers, jnp.zeros((LANES - count, LANES), F32)], 0).T
    for i in range(count):
        rows = pl.ds(i * LANES, LANES)
        column = jnp.broadcast_to(numbers[:, i : i + 1], (LANES, LANES))
        r.ccb[rows, :] = (column - jnp.where(low, 0.0, 1.0)).astype(BF)
        for block in range(2 * plan.G8 // LANES):
            place = (lane((1, LANES)) + block * LANES) % plan.G8
            number = place // PAD * SEG + place % SEG
            r.oh2[rows, block * LANES : (block + 1) * LANES] = jnp.where(
                column == number.astype(F32), 1.0, 0.0
            ).astype(BF)
    part_of_row = lax.broadcasted_iota(jnp.int32, (plan.G8, LANES), 0) % PAD // SEG

    def pack_totals(table):
        packed = jnp.zeros((plan.G8, LANES), F32)
        for q in range(HM // LANES):
            packed += jnp.where(part_of_row == q, table[:, q * LANES : (q + 1) * LANES], 0.0)
        return packed.reshape(n, PAD, LANES)

    def spread_totals(packed):
        packed = packed.reshape(plan.G8, LANES)
        return jnp.concatenate(
            [jnp.where(part_of_row == q, packed, 0.0) for q in range(HM // LANES)], 1
        )

    def phi(u):
        wide = u.astype(F32)
        squares = wide * wide
        first = jnp.sum(jnp.where(low, squares, 0.0), -1, keepdims=True)
        second = jnp.sum(jnp.where(low, 0.0, squares), -1, keepdims=True)
        projected = dot(u, r.f2[...]) * SCALE
        shift = jnp.where(lane((1, HM)) < M, first, second) * HALF_SQUARE
        return jnp.exp(projected - shift)

    pl.semaphore_wait(barrier, n - 1 + nm - 1)

    def project(i):
        rows = rows_of(i, wide)
        tok_in(i).wait()
        hat, _ = normalised(r.nm[rows, :].astype(F32))
        normed = (hat * r.g1[...] + r.b1[...]).astype(BF)
        r.nm[rows, :] = normed
        u = dot(normed, r.wcat[:, L:]).astype(BF)
        k = u[:, 0:L]
        r.qk[1, rows, :] = k
        r.vv[0, rows, :], r.vv[1, rows, :] = u[:, L : 2 * L], u[:, 2 * L : 3 * L]
        features = phi(k).astype(BF)
        r.kf[rows, :] = features
        r.ft[:, rows] = features.T

    def queries(i):
        rows = rows_of(i, wide)
        q = dot(r.nm[rows, :], r.wcat[:, 0:L]).astype(BF)
        r.qk[0, rows, :] = q
        r.qf[rows, :] = phi(q).astype(BF)

    shards = [
        (r.ow, r.ow_g),
        (r.up, r.up_g),
        (r.ub, r.ub_g),
        (r.dn, r.dn_g),
        (r.wqkv, r.wq_g),
    ]
    own_copies, y_copies, core_copies = [], [], []
    for i, (src, dst) in enumerate(shards):
        own_copies.append(local(src, dst.at[m], 1 + i))
        y_copies.append(copy(src, dst.at[m], "wy", i, mp=far))
        core_copies.append(copy(src, dst.at[m], "wc", 2 * i, mp=sib))
    for c in own_copies + y_copies + core_copies:
        c.start()
    lax.fori_loop(0, wides, lambda i, carry: (project(i), carry)[1], 0)

    def state_pair(ref, p, stage):
        if plan.big:
            pltpu.sync_copy(ref.at[pl.ds(2 * p, 2)], stage)
            return stage
        return ref.at[pl.ds(2 * p, 2)]

    def masked_pair(rows, dup, p):
        code = r.ccb[rows, :]
        first = jnp.full((1, LANES), 1.0, F32) * (4 * p)
        left = jnp.where(code == first.astype(BF), dup, jnp.zeros_like(dup))
        right = jnp.where(code == (first + 2.0).astype(BF), dup, jnp.zeros_like(dup))
        return jnp.concatenate([left, right], 1)

    everything = pl.ds(0, T)

    def head_rows(h):
        return pl.ds(h * M, M) if isinstance(h, int) else pl.ds(pl.multiple_of(h * M, M), M)

    def at_first(h, body):
        if isinstance(h, int):
            if h == 0:
                body()
        else:
            pl.when(h == 0)(body)

    class Pair:
        def __init__(self, h, state, totals):
            self.h, self.state, self.totals = h, state, totals

        def start(self):
            self.state.start()
            at_first(self.h, lambda: self.totals().start())

        def wait_recv(self):
            self.state.wait_recv()
            at_first(self.h, lambda: self.totals().wait_recv())

        def wait_send(self):
            self.state.wait_send()
            at_first(self.h, lambda: self.totals().wait_send())

    class States:
        def __init__(self, all_s, all_t, names):
            self.all_s, self.all_t = all_s, all_t
            self.x, self.tx, self.z, self.tz, self.gz, self.hz, self.gx, self.hx = names

        def both(self, h, state, totals):
            return Pair(h, state, totals)

        def to_x(self, p, h):
            j, hs = 2 * p + 1 - xme, head_rows(h)
            return self.both(
                h,
                copy(r.sp.at[j, hs], r.rb.at[p, hs], self.x, p * H + h, dp=xpart),
                lambda: copy(r.tp.at[j], r.trb.at[p], self.tx, p, dp=xpart),
            )

        def to_z(self, p, h):
            j, hs = 2 * p + xme, head_rows(h)
            return self.both(
                h,
                copy(
                    r.sp.at[j, hs],
                    r.rb.at[n2 + zme, hs],
                    self.z,
                    p * H + h,
                    dp=j,
                    got=zme * H + h,
                ),
                lambda: copy(r.tp.at[j], r.trb.at[n2 + zme], self.tz, p, dp=j, got=zme),
            )

        def from_z(self, p, h):
            j, hs = 2 * p + xme, head_rows(h)
            return self.both(
                h,
                copy(r.sp.at[j, hs], r.rb.at[n2 + p, hs], self.z, p * H + h, dp=j),
                lambda: copy(r.tp.at[j], r.trb.at[n2 + p], self.tz, p, dp=j),
            )

        def out_z(self, p, h):
            j, hs = 2 * p + xme, head_rows(h)
            s, t = self.all_s.at[me, hs], self.all_t.at[me]
            return self.both(
                h,
                copy(s, s, self.gz, p * H + h, dp=j, got=zme * H + h),
                lambda: copy(t, t, self.hz, p, dp=j, got=zme),
            )

        def in_z(self, p, h):
            j, hs = 2 * p + xme, head_rows(h)
            s, t = self.all_s.at[j, hs], self.all_t.at[j]
            return self.both(
                h,
                copy(s, s, self.gz, p * H + h, dp=j),
                lambda: copy(t, t, self.hz, p, dp=j),
            )

        def out_x(self, p, h, other=False):
            j, hs = 2 * p + (1 - xme if other else xme), head_rows(h)
            s, t = self.all_s.at[j, hs], self.all_t.at[j]
            return self.both(
                h,
                copy(s, s, self.gx, p * H + h, dp=xpart),
                lambda: copy(t, t, self.hx, p, dp=xpart),
            )

        def start(self, dup):
            def pair(q, carry):
                h, p = q // n2, lax.rem(zme + 1 + lax.rem(q, n2), n2)
                block = dot(r.ft[head_rows(h), :], masked_pair(everything, dup[h], p))
                put_state(r.sp, 2 * p, h, block[:, :LANES].astype(BF))
                put_state(r.sp, 2 * p + 1, h, block[:, LANES:].astype(BF))
                self.to_x(p, h).start()
                return carry

            lax.fori_loop(0, H * n2, pair, 0)

        def add_x(self, p, h):
            self.to_x(p, h).wait_recv()
            j = 2 * p + xme

            def totals():
                r.tp[j] += r.trb[p]

            at_first(h, totals)
            return get_state(r.sp, j, h) + get_state(r.rb, p, h)

        def near(self, h, k):
            p = lax.rem(zme + 1 + k, n2)
            put_state(r.sp, 2 * p + xme, h, self.add_x(p, h).astype(BF))
            self.to_z(p, h).start()

        def own(self, h):
            r.acc[head_rows(h), :] = self.add_x(zme, h)

        def whole(self, h):
            def take(k):
                p = lax.rem(zme + 1 + k, n2)
                self.from_z(p, h).wait_recv()
                r.acc[head_rows(h), :] += get_state(r.rb, n2 + p, h)
                if h == 0:
                    r.tp[me] += r.trb[n2 + p]

            loop(n2 - 1, take)
            if h == 0:
                self.all_t[me] = r.tp[me]
            put_state(self.all_s, me, h, r.acc[head_rows(h), :].astype(BF))

            def send(k):
                self.out_z(lax.rem(zme + 1 + k, n2), h).start()

            loop(n2 - 1, send)
            self.out_x(zme, h).start()

        def onward(self, h, k):
            p = lax.rem(zme + 1 + k, n2)
            self.in_z(p, h).wait_recv()
            self.out_x(p, h).start()

        def arrived(self, p, h):
            self.out_x(p, h, other=True).wait_recv()

        def run(self, work, rest, use, midway):
            others = n2 - 1
            steps = H * others

            def step(q, carry):
                h, k = q // others, lax.rem(q, others)
                pl.when(q == steps - 1)(lambda: self.whole(0))
                self.near(h, k)
                work(q)
                pl.when(k == others - 1)(lambda: self.own(h))
                return carry

            lax.fori_loop(0, steps, step, 0)
            rest()
            self.whole(H - 1)
            loop(others, lambda k: self.onward(0, k))
            for h in range(H):
                loop(n2, lambda p, h=h: self.arrived(p, h))
                if h < H - 1:
                    loop(others, lambda k, h=h: self.onward(h + 1, k))
                    use(h)
                    midway()
            for h in range(H):

                def sent(p, h=h):
                    self.to_x(p, h).wait_send()
                    self.out_x(p, h).wait_send()

                loop(n2, sent)

                def sent_z(k, h=h):
                    p = lax.rem(zme + 1 + k, n2)
                    self.to_z(p, h).wait_send()
                    self.out_z(p, h).wait_send()

                loop(others, sent_z)
            total = spread_totals(self.all_t[...])
            top = total.astype(BF)
            r.tot2[0 : plan.G8, :] = top
            r.tot2[plan.G8 :, :] = (total - top.astype(F32)).astype(BF)

    def put_state(ref, j, h, values):
        if plan.big:
            spot = r.stage_b.at[0, head_rows(h)]
            spot[...] = values
            pltpu.sync_copy(spot, ref.at[j, head_rows(h)])
        else:
            ref[j, head_rows(h), :] = values

    def get_state(ref, j, h):
        if plan.big:
            spot = r.stage_b.at[1, head_rows(h)]
            pltpu.sync_copy(ref.at[j, head_rows(h)], spot)
            return spot[...].astype(F32)
        return ref[j, head_rows(h), :].astype(F32)

    def state_columns(ref, p, h):
        blocks = state_pair(ref, p, r.stage_a if plan.big else None)
        return jnp.concatenate([blocks[0, head_rows(h), :], blocks[1, head_rows(h), :]], 1)

    def pick(code, product, p, rest):
        first = jnp.full((1, LANES), 1.0, F32) * (4 * p)
        rest = jnp.where(code == first, product[:, :LANES], rest)
        return jnp.where(code == first + 2.0, product[:, LANES:], rest)

    def times_state(rows, left, all_s, h):
        code, features = r.ccb[rows, :].astype(F32), left[rows, head_rows(h)]

        def pair(p, total):
            return pick(code, dot(features, state_columns(all_s, p, h)), p, total)

        total = jnp.zeros((rows.size, LANES), F32)
        if plan.big:
            return lax.fori_loop(0, n2, pair, total)
        for p in range(n2):
            total = pair(p, total)
        return total

    def own_state(rows, left, all_s):
        ready = [] if plan.big else [r.num[rows, :]]
        heads = ready + [times_state(rows, left, all_s, h) for h in range(len(ready), H)]
        return halves(*(head + roll_half(head) for head in heads))

    def halves(first, second):
        return jnp.where(low, first, second)

    def early(left, all_s):
        def run(h):
            if plan.big:
                return

            def tile(i, carry):
                rows = rows_of(i, wide)
                r.num[rows, :] = times_state(rows, left, all_s, h)
                return carry

            lax.fori_loop(0, wides, tile, 0)

        return run

    first = States(
        r.sall, r.tall, ("rsx", "rtx", "rsz", "rtz", "agz", "atz", "agx", "atx")
    )
    r.tp[...] = pack_totals(dot_tn(r.oh2[:, : plan.G8], r.kf[...]))
    first.start(r.vv)

    onward = []

    def weights_on(which):
        for i in which:
            dst = shards[i][1]
            copy(dst.at[far], dst.at[far], "wy", i, mp=far).wait_recv()
            c = copy(dst.at[far], dst.at[far], "wc", 2 * i + 1, mp=sib)
            c.start()
            onward.append(c)

    def turn(source):
        def tile(i):
            rows = rows_of(i, TILE)
            r.ft[:, rows] = source[rows, :].T

        return lambda: loop(tiles, tile)

    def in_quarters(body, size):
        quarter = T // size // 4

        def work(q):
            def tile(i, carry):
                body(q * quarter + i)
                return carry

            pl.when(q < 4)(lambda: (lax.fori_loop(0, quarter, tile, 0), None)[1])

        return work

    first.run(
        in_quarters(queries, wide),
        turn(r.qf),
        early(r.qf, r.sall),
        lambda: weights_on(range(4)),
    )

    def own_totals(rows):
        return dot(r.oh2[rows, :], r.tot2[...])

    def attend(i):
        rows = rows_of(i, TILE)
        numerator = own_state(rows, r.qf, r.sall)
        product = r.qf[rows, :].astype(F32) * own_totals(rows)
        denominator = halves(
            jnp.sum(product[:, :M], -1, keepdims=True),
            jnp.sum(product[:, M:], -1, keepdims=True),
        )
        inverse = 1.0 / denominator
        attention = numerator / denominator
        r.attf[rows, :] = attention
        r.inv[rows, :] = inverse
        r.attb[rows, :] = attention.astype(BF)

    per = plan.per
    chunk_order = [far, farsib, sib, m]
    others_mp = chunk_order[: nm - 1]

    def swap(src, dst, name, target, i):
        return copy(src, dst, name, target * per + i, mp=target, got=m * per + i)

    def swapped(dst, name, source, i):
        return copy(dst, dst, name, source * per + i, mp=source)

    def attention_copy(target, i):
        return swap(
            r.attb.at[rows_of(target * per + i, TILE)],
            r.arow.at[m, rows_of(i, TILE)],
            "a2a",
            target,
            i,
        )

    def each_tile(body, after, middle=None):
        def step(q, carry):
            i, k = q // nm, lax.rem(q, nm)
            start = lax.rem(m + (1 - k // 2) * (nm // 2), nm)
            target = start + lax.rem((k + 1) // 2, 2) * (1 - 2 * lax.rem(start, 2))
            body(target * per + i)
            pl.when(k < nm - 1)(lambda: after(target, i).start())
            return carry

        half = per // 2 * nm
        lax.fori_loop(0, half, step, 0)
        if middle is not None:
            middle()
        lax.fori_loop(half, per * nm, step, 0)

    each_tile(attend, attention_copy)
    r.arow[m] = r.attb[rows_of(m, Tm), :]

    def weights_wait(which):
        for i in which:
            dst = shards[i][1]
            own_copies[i].wait()
            copy(dst.at[sib], dst.at[sib], "wc", 2 * i, mp=sib).wait_recv()
            copy(dst.at[farsib], dst.at[farsib], "wc", 2 * i + 1, mp=sib).wait_recv()
            for c in (y_copies[i], core_copies[i], onward[i]):
                c.wait_send()

    weights_wait(range(4))
    for c in own_in:
        c.wait()

    r.small[...] = jnp.zeros((16, D), F32)

    beside = 1 if plan.big else 2

    def units(rows, group):
        both = [beside * group + i for i in range(beside)]
        normed, cotangent = r.nm2[rows, :], r.cotv[rows, :]
        preacts = [dot(normed, r.up_g[s]) + r.ub_g[s] for s in both]
        backs = [dot_nt(cotangent, r.dn_g[s]) for s in both]
        forward, backward = r.bo[...], r.gn2[...]
        for s, preact, back in zip(both, preacts, backs, strict=True):
            spread = 0.5 + 0.5 * lax.erf(preact * (0.5**0.5))
            active = (preact * spread).astype(BF)
            r.act[s, rows, :] = active
            slope = spread + preact * jnp.exp(preact * preact * -0.5) * 0.3989422804014327
            grad = (back * slope).astype(BF)
            r.gp[s, rows, :] = grad
            forward += dot(active, r.dn_g[s])
            backward += dot_nt(grad, r.up_g[s])
            r.small[pl.ds(8 + s, 1), :] += jnp.sum(grad.astype(F32), 0, keepdims=True)
        r.bo[...] = forward
        r.gn2[...] = backward

    gas = r.attb.reshape(nm, Tm, L)

    def grad_copy(target, i):
        rows = rows_of(i, TILE)
        return swap(gas.at[target, rows], r.gar.at[m, rows], "gaa", target, i)

    def middle_rows(i):
        rows = rows_of(i, TILE)
        for target in others_mp:
            swapped(r.arow.at[target, rows], "a2a", target, i).wait_recv()
            attention_copy(target, i).wait_send()
        columns = jnp.concatenate([r.arow[s, rows, :] for s in range(nm)], 1)
        branch = dot(columns, r.ow_g[...].reshape(D, D)).astype(BF).astype(F32)
        middle = r.tokv[rows, :].astype(F32) + branch + r.ob[...]
        hat, scale = normalised(middle)
        normed = hat * r.g2[...] + r.b2[...]
        r.mid[rows, :] = middle
        r.nm2[rows, :] = normed.astype(BF)
        r.bo[...] = jnp.zeros((TILE, D), F32)
        r.gn2[...] = jnp.zeros((TILE, D), F32)
        lax.fori_loop(0, nm // beside, lambda s, carry: (units(rows, s), carry)[1], 0)
        middle = r.mid[rows, :]
        r.outv[rows, :] = (middle + r.bo[...] + r.db[...]).astype(BF)
        hat, scale = normalised(middle)
        upstream = r.gn2[...]
        cotangent = r.cotv[rows, :].astype(F32)
        grad = cotangent + norm_back(upstream, hat, scale, r.g2[...])
        low_grad = grad.astype(BF)
        back = dot_nt(low_grad, r.ow_g[...].reshape(D, D)).astype(BF)
        for s in range(nm):
            gas[s, rows, :] = back[:, s * L : (s + 1) * L]
        for target in others_mp:
            grad_copy(target, i).start()
        r.mid[rows, :] = grad
        r.gb[rows, :] = low_grad
        r.small[0:1, :] += jnp.sum(cotangent, 0, keepdims=True)
        r.small[1:2, :] += jnp.sum(upstream * hat, 0, keepdims=True)
        r.small[2:3, :] += jnp.sum(upstream, 0, keepdims=True)
        r.small[3:4, :] += jnp.sum(grad, 0, keepdims=True)

    lax.fori_loop(0, per, lambda i, carry: (middle_rows(i), carry)[1], 0)
    r.gar[m] = gas[m]

    up_core = [
        copy(r.upp.at[sib], r.upc.at[0], "uc", 0, mp=sib),
        copy(r.upp.at[farsib], r.upc.at[1], "uc", 1, mp=sib),
    ]
    dn_core = [
        copy(r.dnp.at[sib], r.dnc.at[0], "dc", 0, mp=sib),
        copy(r.dnp.at[farsib], r.dnc.at[1], "dc", 1, mp=sib),
    ]

    def up_part(s):
        r.upp[s] = dot_tn(r.nm2[...], r.gp[s]).astype(BF)

    def down_part(s):
        r.dnp[s, 0:hidden, :] = dot_tn(r.act[s], r.cotv[...]).astype(BF)
        r.dnp[s, hidden : hidden + L, :] = dot_tn(r.arow[s], r.gb[...]).astype(BF)

    lax.fori_loop(0, nm, lambda s, carry: (up_part(s), carry)[1], 0)
    for c in up_core:
        c.start()
    lax.fori_loop(0, nm, lambda s, carry: (down_part(s), carry)[1], 0)
    for c in dn_core:
        c.start()

    def flat_rows(ref):
        return ref.reshape(ref.shape[0] * ref.shape[1], ref.shape[2])

    def core_sum(copies, part, other, y, name):
        for c in copies:
            c.wait()
        rows = part.shape[1]

        def add(i):
            strip = rows_of(i, LANES)
            part[far, strip, :] = (
                part[far, strip, :].astype(F32) + other[1, strip, :].astype(F32)
            ).astype(BF)

        loop(rows // LANES, add)
        return copy(part.at[far], flat_rows(y).at[pl.ds(0, rows)], name, 0, mp=far)

    def y_sum(sent, part, other, y):
        sent.wait()
        flat = flat_rows(y)

        def add(i):
            strip = rows_of(i, LANES)
            flat[strip, :] = (
                part[m, strip, :].astype(F32)
                + other[0, strip, :].astype(F32)
                + flat[strip, :].astype(F32)
            ).astype(BF)

        loop(part.shape[1] // LANES, add)

    class Reduction:
        def __init__(self, source, rx, rz, out, names):
            self.source, self.rx, self.rz, self.out = source, rx, rz, out
            self.x, self.z, self.gz, self.gx = names

        def block(self, k):
            return self.source.at[xme * n2 + k]

        def to_x(self, k):
            return copy(self.source.at[(1 - xme) * n2 + k], self.rx.at[k], self.x, k, dp=xpart)

        def start(self):
            loop(n2, lambda k: self.to_x(lax.rem(zme + 1 + k, n2)).start())

        def scatter(self):
            def add(k):
                self.to_x(k).wait()
                ref = self.block(k)
                ref[...] = (ref[...].astype(F32) + self.rx[k].astype(F32)).astype(BF)

            def send(k):
                z = lax.rem(zme + 1 + k, n2)
                add(z)
                copy(self.block(z), self.rz.at[zme], self.z, z, dp=2 * z + xme, got=zme).start()

            loop(n2 - 1, send)
            add(zme)

        def gather(self):
            own = self.block(zme)

            def take(k, total):
                z = lax.rem(zme + 1 + k, n2)
                copy(self.block(z), self.rz.at[z], self.z, z, dp=2 * z + xme).wait()
                return total + self.rz[z].astype(F32)

            total = own[...].astype(F32)
            if n2 <= 4:
                for k in range(n2 - 1):
                    total = take(k, total)
            else:
                total = lax.fori_loop(0, n2 - 1, take, total)
            own[...] = total.astype(BF)
            self.place(xme * n2 + zme, 1)[...] = own[...]
            spot = self.place(xme * n2 + zme, 1)

            def send(k):
                z = lax.rem(zme + 1 + k, n2)
                copy(own, spot, self.gz, z, dp=2 * z + xme, got=zme).start()

            loop(n2 - 1, send)
            self.over_x(zme).start()

        def over_x(self, z, side=None):
            spot = self.place((xme if side is None else side) * n2 + z, 1)
            return copy(spot, spot, self.gx, z, dp=xpart)

        def spread(self):
            own = self.block(zme)

            def onward(k):
                z = lax.rem(zme + 1 + k, n2)
                copy(own, self.place(xme * n2 + z, 1), self.gz, z, dp=2 * z + xme).wait()
                self.over_x(z).start()

            loop(n2 - 1, onward)

        def finish(self):
            def wait(z):
                self.over_x(z, 1 - xme).wait_recv()
                self.over_x(z).wait_send()

            loop(n2, wait)

        def place(self, index, count):
            rows = self.source.shape[1]
            return self.out.at[pl.ds(pl.multiple_of(index * rows, rows), count * rows)]

    up = Reduction(r.upy, r.upx, r.upz, flat_rows(r.upc), ("ux", "uz", "ugz", "ugx"))
    dn = Reduction(r.dny, r.dnx, r.dnz, flat_rows(r.dnc), ("dx", "dz", "dgz", "dgx"))

    class Sums:
        def __init__(self, own, over_m, names):
            self.own, self.over_m, self.names = own, over_m, names

        def start(self):
            for target in others_mp:
                copy(
                    self.own, self.over_m.at[m], self.names[0], target, mp=target, got=m
                ).start()

        def scatter(self, send, over_d, keep):
            total = self.own[...]
            for target in others_mp:
                copy(self.own, self.over_m.at[target], self.names[0], target, mp=target).wait()
                total += self.over_m[target]
            self.send, self.over_d = send, over_d
            self.send[...] = keep(total)

            def go(k):
                j = lax.rem(me + 1 + k, n)
                copy(self.send, over_d.at[me], self.names[1], j, dp=j, got=me).start()

            loop(n - 1, go)

        def gather(self):
            self.total = self.send[...]

            def take(k, total):
                j = lax.rem(me + 1 + k, n)
                copy(self.send, self.over_d.at[j], self.names[1], j, dp=j).wait()
                return total + self.over_d[j]

            return lax.fori_loop(0, n - 1, take, self.send[...])

    small = Sums(r.small, r.small_m, ("sm", "sd"))
    last = Sums(r.last, r.last_m, ("lm", "ld"))
    small.start()
    weights_on([4])
    for i in range(per):
        for target in others_mp:
            swapped(r.gar.at[target, rows_of(i, TILE)], "gaa", target, i).wait_recv()
    up_y = core_sum(up_core, r.upp, r.upc, r.upy, "uy")
    up_y.start()

    def grad_rows(i):
        rows = rows_of(i, wide)
        s = i // (Tm // wide)
        inner = rows_of(i - s * (Tm // wide), wide)
        grad = r.gar[s, inner, :].astype(F32)
        inv = r.inv[rows, :]
        scaled = grad * inv
        g_roll, s_roll = roll_half(grad), roll_half(scaled)
        r.gad[0, rows, :] = halves(grad, g_roll).astype(BF)
        r.gad[1, rows, :] = halves(g_roll, grad).astype(BF)
        r.gg[0, rows, :] = halves(scaled, s_roll).astype(BF)
        r.gg[1, rows, :] = halves(s_roll, scaled).astype(BF)
        product = scaled * r.attf[rows, :]
        r.gd[rows, :] = -halves(
            jnp.sum(jnp.where(low, product, 0.0), -1, keepdims=True),
            jnp.sum(jnp.where(low, 0.0, product), -1, keepdims=True),
        )

    lax.fori_loop(0, wides, lambda i, carry: (grad_rows(i), carry)[1], 0)

    def head_column(values, h):
        return values[:, h * HD : h * HD + 1]

    head_totals = []
    for h in range(H):
        column = r.gd[:, h * HD : h * HD + 1]
        top = column.astype(BF).astype(F32)
        upper = lane((1, 2 * plan.G8)) < plan.G8
        weights = r.oh2[...] * jnp.where(upper, top, column - top).astype(BF)
        summed = dot_tn(weights, r.qf[:, h * M : (h + 1) * M])
        head_totals.append(summed[: plan.G8] + summed[plan.G8 :])
    r.tp[...] = pack_totals(jnp.concatenate(head_totals, 1))
    dn_y = core_sum(dn_core, r.dnp, r.dnc, r.dny, "dy")
    dn_y.start()
    second = States(
        r.gall, r.gtall, ("gsx", "gtx", "gsz", "gtz", "ggz", "hgz", "ggx", "hgx")
    )
    second.start(r.gg)

    def contract(rows, dup, all_s, h):
        def pair(p, total):
            return total + dot_nt(masked_pair(rows, dup[h, rows, :], p), state_columns(all_s, p, h))

        total = jnp.zeros((rows.size, M), F32)
        if plan.big:
            return lax.fori_loop(0, n2, pair, total)
        for p in range(n2):
            total = pair(p, total)
        return total

    def early_keys(h):
        if plan.big:
            return

        def tile(i, carry):
            rows = rows_of(i, wide)
            r.gkf[rows, :] = contract(rows, r.vv, r.gall, h)
            return carry

        lax.fori_loop(0, wides, tile, 0)
        early(r.kf, r.gall)(h)

    def feature_back(rows, which, grad_features):
        u = r.qk[which, rows, :]
        weighted = (grad_features * phi(u)).astype(BF)
        both = dot(weighted, r.wb[...])
        return (
            both[:, :L] * SCALE - both[:, L:] * u.astype(F32) * (SCALE * SCALE)
        ).astype(BF)

    def query_back(i):
        rows = rows_of(i, wide)
        totals = own_totals(rows)
        inv, gd = r.inv[rows, :], r.gd[rows, :]
        parts = [
            contract(rows, r.gad, r.sall, h) * head_column(inv, h)
            + totals[:, h * M : (h + 1) * M] * head_column(gd, h)
            for h in range(H)
        ]
        r.grads[0, rows, :] = feature_back(rows, 0, jnp.concatenate(parts, 1))

    def own_unit_sums(total):
        rows = lax.broadcasted_iota(jnp.int32, (16, 1), 0)
        units_row = jnp.sum(jnp.where(rows == 8 + m, total, 0.0), 0, keepdims=True)
        return jnp.concatenate([total[0:4], units_row, jnp.zeros((3, D), F32)], 0)

    def small_scatter():
        small.scatter(r.small_s, r.small_d, own_unit_sums)

    def send_query_grads():
        for target in others_mp:
            copy(
                r.grads.at[0, rows_of(target, Tm)], r.garr.at[m, 0], "grq", target, mp=target, got=m
            ).start()

    def query_projection():
        part = dot(r.ft[...], r.grads[0]).astype(BF)
        flat = flat_rows(r.dny)
        for c in range(D // L):
            flat[plan.rest : plan.tail, c * L : (c + 1) * L] = part[c * L : (c + 1) * L, :]

    gtv = r.nm2
    out_land, tok_land = flat_rows(r.dn_g), flat_rows(r.up_g)
    out_y = copy(r.outv, out_land.at[mine], "oy", 0, mp=far)
    out_core = copy(r.outv, out_land.at[mine], "oc", 0, mp=sib)

    def start_up():
        y_sum(up_y, r.upp, r.upc, r.upy)
        up.start()

    def midway():
        y_sum(dn_y, r.dnp, r.dnc, r.dny)
        dn.start()
        out_y.start()
        out_core.start()
        up.scatter()

    def after_queries():
        send_query_grads()
        turn(r.nm)()
        query_projection()
        start_up()
        small_scatter()

    second.run(in_quarters(query_back, wide), after_queries, early_keys, midway)

    def key_back(i):
        rows = rows_of(i, TILE)
        totals = own_totals(rows)
        ready = [] if plan.big else [r.gkf[rows, :]]
        parts = ready + [contract(rows, r.vv, r.gall, h) for h in range(len(ready), H)]
        gkf = jnp.concatenate(parts, 1)
        r.grads[1, rows, :] = feature_back(rows, 1, gkf + totals)
        r.grads[2, rows, :] = own_state(rows, r.kf, r.gall).astype(BF)

    both = pl.ds(1, 2)

    def key_copy(target, i):
        return swap(
            r.grads.at[both, rows_of(target * per + i, TILE)],
            r.garr.at[m, both, rows_of(i, TILE)],
            "grk",
            target,
            i,
        )

    def between_halves():
        up.gather()
        dn.scatter()
        out_land[mine, :] = r.outv[...]

    each_tile(key_back, key_copy, between_halves)
    for a in range(3):
        r.garr[m, a] = r.grads[a, rows_of(m, Tm), :]

    part = dot(r.ft[...], jnp.concatenate([r.grads[1], r.grads[2]], 1)).astype(BF)
    flat = flat_rows(r.kvp)
    flat[0:D, :] = part[:, :L]
    flat[D : 2 * D, :] = part[:, L:]

    def kv_send(k):
        j = lax.rem(me + 1 + k, n)
        copy(r.kvp.at[j], r.kvr.at[me], "ks", j, dp=j, got=me).start()

    loop(n - 1, kv_send)

    out_far = out_land.at[rows_of(far, Tm)]
    copy(out_far, out_far, "oy", 0, mp=far).wait_recv()
    out_on = copy(out_far, out_far, "oc", 1, mp=sib)
    out_on.start()

    for target in others_mp:
        copy(r.garr.at[target, 0], r.garr.at[target, 0], "grq", target, mp=target).wait_recv()
    weights_wait([4])
    r.ends[...] = jnp.zeros((8, D), F32)

    quarters = D // LANES

    def send_ends():
        for row in range(2):
            for q in range(quarters):
                spot = row * quarters + q
                r.last[spot : spot + 1, :] = r.ends[row : row + 1, q * LANES : (q + 1) * LANES]
        last.start()

    def norm1_back(i):
        rows = rows_of(i, TILE)
        for target in others_mp:
            swapped(r.garr.at[target, both, rows], "grk", target, i).wait_recv()
        upstream = jnp.zeros((TILE, D), F32)
        for s in range(nm):
            left = jnp.concatenate([r.garr[s, a, rows, :] for a in range(3)], 1)
            right = jnp.concatenate([r.wq_g[s, a] for a in range(3)], 1)
            upstream += dot_nt(left, right)
        upstream = upstream.astype(BF).astype(F32)
        hat, scale = normalised(r.tokv[rows, :].astype(F32))
        gtv[rows, :] = (r.mid[rows, :] + norm_back(upstream, hat, scale, r.g1[...])).astype(BF)
        r.ends[0:1, :] += jnp.sum(upstream * hat, 0, keepdims=True)
        r.ends[1:2, :] += jnp.sum(upstream, 0, keepdims=True)
        pl.when(i == per - 1)(send_ends)
        for c in tok_copies(i):
            c.start()

        @pl.when(i == 0)
        def _():
            dn.gather()
            up.spread()

    def tok_copies(i):
        rows = rows_of(i, TILE)
        spot = tok_land.at[rows_of(m * per + i, TILE)]
        return (
            copy(gtv.at[rows], spot, "ty", i, mp=far),
            copy(gtv.at[rows], spot, "tc", 2 * i, mp=sib),
        )

    lax.fori_loop(0, per, lambda i, carry: (norm1_back(i), carry)[1], 0)
    tok_land[mine, :] = gtv[...]

    def kv_sum():
        total = r.kvp[me].astype(F32)

        def take(k, total):
            j = lax.rem(me + 1 + k, n)
            copy(r.kvp.at[j], r.kvr.at[j], "ks", j, dp=j).wait()
            return total + r.kvr[j].astype(F32)

        r.kvp[me] = lax.fori_loop(0, n - 1, take, total).astype(BF)

    kv_sum()
    last.scatter(r.last, r.last_d, lambda total: total)
    kv_spot = r.kvl.at[me]
    r.kvl[me] = r.kvp[me]

    def kv_spread(k):
        j = lax.rem(me + 1 + k, n)
        copy(r.kvp.at[me], kv_spot, "kg", j, dp=j, got=me).start()

    loop(n - 1, kv_spread)
    dn.spread()
    tok_on = []

    def tok_forward(i):
        spot = tok_land.at[rows_of(far * per + i, TILE)]
        copy(spot, spot, "ty", i, mp=far).wait_recv()
        c = copy(spot, spot, "tc", 2 * i + 1, mp=sib)
        c.start()
        tok_on.append(c)

    sums = small.gather()
    ends = last.gather()
    r.small_o[0:4, :] = sums[0:4]
    for row in range(2):
        for q in range(quarters):
            spot = row * quarters + q
            r.small_o[4 + row : 5 + row, q * LANES : (q + 1) * LANES] = ends[spot : spot + 1]
    r.small_o[6:7, :] = sums[4:5]

    written = []

    def write(src, dst):
        c = local(src, dst, len(written))
        c.start()
        written.append(c)

    def kv_wait(k):
        j = lax.rem(me + 1 + k, n)
        copy(r.kvp.at[me], r.kvl.at[j], "kg", j, dp=j).wait()

    for index, owner in enumerate((sib, farsib)):
        spot = out_land.at[rows_of(owner, Tm)]
        copy(spot, spot, "oc", index, mp=sib).wait_recv()
    write(out_land, r.out_o)
    for i in range(per):
        tok_forward(i)
    up.finish()
    write(up.out.at[pl.ds(0, D)], r.upg_o)
    loop(n - 1, kv_wait)
    write(flat_rows(r.kvl).at[pl.ds(0, 2 * D)], r.kvg_o)
    for i in range(per):
        for index, owner in enumerate((sib, farsib)):
            spot = tok_land.at[rows_of(owner * per + i, TILE)]
            copy(spot, spot, "tc", 2 * i + index, mp=sib).wait_recv()
    write(tok_land, r.gtok_o)
    dn.finish()
    write(dn.out.at[pl.ds(0, plan.tail)], r.dng_o)
    for i in range(per):
        for c in tok_copies(i):
            c.wait_send()
    for c in (out_y, out_core, out_on, *tok_on):
        c.wait_send()
    for c in written:
        c.wait()
    for target in others_mp:
        for i in range(per):
            for c in (grad_copy(target, i), key_copy(target, i)):
                c.wait_send()
        copy(r.grads.at[0, rows_of(target, Tm)], r.garr.at[m, 0], "grq", target, mp=target).wait_send()


def widen_kernel(plan, *refs):
    (output, tokens, up, down, kv, small), refs = refs[:6], refs[6:]
    (out_o, tok_o, qkv_o, ow_o, ob_o, g1_o, b1_o, g2_o, b2_o, up_o, ub_o, dn_o, db_o), refs = (
        refs[:13],
        refs[13:],
    )
    tok_v, out_v, up_v, dn_v, kv_v, tok_w, up_w, dn_w, ow_w, qkv_w, sem_in, sem_out = refs
    D, L, hidden, T = plan.D, plan.L, plan.F, plan.T
    pieces = 8
    size = T // pieces
    reads = [
        pltpu.make_async_copy(a, b, sem_in.at[i])
        for i, (a, b) in enumerate([(up, up_v), (down, dn_v), (kv, kv_v), (output, out_v)])
    ]
    token_reads = [
        pltpu.make_async_copy(
            tokens.at[pl.ds(i * size, size)], tok_v.at[pl.ds(i * size, size)], sem_in.at[4 + i]
        )
        for i in range(pieces)
    ]
    for c in token_reads + reads:
        c.start()
    for row, ref in ((3, ob_o), (4, g1_o), (5, b1_o), (1, g2_o), (2, b2_o), (6, ub_o), (0, db_o)):
        ref[...] = small[row : row + 1, :]
    writes = []

    def send(src, dst):
        c = pltpu.make_async_copy(src, dst, sem_out.at[len(writes)])
        c.start()
        writes.append(c)

    for i in range(pieces):
        token_reads[i].wait()
        if i == 1:
            reads[3].wait()
            for part in range(2):
                through = pl.ds(part * (T // 2), T // 2)
                send(out_v.at[through], out_o.at[through])
        rows = pl.ds(i * size, size)
        tok_w[rows, :] = tok_v[rows, :].astype(F32)
        send(tok_w.at[rows], tok_o.at[rows])
    for c in reads[:3]:
        c.wait()
    up_w[...] = up_v[...].astype(F32)
    send(up_w, up_o)
    dn_w[...] = dn_v[0:hidden, :].astype(F32)
    send(dn_w, dn_o)
    ow_w[...] = dn_v[hidden : hidden + L, :].astype(F32)
    send(ow_w, ow_o)
    for c in range(D // L):
        qkv_w[0, c * L : (c + 1) * L, :] = dn_v[
            plan.rest : plan.tail, c * L : (c + 1) * L
        ].astype(F32)
    qkv_w[1] = kv_v[0:D, :].astype(F32)
    qkv_w[2] = kv_v[D : 2 * D, :].astype(F32)
    send(qkv_w, qkv_o)
    for c in writes:
        c.wait()


def widen(plan, *gathered):
    D, L, hidden, T = plan.D, plan.L, plan.F, plan.T
    line = ("vmem", (1, D))
    outs = [
        ("hbm", (T, D)),
        ("hbm", (T, D)),
        ("hbm", (3, D, L)),
        ("hbm", (L, D)),
        *[line] * 5,
        ("hbm", (D, hidden)),
        ("vmem", (1, hidden)),
        ("hbm", (hidden, D)),
        line,
    ]
    spaces = {"vmem": pltpu.VMEM, "hbm": pl.ANY}
    results = pl.pallas_call(
        functools.partial(widen_kernel, plan),
        out_shape=[
            jax.ShapeDtypeStruct(shape, BF if i == 0 else F32) for i, (_, shape) in enumerate(outs)
        ],
        in_specs=[pl.BlockSpec(memory_space=pl.ANY)] * 5 + [pl.BlockSpec(memory_space=pltpu.VMEM)],
        out_specs=[pl.BlockSpec(memory_space=spaces[kind]) for kind, _ in outs],
        scratch_shapes=[
            pltpu.VMEM((T, D), BF),
            pltpu.VMEM((T, D), BF),
            pltpu.VMEM((D, hidden), BF),
            pltpu.VMEM((plan.tail, D), BF),
            pltpu.VMEM((2 * D, L), BF),
            pltpu.VMEM((T, D), F32),
            pltpu.VMEM((D, hidden), F32),
            pltpu.VMEM((hidden, D), F32),
            pltpu.VMEM((L, D), F32),
            pltpu.VMEM((3, D, L), F32),
            pltpu.SemaphoreType.DMA((16,)),
            pltpu.SemaphoreType.DMA((24,)),
        ],
        compiler_params=pltpu.CompilerParams(vmem_limit_bytes=60 << 20),
        name="widen",
    )(*gathered)
    return tuple(v.reshape(-1) if v.shape[0] == 1 else v for v in results)


def per_device(
    n,
    nm,
    tokens,
    cotangent,
    bucket,
    cell,
    features,
    qkv_weight,
    out_weight,
    out_bias,
    norm1_gain,
    norm1_bias,
    norm2_gain,
    norm2_bias,
    up_weight,
    up_bias,
    down_weight,
    down_bias,
):
    count, width = tokens.shape
    local, hidden = qkv_weight.shape[2], up_weight.shape[1]
    plan = Plan(n, nm, count, width, local, features.shape[2], hidden)
    spaces = {"vmem": pltpu.VMEM, "hbm": pl.ANY}
    line = lambda v: v.reshape(1, -1)
    grid_ids = (count // LANES, LANES)
    outs = pl.pallas_call(
        functools.partial(layer_kernel, plan),
        out_shape=[jax.ShapeDtypeStruct(s, d) for _, _, s, d in plan.outputs],
        in_specs=[pl.BlockSpec(memory_space=spaces[k]) for _, k in plan.inputs],
        out_specs=[pl.BlockSpec(memory_space=spaces[k]) for _, k, _, _ in plan.outputs],
        scratch_shapes=[pltpu.VMEM(s, d) for _, s, d in plan.scratch]
        + [pltpu.SemaphoreType.DMA((c,)) for c in plan.sems.values() for _ in range(2)]
        + [pltpu.SemaphoreType.DMA((plan.local_sems,))],
        compiler_params=pltpu.CompilerParams(
            collective_id=1, has_side_effects=True, vmem_limit_bytes=63 << 20
        ),
        name="performer_layer",
    )(
        tokens,
        bucket.reshape(grid_ids),
        cell.reshape(grid_ids),
        features,
        qkv_weight,
        line(norm1_gain),
        line(norm1_bias),
        line(out_bias),
        line(norm2_gain),
        line(norm2_bias),
        line(down_bias),
        cotangent,
        out_weight,
        up_weight,
        line(up_bias),
        down_weight,
    )
    return widen(plan, *outs[:6])


def solution(mesh):
    return jax.shard_map(
        functools.partial(per_device, mesh.shape["dp"], mesh.shape["mp"]),
        mesh=mesh,
        in_specs=(
            P("dp", None),
            P("dp", None),
            P("dp", None),
            P("dp"),
            P(),
            P(None, None, "mp"),
            P("mp", None),
            P(),
            P(),
            P(),
            P(),
            P(),
            P(None, "mp"),
            P("mp"),
            P("mp", None),
            P(),
        ),
        out_specs=(
            P("dp", None),
            P("dp", None),
            P(None, None, "mp"),
            P("mp", None),
            P(),
            P(),
            P(),
            P(),
            P(),
            P(None, "mp"),
            P("mp"),
            P("mp", None),
            P(),
        ),
        check_vma=False,
    )
```

```python
import functools
from types import SimpleNamespace

import jax
import jax.numpy as jnp
from jax import lax
from jax.experimental import pallas as pl
from jax.experimental.pallas import tpu as pltpu
from jax.sharding import PartitionSpec as P

HD = 64
FEATS = 4
STEP = 5
SEG = 2
PAD = 8
SCALE = HD**-0.25
HALF_SQUARE = 0.5 * SCALE * SCALE
EPS = 1e-05

BF = jnp.bfloat16
F32 = jnp.float32
MESH = pl.DeviceIdType.MESH
LANES = 128
TILE = 256


def dot(a, b):
    return jnp.dot(a, b, preferred_element_type=F32)


def dot_nt(a, b):
    return lax.dot_general(a, b, (((1,), (1,)), ((), ())), preferred_element_type=F32)


def dot_tn(a, b):
    return lax.dot_general(a, b, (((0,), (0,)), ((), ())), preferred_element_type=F32)


def lane(shape):
    return lax.broadcasted_iota(jnp.int32, shape, len(shape) - 1)


def roll_half(x):
    return pltpu.roll(x, HD, 1)


def loop(count, body, unroll=False):
    if unroll or count <= 3:
        for i in range(count):
            body(i)
    else:

        def step(i, carry):
            body(i)
            return carry

        lax.fori_loop(0, count, step, 0)


def rows_of(i, size):
    if isinstance(i, int):
        return pl.ds(i * size, size)
    return pl.ds(pl.multiple_of(i * size, size), size)


def normalised(values):
    average = jnp.mean(values, -1, keepdims=True)
    centred = values - average
    spread = jnp.mean(centred * centred, -1, keepdims=True)
    scale = lax.rsqrt(spread + EPS)
    return centred * scale, scale


def norm_back(upstream, hat, scale, gain):
    e = gain * upstream
    return (
        e
        - jnp.mean(e, -1, keepdims=True)
        - hat * jnp.mean(e * hat, -1, keepdims=True)
    ) * scale


def round_up(a, b):
    return (a + b - 1) // b * b


class Plan:
    def __init__(self, n, nm, tokens, width, local, feats, hidden):
        self.n, self.nm, self.T, self.D, self.L, self.M, self.F = (
            n,
            nm,
            tokens,
            width,
            local,
            feats,
            hidden,
        )
        self.H = local // HD
        self.HM = self.H * feats
        self.Tm = tokens // nm
        self.big = n > 8
        self.G8 = n * PAD
        self.rest = hidden + local
        self.tail = self.rest + width * local // width
        self.ru, self.rd, self.rk = (
            round_up((rows + n - 1) // n, 16) for rows in (width, self.tail, 2 * width)
        )
        self.per = self.Tm // TILE
        n2 = n // 2
        T, D, L, HM, Tm = self.T, self.D, self.L, self.HM, self.Tm
        vm = "vmem"
        states = (n, HM, SEG * HD)
        place = "hbm" if self.big else vm
        self.inputs = [
            ("tok", "hbm"),
            ("bkt", vm),
            ("cel", vm),
            ("feat", vm),
            ("wqkv", vm),
            ("g1", vm),
            ("b1", vm),
            ("ob", vm),
            ("g2", vm),
            ("b2", vm),
            ("db", vm),
            ("cot", "hbm"),
            ("ow", "hbm"),
            ("up", "hbm"),
            ("ub", "hbm"),
            ("dn", "hbm"),
        ]
        self.outputs = [
            ("out_o", "hbm", (T, D), BF),
            ("gtok_o", "hbm", (T, D), BF),
            ("upg_o", "hbm", (D, hidden), BF),
            ("dng_o", "hbm", (self.tail, D), BF),
            ("kvg_o", "hbm", (2 * D, L), BF),
            ("small_o", vm, (8, D), F32),
        ]
        big_states = [("sp", states), ("rb", states), ("sall", states), ("gall", states)]
        if self.big:
            self.outputs += [(name, "hbm", shape, BF) for name, shape in big_states]
        self.scratch = [
            ("wcat", (D, 4 * L), BF),
            ("f2", (L, HM), BF),
            ("wb", (HM, 2 * L), BF),
            ("ccb", (T, LANES), BF),
            ("oh2", (T, 2 * self.G8), BF),
            ("nm", (T, D), BF),
            ("qk", (2, T, L), BF),
            ("vv", (2, T, L), BF),
            ("qf", (T, HM), BF),
            ("kf", (T, HM), BF),
            ("ft", (HM, T), BF),
            ("tp", (n, PAD, LANES), F32),
            ("trb", (n, PAD, LANES), F32),
            ("tall", (n, PAD, LANES), F32),
            ("gtall", (n, PAD, LANES), F32),
            ("tot2", (2 * self.G8, HM), BF),
            ("acc", (HM, SEG * HD), F32),
            ("attf", (T, L), F32),
            ("inv", (T, L), F32),
            ("attb", (T, L), BF),
            ("arow", (nm, Tm, L), BF),
            ("wq_g", (nm, 3, D, L), BF),
            ("ow_g", (nm, L, D), BF),
            ("up_g", (nm, D, hidden), BF),
            ("ub_g", (nm, 1, hidden), F32),
            ("dn_g", (nm, hidden, D), BF),
            ("cotv", (Tm, D), BF),
            ("tokv", (Tm, D), BF),
            ("mid", (Tm, D), F32),
            ("nm2", (Tm, D), BF),
            ("act", (nm, Tm, hidden), BF),
            ("gp", (nm, Tm, hidden), BF),
            ("bo", (TILE, D), F32),
            ("gn2", (TILE, D), F32),
            ("gb", (Tm, D), BF),
            ("outv", (Tm, D), BF),
            ("small", (16, D), F32),
            ("small_m", (nm, 16, D), F32),
            ("small_d", (n, 8, D), F32),
            ("small_s", (8, D), F32),
            ("ends", (8, D), F32),
            ("last", (8, LANES), F32),
            ("last_m", (nm, 8, LANES), F32),
            ("last_d", (n, 8, LANES), F32),
            ("upp", (nm, D, hidden), BF),
            ("upc", (2, D, hidden), BF),
            ("upy", (n, self.ru, D), BF),
            ("upx", (n2, self.ru, D), BF),
            ("upz", (n2, self.ru, D), BF),
            ("dnp", (nm, self.rest, D), BF),
            ("dnc", (2, self.rest, D), BF),
            ("dny", (n, self.rd, D), BF),
            ("dnx", (n2, self.rd, D), BF),
            ("dnz", (n2, self.rd, D), BF),
            ("gar", (nm, Tm, L), BF),
            ("gad", (2, T, L), BF),
            ("gg", (2, T, L), BF),
            ("gd", (T, L), F32),
            ("grads", (3, T, L), BF),
            ("garr", (nm, 3, Tm, L), BF),
            ("kvp", (n, self.rk, L), BF),
            ("kvr", (n, self.rk, L), BF),
            ("kvl", (n, self.rk, L), BF),
        ]
        if self.big:
            self.scratch += [("stage_a", (2, HM, SEG * HD), BF), ("stage_b", (2, HM, SEG * HD), BF)]
        else:
            self.scratch += [(name, shape, BF) for name, shape in big_states]
            self.scratch += [("num", (T, LANES), F32), ("gkf", (T, self.M), F32)]
        self.sems = {
            **{name: n2 * self.H for name in ("rsx", "rsz", "agz", "agx", "gsx", "gsz", "ggz", "ggx")},
            **{name: n2 for name in ("rtx", "rtz", "atz", "atx", "gtx", "gtz", "hgz", "hgx")},
            **{name: nm * self.per for name in ("a2a", "gaa", "grk")},
            "grq": nm,
            "wy": 5,
            "wc": 10,
            "uc": 2,
            "uy": 1,
            "ux": n2,
            "uz": n2,
            "ugz": n2,
            "ugx": n2,
            "dc": 2,
            "dy": 1,
            "dx": n2,
            "dz": n2,
            "dgz": n2,
            "dgx": n2,
            "ks": n,
            "kg": n,
            "oy": 1,
            "oc": 2,
            "ty": self.per,
            "tc": 2 * self.per,
            "sm": nm,
            "sd": n,
            "lm": nm,
            "ld": n,
        }
        self.local_sems = 24

    def names(self):
        return (
            [x[0] for x in self.inputs]
            + [x[0] for x in self.outputs]
            + [x[0] for x in self.scratch]
            + [f"{k}_{end}" for k in self.sems for end in ("s", "r")]
            + ["lsem"]
        )


def layer_kernel(plan, *refs):
    r = SimpleNamespace(**dict(zip(plan.names(), refs, strict=True)))
    n, nm, T, D, L, M, HM, Tm, H = (
        plan.n,
        plan.nm,
        plan.T,
        plan.D,
        plan.L,
        plan.M,
        plan.HM,
        plan.Tm,
        plan.H,
    )
    hidden = plan.F
    n2 = n // 2
    tiles = T // TILE
    wide = TILE if plan.big else 2 * TILE
    me, m = lax.axis_index("dp"), lax.axis_index("mp")
    sib = m + 1 - 2 * lax.rem(m, 2)
    far = lax.rem(m + nm // 2, nm)
    farsib = lax.rem(sib + nm // 2, nm)
    xpart = me + 1 - 2 * lax.rem(me, 2)
    xme, zme = lax.rem(me, 2), me // 2

    def sem(name, index):
        return getattr(r, f"{name}_s").at[index], getattr(r, f"{name}_r").at[index]

    def copy(src, dst, name, sent, dp=None, mp=None, got=None):
        send, _ = sem(name, sent)
        _, recv = sem(name, sent if got is None else got)
        return pltpu.make_async_remote_copy(
            src_ref=src,
            dst_ref=dst,
            send_sem=send,
            recv_sem=recv,
            device_id=(me if dp is None else dp, m if mp is None else mp),
            device_id_type=MESH,
        )

    def local(src, dst, index):
        return pltpu.make_async_copy(src, dst, r.lsem.at[index])

    low = lane((1, LANES)) < HD

    barrier = pltpu.get_barrier_semaphore()

    def greet(k):
        pl.semaphore_signal(
            barrier, inc=1, device_id=(lax.rem(me + 1 + k, n), m), device_id_type=MESH
        )

    loop(n - 1, greet)
    for k in range(1, nm):
        pl.semaphore_signal(
            barrier, inc=1, device_id=(me, lax.rem(m + k, nm)), device_id_type=MESH
        )

    mine = rows_of(m, Tm)
    wides, len_shards = T // wide, 5

    def tok_in(i):
        rows = rows_of(i, wide)
        return local(r.tok.at[rows], r.nm.at[rows], 1 + len_shards + i)

    own_in = [local(r.cot.at[mine], r.cotv, 0), local(r.tok.at[mine], r.tokv, 1 + len_shards + wides)]
    for c in [tok_in(i) for i in range(wides)] + own_in:
        c.start()

    r.wcat[:, 0:L] = r.wqkv[0]
    r.wcat[:, L : 2 * L] = r.wqkv[1]
    wv = r.wqkv[2].astype(F32)
    wv_rolled = roll_half(wv)
    r.wcat[:, 2 * L : 3 * L] = jnp.where(low, wv, wv_rolled).astype(BF)
    r.wcat[:, 3 * L : 4 * L] = jnp.where(low, wv_rolled, wv).astype(BF)
    feature_rows = r.feat[STEP % FEATS]
    r.f2[...] = jnp.zeros((L, HM), BF)
    for h in range(H):
        r.f2[h * HD : (h + 1) * HD, h * M : (h + 1) * M] = feature_rows
    r.wb[:, 0:L] = r.f2[...].astype(F32).T.astype(BF)
    head_of_row = lax.broadcasted_iota(jnp.int32, (HM, L), 0) // M
    r.wb[:, L : 2 * L] = jnp.where(head_of_row == lane((HM, L)) // HD, 1.0, 0.0).astype(BF)

    count = T // LANES
    numbers = SEG * r.bkt[...].astype(F32) + r.cel[...].astype(F32)
    numbers = jnp.concatenate([numbers, jnp.zeros((LANES - count, LANES), F32)], 0).T
    for i in range(count):
        rows = pl.ds(i * LANES, LANES)
        column = jnp.broadcast_to(numbers[:, i : i + 1], (LANES, LANES))
        r.ccb[rows, :] = (column - jnp.where(low, 0.0, 1.0)).astype(BF)
        for block in range(2 * plan.G8 // LANES):
            place = (lane((1, LANES)) + block * LANES) % plan.G8
            number = place // PAD * SEG + place % SEG
            r.oh2[rows, block * LANES : (block + 1) * LANES] = jnp.where(
                column == number.astype(F32), 1.0, 0.0
            ).astype(BF)
    part_of_row = lax.broadcasted_iota(jnp.int32, (plan.G8, LANES), 0) % PAD // SEG

    def pack_totals(table):
        packed = jnp.zeros((plan.G8, LANES), F32)
        for q in range(HM // LANES):
            packed += jnp.where(part_of_row == q, table[:, q * LANES : (q + 1) * LANES], 0.0)
        return packed.reshape(n, PAD, LANES)

    def spread_totals(packed):
        packed = packed.reshape(plan.G8, LANES)
        return jnp.concatenate(
            [jnp.where(part_of_row == q, packed, 0.0) for q in range(HM // LANES)], 1
        )

    def phi(u):
        wide = u.astype(F32)
        squares = wide * wide
        first = jnp.sum(jnp.where(low, squares, 0.0), -1, keepdims=True)
        second = jnp.sum(jnp.where(low, 0.0, squares), -1, keepdims=True)
        projected = dot(u, r.f2[...]) * SCALE
        shift = jnp.where(lane((1, HM)) < M, first, second) * HALF_SQUARE
        return jnp.exp(projected - shift)

    pl.semaphore_wait(barrier, n - 1 + nm - 1)

    def project(i):
        rows = rows_of(i, wide)
        tok_in(i).wait()
        hat, _ = normalised(r.nm[rows, :].astype(F32))
        normed = (hat * r.g1[...] + r.b1[...]).astype(BF)
        r.nm[rows, :] = normed
        u = dot(normed, r.wcat[:, L:]).astype(BF)
        k = u[:, 0:L]
        r.qk[1, rows, :] = k
        r.vv[0, rows, :], r.vv[1, rows, :] = u[:, L : 2 * L], u[:, 2 * L : 3 * L]
        features = phi(k).astype(BF)
        r.kf[rows, :] = features
        r.ft[:, rows] = features.T

    def queries(i):
        rows = rows_of(i, wide)
        q = dot(r.nm[rows, :], r.wcat[:, 0:L]).astype(BF)
        r.qk[0, rows, :] = q
        r.qf[rows, :] = phi(q).astype(BF)

    shards = [
        (r.ow, r.ow_g),
        (r.up, r.up_g),
        (r.ub, r.ub_g),
        (r.dn, r.dn_g),
        (r.wqkv, r.wq_g),
    ]
    own_copies, y_copies, core_copies = [], [], []
    for i, (src, dst) in enumerate(shards):
        own_copies.append(local(src, dst.at[m], 1 + i))
        y_copies.append(copy(src, dst.at[m], "wy", i, mp=far))
        core_copies.append(copy(src, dst.at[m], "wc", 2 * i, mp=sib))
    for c in own_copies + y_copies + core_copies:
        c.start()
    lax.fori_loop(0, wides, lambda i, carry: (project(i), carry)[1], 0)

    def state_pair(ref, p, stage):
        if plan.big:
            pltpu.sync_copy(ref.at[pl.ds(2 * p, 2)], stage)
            return stage
        return ref.at[pl.ds(2 * p, 2)]

    def masked_pair(rows, dup, p):
        code = r.ccb[rows, :]
        first = jnp.full((1, LANES), 1.0, F32) * (4 * p)
        left = jnp.where(code == first.astype(BF), dup, jnp.zeros_like(dup))
        right = jnp.where(code == (first + 2.0).astype(BF), dup, jnp.zeros_like(dup))
        return jnp.concatenate([left, right], 1)

    everything = pl.ds(0, T)

    def head_rows(h):
        return pl.ds(h * M, M) if isinstance(h, int) else pl.ds(pl.multiple_of(h * M, M), M)

    def at_first(h, body):
        if isinstance(h, int):
            if h == 0:
                body()
        else:
            pl.when(h == 0)(body)

    class Pair:
        def __init__(self, h, state, totals):
            self.h, self.state, self.totals = h, state, totals

        def start(self):
            self.state.start()
            at_first(self.h, lambda: self.totals().start())

        def wait_recv(self):
            self.state.wait_recv()
            at_first(self.h, lambda: self.totals().wait_recv())

        def wait_send(self):
            self.state.wait_send()
            at_first(self.h, lambda: self.totals().wait_send())

    class States:
        def __init__(self, all_s, all_t, names):
            self.all_s, self.all_t = all_s, all_t
            self.x, self.tx, self.z, self.tz, self.gz, self.hz, self.gx, self.hx = names

        def both(self, h, state, totals):
            return Pair(h, state, totals)

        def to_x(self, p, h):
            j, hs = 2 * p + 1 - xme, head_rows(h)
            return self.both(
                h,
                copy(r.sp.at[j, hs], r.rb.at[p, hs], self.x, p * H + h, dp=xpart),
                lambda: copy(r.tp.at[j], r.trb.at[p], self.tx, p, dp=xpart),
            )

        def to_z(self, p, h):
            j, hs = 2 * p + xme, head_rows(h)
            return self.both(
                h,
                copy(
                    r.sp.at[j, hs],
                    r.rb.at[n2 + zme, hs],
                    self.z,
                    p * H + h,
                    dp=j,
                    got=zme * H + h,
                ),
                lambda: copy(r.tp.at[j], r.trb.at[n2 + zme], self.tz, p, dp=j, got=zme),
            )

        def from_z(self, p, h):
            j, hs = 2 * p + xme, head_rows(h)
            return self.both(
                h,
                copy(r.sp.at[j, hs], r.rb.at[n2 + p, hs], self.z, p * H + h, dp=j),
                lambda: copy(r.tp.at[j], r.trb.at[n2 + p], self.tz, p, dp=j),
            )

        def out_z(self, p, h):
            j, hs = 2 * p + xme, head_rows(h)
            s, t = self.all_s.at[me, hs], self.all_t.at[me]
            return self.both(
                h,
                copy(s, s, self.gz, p * H + h, dp=j, got=zme * H + h),
                lambda: copy(t, t, self.hz, p, dp=j, got=zme),
            )

        def in_z(self, p, h):
            j, hs = 2 * p + xme, head_rows(h)
            s, t = self.all_s.at[j, hs], self.all_t.at[j]
            return self.both(
                h,
                copy(s, s, self.gz, p * H + h, dp=j),
                lambda: copy(t, t, self.hz, p, dp=j),
            )

        def out_x(self, p, h, other=False):
            j, hs = 2 * p + (1 - xme if other else xme), head_rows(h)
            s, t = self.all_s.at[j, hs], self.all_t.at[j]
            return self.both(
                h,
                copy(s, s, self.gx, p * H + h, dp=xpart),
                lambda: copy(t, t, self.hx, p, dp=xpart),
            )

        def start(self, dup):
            def pair(q, carry):
                h, p = q // n2, lax.rem(zme + 1 + lax.rem(q, n2), n2)
                block = dot(r.ft[head_rows(h), :], masked_pair(everything, dup[h], p))
                put_state(r.sp, 2 * p, h, block[:, :LANES].astype(BF))
                put_state(r.sp, 2 * p + 1, h, block[:, LANES:].astype(BF))
                self.to_x(p, h).start()
                return carry

            lax.fori_loop(0, H * n2, pair, 0)

        def add_x(self, p, h):
            self.to_x(p, h).wait_recv()
            j = 2 * p + xme

            def totals():
                r.tp[j] += r.trb[p]

            at_first(h, totals)
            return get_state(r.sp, j, h) + get_state(r.rb, p, h)

        def near(self, h, k):
            p = lax.rem(zme + 1 + k, n2)
            put_state(r.sp, 2 * p + xme, h, self.add_x(p, h).astype(BF))
            self.to_z(p, h).start()

        def own(self, h):
            r.acc[head_rows(h), :] = self.add_x(zme, h)

        def whole(self, h):
            def take(k):
                p = lax.rem(zme + 1 + k, n2)
                self.from_z(p, h).wait_recv()
                r.acc[head_rows(h), :] += get_state(r.rb, n2 + p, h)
                if h == 0:
                    r.tp[me] += r.trb[n2 + p]

            loop(n2 - 1, take)
            if h == 0:
                self.all_t[me] = r.tp[me]
            put_state(self.all_s, me, h, r.acc[head_rows(h), :].astype(BF))

            def send(k):
                self.out_z(lax.rem(zme + 1 + k, n2), h).start()

            loop(n2 - 1, send)
            self.out_x(zme, h).start()

        def onward(self, h, k):
            p = lax.rem(zme + 1 + k, n2)
            self.in_z(p, h).wait_recv()
            self.out_x(p, h).start()

        def arrived(self, p, h):
            self.out_x(p, h, other=True).wait_recv()

        def run(self, work, rest, use, midway):
            others = n2 - 1
            steps = H * others

            def step(q, carry):
                h, k = q // others, lax.rem(q, others)
                pl.when(q == steps - 1)(lambda: self.whole(0))
                self.near(h, k)
                work(q)
                pl.when(k == others - 1)(lambda: self.own(h))
                return carry

            lax.fori_loop(0, steps, step, 0)
            rest()
            self.whole(H - 1)
            loop(others, lambda k: self.onward(0, k))
            for h in range(H):
                loop(n2, lambda p, h=h: self.arrived(p, h))
                if h < H - 1:
                    loop(others, lambda k, h=h: self.onward(h + 1, k))
                    use(h)
                    midway()
            for h in range(H):

                def sent(p, h=h):
                    self.to_x(p, h).wait_send()
                    self.out_x(p, h).wait_send()

                loop(n2, sent)

                def sent_z(k, h=h):
                    p = lax.rem(zme + 1 + k, n2)
                    self.to_z(p, h).wait_send()
                    self.out_z(p, h).wait_send()

                loop(others, sent_z)
            total = spread_totals(self.all_t[...])
            top = total.astype(BF)
            r.tot2[0 : plan.G8, :] = top
            r.tot2[plan.G8 :, :] = (total - top.astype(F32)).astype(BF)

    def put_state(ref, j, h, values):
        if plan.big:
            spot = r.stage_b.at[0, head_rows(h)]
            spot[...] = values
            pltpu.sync_copy(spot, ref.at[j, head_rows(h)])
        else:
            ref[j, head_rows(h), :] = values

    def get_state(ref, j, h):
        if plan.big:
            spot = r.stage_b.at[1, head_rows(h)]
            pltpu.sync_copy(ref.at[j, head_rows(h)], spot)
            return spot[...].astype(F32)
        return ref[j, head_rows(h), :].astype(F32)

    def state_columns(ref, p, h):
        blocks = state_pair(ref, p, r.stage_a if plan.big else None)
        return jnp.concatenate([blocks[0, head_rows(h), :], blocks[1, head_rows(h), :]], 1)

    def pick(code, product, p, rest):
        first = jnp.full((1, LANES), 1.0, F32) * (4 * p)
        rest = jnp.where(code == first, product[:, :LANES], rest)
        return jnp.where(code == first + 2.0, product[:, LANES:], rest)

    def times_state(rows, left, all_s, h):
        code, features = r.ccb[rows, :].astype(F32), left[rows, head_rows(h)]

        def pair(p, total):
            return pick(code, dot(features, state_columns(all_s, p, h)), p, total)

        total = jnp.zeros((rows.size, LANES), F32)
        if plan.big:
            return lax.fori_loop(0, n2, pair, total)
        for p in range(n2):
            total = pair(p, total)
        return total

    def own_state(rows, left, all_s):
        ready = [] if plan.big else [r.num[rows, :]]
        heads = ready + [times_state(rows, left, all_s, h) for h in range(len(ready), H)]
        return halves(*(head + roll_half(head) for head in heads))

    def halves(first, second):
        return jnp.where(low, first, second)

    def early(left, all_s):
        def run(h):
            if plan.big:
                return

            def tile(i, carry):
                rows = rows_of(i, wide)
                r.num[rows, :] = times_state(rows, left, all_s, h)
                return carry

            lax.fori_loop(0, wides, tile, 0)

        return run

    first = States(
        r.sall, r.tall, ("rsx", "rtx", "rsz", "rtz", "agz", "atz", "agx", "atx")
    )
    r.tp[...] = pack_totals(dot_tn(r.oh2[:, : plan.G8], r.kf[...]))
    first.start(r.vv)

    onward = []

    def weights_on(which):
        for i in which:
            dst = shards[i][1]
            copy(dst.at[far], dst.at[far], "wy", i, mp=far).wait_recv()
            c = copy(dst.at[far], dst.at[far], "wc", 2 * i + 1, mp=sib)
            c.start()
            onward.append(c)

    def turn(source):
        def tile(i):
            rows = rows_of(i, TILE)
            r.ft[:, rows] = source[rows, :].T

        return lambda: loop(tiles, tile)

    def in_quarters(body, size):
        quarter = T // size // 4

        def work(q):
            def tile(i, carry):
                body(q * quarter + i)
                return carry

            pl.when(q < 4)(lambda: (lax.fori_loop(0, quarter, tile, 0), None)[1])

        return work

    first.run(
        in_quarters(queries, wide),
        turn(r.qf),
        early(r.qf, r.sall),
        lambda: weights_on(range(4)),
    )

    def own_totals(rows):
        return dot(r.oh2[rows, :], r.tot2[...])

    def attend(i):
        rows = rows_of(i, TILE)
        numerator = own_state(rows, r.qf, r.sall)
        product = r.qf[rows, :].astype(F32) * own_totals(rows)
        denominator = halves(
            jnp.sum(product[:, :M], -1, keepdims=True),
            jnp.sum(product[:, M:], -1, keepdims=True),
        )
        inverse = 1.0 / denominator
        attention = numerator / denominator
        r.attf[rows, :] = attention
        r.inv[rows, :] = inverse
        r.attb[rows, :] = attention.astype(BF)

    per = plan.per
    chunk_order = [far, farsib, sib, m]
    others_mp = chunk_order[: nm - 1]

    def swap(src, dst, name, target, i):
        return copy(src, dst, name, target * per + i, mp=target, got=m * per + i)

    def swapped(dst, name, source, i):
        return copy(dst, dst, name, source * per + i, mp=source)

    def attention_copy(target, i):
        return swap(
            r.attb.at[rows_of(target * per + i, TILE)],
            r.arow.at[m, rows_of(i, TILE)],
            "a2a",
            target,
            i,
        )

    def each_tile(body, after, middle=None):
        def step(q, carry):
            i, k = q // nm, lax.rem(q, nm)
            start = lax.rem(m + (1 - k // 2) * (nm // 2), nm)
            target = start + lax.rem((k + 1) // 2, 2) * (1 - 2 * lax.rem(start, 2))
            body(target * per + i)
            pl.when(k < nm - 1)(lambda: after(target, i).start())
            return carry

        half = per // 2 * nm
        lax.fori_loop(0, half, step, 0)
        if middle is not None:
            middle()
        lax.fori_loop(half, per * nm, step, 0)

    each_tile(attend, attention_copy)
    r.arow[m] = r.attb[rows_of(m, Tm), :]

    def weights_wait(which):
        for i in which:
            dst = shards[i][1]
            own_copies[i].wait()
            copy(dst.at[sib], dst.at[sib], "wc", 2 * i, mp=sib).wait_recv()
            copy(dst.at[farsib], dst.at[farsib], "wc", 2 * i + 1, mp=sib).wait_recv()
            for c in (y_copies[i], core_copies[i], onward[i]):
                c.wait_send()

    weights_wait(range(4))
    for c in own_in:
        c.wait()

    r.small[...] = jnp.zeros((16, D), F32)

    beside = 1 if plan.big else 2

    def units(rows, group):
        both = [beside * group + i for i in range(beside)]
        normed, cotangent = r.nm2[rows, :], r.cotv[rows, :]
        preacts = [dot(normed, r.up_g[s]) + r.ub_g[s] for s in both]
        backs = [dot_nt(cotangent, r.dn_g[s]) for s in both]
        forward, backward = r.bo[...], r.gn2[...]
        for s, preact, back in zip(both, preacts, backs, strict=True):
            spread = 0.5 + 0.5 * lax.erf(preact * (0.5**0.5))
            active = (preact * spread).astype(BF)
            r.act[s, rows, :] = active
            slope = spread + preact * jnp.exp(preact * preact * -0.5) * 0.3989422804014327
            grad = (back * slope).astype(BF)
            r.gp[s, rows, :] = grad
            forward += dot(active, r.dn_g[s])
            backward += dot_nt(grad, r.up_g[s])
            r.small[pl.ds(8 + s, 1), :] += jnp.sum(grad.astype(F32), 0, keepdims=True)
        r.bo[...] = forward
        r.gn2[...] = backward

    gas = r.attb.reshape(nm, Tm, L)

    def grad_copy(target, i):
        rows = rows_of(i, TILE)
        return swap(gas.at[target, rows], r.gar.at[m, rows], "gaa", target, i)

    def middle_rows(i):
        rows = rows_of(i, TILE)
        for target in others_mp:
            swapped(r.arow.at[target, rows], "a2a", target, i).wait_recv()
            attention_copy(target, i).wait_send()
        columns = jnp.concatenate([r.arow[s, rows, :] for s in range(nm)], 1)
        branch = dot(columns, r.ow_g[...].reshape(D, D)).astype(BF).astype(F32)
        middle = r.tokv[rows, :].astype(F32) + branch + r.ob[...]
        hat, scale = normalised(middle)
        normed = hat * r.g2[...] + r.b2[...]
        r.mid[rows, :] = middle
        r.nm2[rows, :] = normed.astype(BF)
        r.bo[...] = jnp.zeros((TILE, D), F32)
        r.gn2[...] = jnp.zeros((TILE, D), F32)
        lax.fori_loop(0, nm // beside, lambda s, carry: (units(rows, s), carry)[1], 0)
        middle = r.mid[rows, :]
        r.outv[rows, :] = (middle + r.bo[...] + r.db[...]).astype(BF)
        hat, scale = normalised(middle)
        upstream = r.gn2[...]
        cotangent = r.cotv[rows, :].astype(F32)
        grad = cotangent + norm_back(upstream, hat, scale, r.g2[...])
        low_grad = grad.astype(BF)
        back = dot_nt(low_grad, r.ow_g[...].reshape(D, D)).astype(BF)
        for s in range(nm):
            gas[s, rows, :] = back[:, s * L : (s + 1) * L]
        for target in others_mp:
            grad_copy(target, i).start()
        r.mid[rows, :] = grad
        r.gb[rows, :] = low_grad
        r.small[0:1, :] += jnp.sum(cotangent, 0, keepdims=True)
        r.small[1:2, :] += jnp.sum(upstream * hat, 0, keepdims=True)
        r.small[2:3, :] += jnp.sum(upstream, 0, keepdims=True)
        r.small[3:4, :] += jnp.sum(grad, 0, keepdims=True)

    lax.fori_loop(0, per, lambda i, carry: (middle_rows(i), carry)[1], 0)
    r.gar[m] = gas[m]

    up_core = [
        copy(r.upp.at[sib], r.upc.at[0], "uc", 0, mp=sib),
        copy(r.upp.at[farsib], r.upc.at[1], "uc", 1, mp=sib),
    ]
    dn_core = [
        copy(r.dnp.at[sib], r.dnc.at[0], "dc", 0, mp=sib),
        copy(r.dnp.at[farsib], r.dnc.at[1], "dc", 1, mp=sib),
    ]

    def up_part(s):
        r.upp[s] = dot_tn(r.nm2[...], r.gp[s]).astype(BF)

    def down_part(s):
        r.dnp[s, 0:hidden, :] = dot_tn(r.act[s], r.cotv[...]).astype(BF)
        r.dnp[s, hidden : hidden + L, :] = dot_tn(r.arow[s], r.gb[...]).astype(BF)

    lax.fori_loop(0, nm, lambda s, carry: (up_part(s), carry)[1], 0)
    for c in up_core:
        c.start()
    lax.fori_loop(0, nm, lambda s, carry: (down_part(s), carry)[1], 0)
    for c in dn_core:
        c.start()

    def flat_rows(ref):
        return ref.reshape(ref.shape[0] * ref.shape[1], ref.shape[2])

    def core_sum(copies, part, other, y, name):
        for c in copies:
            c.wait()
        rows = part.shape[1]

        def add(i):
            strip = rows_of(i, LANES)
            part[far, strip, :] = (
                part[far, strip, :].astype(F32) + other[1, strip, :].astype(F32)
            ).astype(BF)

        loop(rows // LANES, add)
        return copy(part.at[far], flat_rows(y).at[pl.ds(0, rows)], name, 0, mp=far)

    def y_sum(sent, part, other, y):
        sent.wait()
        flat = flat_rows(y)

        def add(i):
            strip = rows_of(i, LANES)
            flat[strip, :] = (
                part[m, strip, :].astype(F32)
                + other[0, strip, :].astype(F32)
                + flat[strip, :].astype(F32)
            ).astype(BF)

        loop(part.shape[1] // LANES, add)

    class Reduction:
        def __init__(self, source, rx, rz, out, names):
            self.source, self.rx, self.rz, self.out = source, rx, rz, out
            self.x, self.z, self.gz, self.gx = names

        def block(self, k):
            return self.source.at[xme * n2 + k]

        def to_x(self, k):
            return copy(self.source.at[(1 - xme) * n2 + k], self.rx.at[k], self.x, k, dp=xpart)

        def start(self):
            loop(n2, lambda k: self.to_x(lax.rem(zme + 1 + k, n2)).start())

        def scatter(self):
            def add(k):
                self.to_x(k).wait()
                ref = self.block(k)
                ref[...] = (ref[...].astype(F32) + self.rx[k].astype(F32)).astype(BF)

            def send(k):
                z = lax.rem(zme + 1 + k, n2)
                add(z)
                copy(self.block(z), self.rz.at[zme], self.z, z, dp=2 * z + xme, got=zme).start()

            loop(n2 - 1, send)
            add(zme)

        def gather(self):
            own = self.block(zme)

            def take(k, total):
                z = lax.rem(zme + 1 + k, n2)
                copy(self.block(z), self.rz.at[z], self.z, z, dp=2 * z + xme).wait()
                return total + self.rz[z].astype(F32)

            total = own[...].astype(F32)
            if n2 <= 4:
                for k in range(n2 - 1):
                    total = take(k, total)
            else:
                total = lax.fori_loop(0, n2 - 1, take, total)
            own[...] = total.astype(BF)
            self.place(xme * n2 + zme, 1)[...] = own[...]
            spot = self.place(xme * n2 + zme, 1)

            def send(k):
                z = lax.rem(zme + 1 + k, n2)
                copy(own, spot, self.gz, z, dp=2 * z + xme, got=zme).start()

            loop(n2 - 1, send)
            self.over_x(zme).start()

        def over_x(self, z, side=None):
            spot = self.place((xme if side is None else side) * n2 + z, 1)
            return copy(spot, spot, self.gx, z, dp=xpart)

        def spread(self):
            own = self.block(zme)

            def onward(k):
                z = lax.rem(zme + 1 + k, n2)
                copy(own, self.place(xme * n2 + z, 1), self.gz, z, dp=2 * z + xme).wait()
                self.over_x(z).start()

            loop(n2 - 1, onward)

        def finish(self):
            def wait(z):
                self.over_x(z, 1 - xme).wait_recv()
                self.over_x(z).wait_send()

            loop(n2, wait)

        def place(self, index, count):
            rows = self.source.shape[1]
            return self.out.at[pl.ds(pl.multiple_of(index * rows, rows), count * rows)]

    up = Reduction(r.upy, r.upx, r.upz, flat_rows(r.upc), ("ux", "uz", "ugz", "ugx"))
    dn = Reduction(r.dny, r.dnx, r.dnz, flat_rows(r.dnc), ("dx", "dz", "dgz", "dgx"))

    class Sums:
        def __init__(self, own, over_m, names):
            self.own, self.over_m, self.names = own, over_m, names

        def start(self):
            for target in others_mp:
                copy(
                    self.own, self.over_m.at[m], self.names[0], target, mp=target, got=m
                ).start()

        def scatter(self, send, over_d, keep):
            total = self.own[...]
            for target in others_mp:
                copy(self.own, self.over_m.at[target], self.names[0], target, mp=target).wait()
                total += self.over_m[target]
            self.send, self.over_d = send, over_d
            self.send[...] = keep(total)

            def go(k):
                j = lax.rem(me + 1 + k, n)
                copy(self.send, over_d.at[me], self.names[1], j, dp=j, got=me).start()

            loop(n - 1, go)

        def gather(self):
            self.total = self.send[...]

            def take(k, total):
                j = lax.rem(me + 1 + k, n)
                copy(self.send, self.over_d.at[j], self.names[1], j, dp=j).wait()
                return total + self.over_d[j]

            return lax.fori_loop(0, n - 1, take, self.send[...])

    small = Sums(r.small, r.small_m, ("sm", "sd"))
    last = Sums(r.last, r.last_m, ("lm", "ld"))
    small.start()
    weights_on([4])
    for i in range(per):
        for target in others_mp:
            swapped(r.gar.at[target, rows_of(i, TILE)], "gaa", target, i).wait_recv()
    up_y = core_sum(up_core, r.upp, r.upc, r.upy, "uy")
    up_y.start()

    def grad_rows(i):
        rows = rows_of(i, wide)
        s = i // (Tm // wide)
        inner = rows_of(i - s * (Tm // wide), wide)
        grad = r.gar[s, inner, :].astype(F32)
        inv = r.inv[rows, :]
        scaled = grad * inv
        g_roll, s_roll = roll_half(grad), roll_half(scaled)
        r.gad[0, rows, :] = halves(grad, g_roll).astype(BF)
        r.gad[1, rows, :] = halves(g_roll, grad).astype(BF)
        r.gg[0, rows, :] = halves(scaled, s_roll).astype(BF)
        r.gg[1, rows, :] = halves(s_roll, scaled).astype(BF)
        product = scaled * r.attf[rows, :]
        r.gd[rows, :] = -halves(
            jnp.sum(jnp.where(low, product, 0.0), -1, keepdims=True),
            jnp.sum(jnp.where(low, 0.0, product), -1, keepdims=True),
        )

    lax.fori_loop(0, wides, lambda i, carry: (grad_rows(i), carry)[1], 0)

    def head_column(values, h):
        return values[:, h * HD : h * HD + 1]

    head_totals = []
    for h in range(H):
        column = r.gd[:, h * HD : h * HD + 1]
        top = column.astype(BF).astype(F32)
        upper = lane((1, 2 * plan.G8)) < plan.G8
        weights = r.oh2[...] * jnp.where(upper, top, column - top).astype(BF)
        summed = dot_tn(weights, r.qf[:, h * M : (h + 1) * M])
        head_totals.append(summed[: plan.G8] + summed[plan.G8 :])
    r.tp[...] = pack_totals(jnp.concatenate(head_totals, 1))
    dn_y = core_sum(dn_core, r.dnp, r.dnc, r.dny, "dy")
    dn_y.start()
    second = States(
        r.gall, r.gtall, ("gsx", "gtx", "gsz", "gtz", "ggz", "hgz", "ggx", "hgx")
    )
    second.start(r.gg)

    def contract(rows, dup, all_s, h):
        def pair(p, total):
            return total + dot_nt(masked_pair(rows, dup[h, rows, :], p), state_columns(all_s, p, h))

        total = jnp.zeros((rows.size, M), F32)
        if plan.big:
            return lax.fori_loop(0, n2, pair, total)
        for p in range(n2):
            total = pair(p, total)
        return total

    def early_keys(h):
        if plan.big:
            return

        def tile(i, carry):
            rows = rows_of(i, wide)
            r.gkf[rows, :] = contract(rows, r.vv, r.gall, h)
            return carry

        lax.fori_loop(0, wides, tile, 0)
        early(r.kf, r.gall)(h)

    def feature_back(rows, which, grad_features):
        u = r.qk[which, rows, :]
        weighted = (grad_features * phi(u)).astype(BF)
        both = dot(weighted, r.wb[...])
        return (
            both[:, :L] * SCALE - both[:, L:] * u.astype(F32) * (SCALE * SCALE)
        ).astype(BF)

    def query_back(i):
        rows = rows_of(i, wide)
        totals = own_totals(rows)
        inv, gd = r.inv[rows, :], r.gd[rows, :]
        parts = [
            contract(rows, r.gad, r.sall, h) * head_column(inv, h)
            + totals[:, h * M : (h + 1) * M] * head_column(gd, h)
            for h in range(H)
        ]
        r.grads[0, rows, :] = feature_back(rows, 0, jnp.concatenate(parts, 1))

    def own_unit_sums(total):
        rows = lax.broadcasted_iota(jnp.int32, (16, 1), 0)
        units_row = jnp.sum(jnp.where(rows == 8 + m, total, 0.0), 0, keepdims=True)
        return jnp.concatenate([total[0:4], units_row, jnp.zeros((3, D), F32)], 0)

    def small_scatter():
        small.scatter(r.small_s, r.small_d, own_unit_sums)

    def send_query_grads():
        for target in others_mp:
            copy(
                r.grads.at[0, rows_of(target, Tm)], r.garr.at[m, 0], "grq", target, mp=target, got=m
            ).start()

    def query_projection():
        part = dot(r.ft[...], r.grads[0]).astype(BF)
        flat = flat_rows(r.dny)
        for c in range(D // L):
            flat[plan.rest : plan.tail, c * L : (c + 1) * L] = part[c * L : (c + 1) * L, :]

    gtv = r.nm2
    out_land, tok_land = flat_rows(r.dn_g), flat_rows(r.up_g)
    out_y = copy(r.outv, out_land.at[mine], "oy", 0, mp=far)
    out_core = copy(r.outv, out_land.at[mine], "oc", 0, mp=sib)

    def start_up():
        y_sum(up_y, r.upp, r.upc, r.upy)
        up.start()

    def midway():
        out_y.start()
        out_core.start()
        y_sum(dn_y, r.dnp, r.dnc, r.dny)
        dn.start()
        up.scatter()

    def after_queries():
        send_query_grads()
        turn(r.nm)()
        query_projection()
        start_up()
        small_scatter()

    second.run(in_quarters(query_back, wide), after_queries, early_keys, midway)

    def key_back(i):
        rows = rows_of(i, TILE)
        totals = own_totals(rows)
        ready = [] if plan.big else [r.gkf[rows, :]]
        parts = ready + [contract(rows, r.vv, r.gall, h) for h in range(len(ready), H)]
        gkf = jnp.concatenate(parts, 1)
        r.grads[1, rows, :] = feature_back(rows, 1, gkf + totals)
        r.grads[2, rows, :] = own_state(rows, r.kf, r.gall).astype(BF)

    both = pl.ds(1, 2)

    def key_copy(target, i):
        return swap(
            r.grads.at[both, rows_of(target * per + i, TILE)],
            r.garr.at[m, both, rows_of(i, TILE)],
            "grk",
            target,
            i,
        )

    def between_halves():
        up.gather()
        dn.scatter()
        out_land[mine, :] = r.outv[...]

    each_tile(key_back, key_copy, between_halves)
    for a in range(3):
        r.garr[m, a] = r.grads[a, rows_of(m, Tm), :]

    part = dot(r.ft[...], jnp.concatenate([r.grads[1], r.grads[2]], 1)).astype(BF)
    flat = flat_rows(r.kvp)
    flat[0:D, :] = part[:, :L]
    flat[D : 2 * D, :] = part[:, L:]

    def kv_send(k):
        j = lax.rem(me + 1 + k, n)
        copy(r.kvp.at[j], r.kvr.at[me], "ks", j, dp=j, got=me).start()

    loop(n - 1, kv_send)

    out_far = out_land.at[rows_of(far, Tm)]
    copy(out_far, out_far, "oy", 0, mp=far).wait_recv()
    out_on = copy(out_far, out_far, "oc", 1, mp=sib)
    out_on.start()

    for target in others_mp:
        copy(r.garr.at[target, 0], r.garr.at[target, 0], "grq", target, mp=target).wait_recv()
    weights_wait([4])
    r.ends[...] = jnp.zeros((8, D), F32)

    quarters = D // LANES

    def send_ends():
        for row in range(2):
            for q in range(quarters):
                spot = row * quarters + q
                r.last[spot : spot + 1, :] = r.ends[row : row + 1, q * LANES : (q + 1) * LANES]
        last.start()

    def norm1_back(i):
        rows = rows_of(i, TILE)
        for target in others_mp:
            swapped(r.garr.at[target, both, rows], "grk", target, i).wait_recv()
        upstream = jnp.zeros((TILE, D), F32)
        for s in range(nm):
            left = jnp.concatenate([r.garr[s, a, rows, :] for a in range(3)], 1)
            right = jnp.concatenate([r.wq_g[s, a] for a in range(3)], 1)
            upstream += dot_nt(left, right)
        upstream = upstream.astype(BF).astype(F32)
        hat, scale = normalised(r.tokv[rows, :].astype(F32))
        gtv[rows, :] = (r.mid[rows, :] + norm_back(upstream, hat, scale, r.g1[...])).astype(BF)
        r.ends[0:1, :] += jnp.sum(upstream * hat, 0, keepdims=True)
        r.ends[1:2, :] += jnp.sum(upstream, 0, keepdims=True)
        pl.when(i == per - 1)(send_ends)
        for c in tok_copies(i):
            c.start()

        @pl.when(i == 0)
        def _():
            dn.gather()
            up.spread()

    def tok_copies(i):
        rows = rows_of(i, TILE)
        spot = tok_land.at[rows_of(m * per + i, TILE)]
        return (
            copy(gtv.at[rows], spot, "ty", i, mp=far),
            copy(gtv.at[rows], spot, "tc", 2 * i, mp=sib),
        )

    lax.fori_loop(0, per, lambda i, carry: (norm1_back(i), carry)[1], 0)
    tok_land[mine, :] = gtv[...]

    def kv_sum():
        total = r.kvp[me].astype(F32)

        def take(k, total):
            j = lax.rem(me + 1 + k, n)
            copy(r.kvp.at[j], r.kvr.at[j], "ks", j, dp=j).wait()
            return total + r.kvr[j].astype(F32)

        r.kvp[me] = lax.fori_loop(0, n - 1, take, total).astype(BF)

    kv_sum()
    last.scatter(r.last, r.last_d, lambda total: total)
    kv_spot = r.kvl.at[me]
    r.kvl[me] = r.kvp[me]

    def kv_spread(k):
        j = lax.rem(me + 1 + k, n)
        copy(r.kvp.at[me], kv_spot, "kg", j, dp=j, got=me).start()

    loop(n - 1, kv_spread)
    dn.spread()
    tok_on = []

    def tok_forward(i):
        spot = tok_land.at[rows_of(far * per + i, TILE)]
        copy(spot, spot, "ty", i, mp=far).wait_recv()
        c = copy(spot, spot, "tc", 2 * i + 1, mp=sib)
        c.start()
        tok_on.append(c)

    sums = small.gather()
    ends = last.gather()
    r.small_o[0:4, :] = sums[0:4]
    for row in range(2):
        for q in range(quarters):
            spot = row * quarters + q
            r.small_o[4 + row : 5 + row, q * LANES : (q + 1) * LANES] = ends[spot : spot + 1]
    r.small_o[6:7, :] = sums[4:5]

    written = []

    def write(src, dst):
        c = local(src, dst, len(written))
        c.start()
        written.append(c)

    def kv_wait(k):
        j = lax.rem(me + 1 + k, n)
        copy(r.kvp.at[me], r.kvl.at[j], "kg", j, dp=j).wait()

    for index, owner in enumerate((sib, farsib)):
        spot = out_land.at[rows_of(owner, Tm)]
        copy(spot, spot, "oc", index, mp=sib).wait_recv()
    write(out_land, r.out_o)
    for i in range(per):
        tok_forward(i)
    up.finish()
    write(up.out.at[pl.ds(0, D)], r.upg_o)
    loop(n - 1, kv_wait)
    write(flat_rows(r.kvl).at[pl.ds(0, 2 * D)], r.kvg_o)
    for i in range(per):
        for index, owner in enumerate((sib, farsib)):
            spot = tok_land.at[rows_of(owner * per + i, TILE)]
            copy(spot, spot, "tc", 2 * i + index, mp=sib).wait_recv()
    write(tok_land, r.gtok_o)
    dn.finish()
    write(dn.out.at[pl.ds(0, plan.tail)], r.dng_o)
    for i in range(per):
        for c in tok_copies(i):
            c.wait_send()
    for c in (out_y, out_core, out_on, *tok_on):
        c.wait_send()
    for c in written:
        c.wait()
    for target in others_mp:
        for i in range(per):
            for c in (grad_copy(target, i), key_copy(target, i)):
                c.wait_send()
        copy(r.grads.at[0, rows_of(target, Tm)], r.garr.at[m, 0], "grq", target, mp=target).wait_send()


def widen_kernel(plan, *refs):
    (output, tokens, up, down, kv, small), refs = refs[:6], refs[6:]
    (out_o, tok_o, qkv_o, ow_o, ob_o, g1_o, b1_o, g2_o, b2_o, up_o, ub_o, dn_o, db_o), refs = (
        refs[:13],
        refs[13:],
    )
    tok_v, out_v, up_v, dn_v, kv_v, tok_w, up_w, dn_w, ow_w, qkv_w, sem_in, sem_out = refs
    D, L, hidden, T = plan.D, plan.L, plan.F, plan.T
    pieces = 8
    size = T // pieces
    reads = [
        pltpu.make_async_copy(a, b, sem_in.at[i])
        for i, (a, b) in enumerate([(up, up_v), (down, dn_v), (kv, kv_v), (output, out_v)])
    ]
    token_reads = [
        pltpu.make_async_copy(
            tokens.at[pl.ds(i * size, size)], tok_v.at[pl.ds(i * size, size)], sem_in.at[4 + i]
        )
        for i in range(pieces)
    ]
    for c in token_reads + reads:
        c.start()
    for row, ref in ((3, ob_o), (4, g1_o), (5, b1_o), (1, g2_o), (2, b2_o), (6, ub_o), (0, db_o)):
        ref[...] = small[row : row + 1, :]
    writes = []

    def send(src, dst):
        c = pltpu.make_async_copy(src, dst, sem_out.at[len(writes)])
        c.start()
        writes.append(c)

    for i in range(pieces):
        token_reads[i].wait()
        if i == 1:
            reads[3].wait()
            for part in range(2):
                through = pl.ds(part * (T // 2), T // 2)
                send(out_v.at[through], out_o.at[through])
        rows = pl.ds(i * size, size)
        tok_w[rows, :] = tok_v[rows, :].astype(F32)
        send(tok_w.at[rows], tok_o.at[rows])
    for c in reads[:3]:
        c.wait()
    up_w[...] = up_v[...].astype(F32)
    send(up_w, up_o)
    dn_w[...] = dn_v[0:hidden, :].astype(F32)
    send(dn_w, dn_o)
    ow_w[...] = dn_v[hidden : hidden + L, :].astype(F32)
    send(ow_w, ow_o)
    for c in range(D // L):
        qkv_w[0, c * L : (c + 1) * L, :] = dn_v[
            plan.rest : plan.tail, c * L : (c + 1) * L
        ].astype(F32)
    qkv_w[1] = kv_v[0:D, :].astype(F32)
    qkv_w[2] = kv_v[D : 2 * D, :].astype(F32)
    send(qkv_w, qkv_o)
    for c in writes:
        c.wait()


def widen(plan, *gathered):
    D, L, hidden, T = plan.D, plan.L, plan.F, plan.T
    line = ("vmem", (1, D))
    outs = [
        ("hbm", (T, D)),
        ("hbm", (T, D)),
        ("hbm", (3, D, L)),
        ("hbm", (L, D)),
        *[line] * 5,
        ("hbm", (D, hidden)),
        ("vmem", (1, hidden)),
        ("hbm", (hidden, D)),
        line,
    ]
    spaces = {"vmem": pltpu.VMEM, "hbm": pl.ANY}
    results = pl.pallas_call(
        functools.partial(widen_kernel, plan),
        out_shape=[
            jax.ShapeDtypeStruct(shape, BF if i == 0 else F32) for i, (_, shape) in enumerate(outs)
        ],
        in_specs=[pl.BlockSpec(memory_space=pl.ANY)] * 5 + [pl.BlockSpec(memory_space=pltpu.VMEM)],
        out_specs=[pl.BlockSpec(memory_space=spaces[kind]) for kind, _ in outs],
        scratch_shapes=[
            pltpu.VMEM((T, D), BF),
            pltpu.VMEM((T, D), BF),
            pltpu.VMEM((D, hidden), BF),
            pltpu.VMEM((plan.tail, D), BF),
            pltpu.VMEM((2 * D, L), BF),
            pltpu.VMEM((T, D), F32),
            pltpu.VMEM((D, hidden), F32),
            pltpu.VMEM((hidden, D), F32),
            pltpu.VMEM((L, D), F32),
            pltpu.VMEM((3, D, L), F32),
            pltpu.SemaphoreType.DMA((16,)),
            pltpu.SemaphoreType.DMA((24,)),
        ],
        compiler_params=pltpu.CompilerParams(vmem_limit_bytes=60 << 20),
        name="widen",
    )(*gathered)
    return tuple(v.reshape(-1) if v.shape[0] == 1 else v for v in results)


def per_device(
    n,
    nm,
    tokens,
    cotangent,
    bucket,
    cell,
    features,
    qkv_weight,
    out_weight,
    out_bias,
    norm1_gain,
    norm1_bias,
    norm2_gain,
    norm2_bias,
    up_weight,
    up_bias,
    down_weight,
    down_bias,
):
    count, width = tokens.shape
    local, hidden = qkv_weight.shape[2], up_weight.shape[1]
    plan = Plan(n, nm, count, width, local, features.shape[2], hidden)
    spaces = {"vmem": pltpu.VMEM, "hbm": pl.ANY}
    line = lambda v: v.reshape(1, -1)
    grid_ids = (count // LANES, LANES)
    outs = pl.pallas_call(
        functools.partial(layer_kernel, plan),
        out_shape=[jax.ShapeDtypeStruct(s, d) for _, _, s, d in plan.outputs],
        in_specs=[pl.BlockSpec(memory_space=spaces[k]) for _, k in plan.inputs],
        out_specs=[pl.BlockSpec(memory_space=spaces[k]) for _, k, _, _ in plan.outputs],
        scratch_shapes=[pltpu.VMEM(s, d) for _, s, d in plan.scratch]
        + [pltpu.SemaphoreType.DMA((c,)) for c in plan.sems.values() for _ in range(2)]
        + [pltpu.SemaphoreType.DMA((plan.local_sems,))],
        compiler_params=pltpu.CompilerParams(
            collective_id=1, has_side_effects=True, vmem_limit_bytes=63 << 20
        ),
        name="performer_layer",
    )(
        tokens,
        bucket.reshape(grid_ids),
        cell.reshape(grid_ids),
        features,
        qkv_weight,
        line(norm1_gain),
        line(norm1_bias),
        line(out_bias),
        line(norm2_gain),
        line(norm2_bias),
        line(down_bias),
        cotangent,
        out_weight,
        up_weight,
        line(up_bias),
        down_weight,
    )
    return widen(plan, *outs[:6])


def solution(mesh):
    return jax.shard_map(
        functools.partial(per_device, mesh.shape["dp"], mesh.shape["mp"]),
        mesh=mesh,
        in_specs=(
            P("dp", None),
            P("dp", None),
            P("dp", None),
            P("dp"),
            P(),
            P(None, None, "mp"),
            P("mp", None),
            P(),
            P(),
            P(),
            P(),
            P(),
            P(None, "mp"),
            P("mp"),
            P("mp", None),
            P(),
        ),
        out_specs=(
            P("dp", None),
            P("dp", None),
            P(None, None, "mp"),
            P("mp", None),
            P(),
            P(),
            P(),
            P(),
            P(),
            P(None, "mp"),
            P("mp"),
            P("mp", None),
            P(),
        ),
        check_vma=False,
    )
```
